128 devices in a mesh: band: 4 (over y), dom: 32 (over x, z, core).
Axes of the slice: x: 4, y: 4, z: 4, core: 2. Of those that a mesh axis runs over, the one named last changes fastest.
Arguments:
- orbitals: float32 [1024, 131072], P('band', 'dom'), may hold values from -6 to 6
- projectors: float32 [1024, 512, 128], P('dom'), may hold values from -0.25 to 0.25
- window_start: int32 [1024], P('dom'), may hold values from 0 to 3584
- slot_atom: int32 [32, 32], replicated, may hold values from 0 to 95, as said below
- atom_home: int32 [96], replicated, may hold values from 0 to 95, as said below
- atom_matrices: float32 [96, 128, 128], P('dom'), may hold values from -0.1875 to 0.1875
- rotation: float32 [1024, 1024], P('band'), may hold values from -0.1875 to 0.1875
Outputs:
- rotated: float32 [1024, 131072], P('band', 'dom')
The draws below stay inside these ranges and needn't reach their ends.
Inputs may be any that keep to these rules, and one draw needn't show every extreme that they name: `atom_home`: a permutation; atom a is owned by domain atom_home[a] // 3, so every domain owns 3 atoms. `slot_atom`: in one domain at most 2 windows have atoms of one owner; in every domain some owner has exactly 2 of them, and some owner has exactly 2 from every domain.
All inputs are finite; a program needn't handle non-finite values.
Results may differ from the reference program's by a relative error of at most 0.0003.
Values sent between devices are 32-bit elements; how exact they have to be, the bound alone decides.
A program may use at most 128 MiB of HBM per device.

```python
import jax
import jax.numpy as jnp
from jax import lax

BANDS = 1024
PROJS = 128
WINDOW = 512
CELLS = 4096
SLOTS = 32
ATOM_DEV = 3
GRID = 131072
ATOMS = 96
CAPACITY = 2
N_DOM = 32


def intersection_layout(key):
    folded = jax.random.fold_in(key, 4242)
    key_home, key_full, key_second, key_rank, key_order, key_pick = jax.random.split(folded, 6)
    domains = ATOMS // ATOM_DEV
    places = domains * CAPACITY
    atom_home = jax.random.permutation(key_home, ATOMS).astype(jnp.int32)
    atom_at_row = jnp.argsort(atom_home).astype(jnp.int32)
    shared = jax.random.randint(key_full, (), 0, domains)
    second_owner = jax.random.randint(key_second, (domains, 1), 0, domains)
    ranking = jax.vmap(lambda subkey: jax.random.permutation(subkey, places))(jax.random.split(key_rank, domains)).astype(jnp.int32)
    positions = jnp.arange(places, dtype=jnp.int32)[None, :]
    owner_of = positions // CAPACITY
    within = positions % CAPACITY
    priority = ranking + 2 * places
    priority = jnp.where(owner_of == second_owner, CAPACITY + within, priority)
    priority = jnp.where(owner_of == shared, within, priority)
    chosen = jnp.argsort(priority, axis=1)[:, :SLOTS].astype(jnp.int32)
    mixing = jax.vmap(lambda subkey: jax.random.permutation(subkey, SLOTS))(jax.random.split(key_order, domains))
    chosen = jnp.take_along_axis(chosen, mixing, axis=1)
    owners = chosen // CAPACITY
    atom_pick = jax.random.randint(key_pick, (domains, SLOTS), 0, ATOM_DEV)
    slot_atom = atom_at_row[owners * ATOM_DEV + atom_pick]
    return (atom_home, slot_atom.astype(jnp.int32))


def draw_slot_atom(key, part):
    return intersection_layout(key)[1]


def draw_atom_home(key, part):
    return intersection_layout(key)[0]


def with_ends(array, stream_key, low, largest):
    place = [jax.random.randint(jax.random.fold_in(stream_key, axis), (), 0, length) for axis, length in enumerate(array.shape)]
    widest = array.shape.index(max(array.shape))
    next_to = place[:widest] + [(place[widest] + 1) % array.shape[widest]] + place[widest + 1:]
    return array.at[tuple(place)].set(low).at[tuple(next_to)].set(largest)


def shard_levels(rng, extent, cuts, least, largest):
    gain = 1.0
    for position, parts in cuts:
        steps = jax.random.uniform(jax.random.fold_in(jax.random.fold_in(rng, 6), position), (parts,), jnp.float32, least / len(cuts), largest / len(cuts))
        gain = gain * jnp.repeat(jnp.exp(steps), extent[position] // parts).reshape((-1,) + (1,) * (len(extent) - 1 - position))
    return gain


def scatter_about(stream_key, shape, spread, limit, shards=(), kind=jnp.bfloat16):
    level = shard_levels(stream_key, shape, shards, -0.22, 0.18) if shards else 1.0
    entries = jax.random.normal(stream_key, shape, jnp.float32) * spread * level
    return jnp.minimum(jnp.maximum(entries, -limit), limit).astype(kind)


def setup_inputs(seed: int = 0) -> dict:
    streams_of = jax.random.split(jax.random.key(seed), 8)
    orbitals = scatter_about(streams_of[0], (BANDS, GRID), 1.0, 6.0, ((0, 4), (1, 32)), jnp.float32)
    projectors = scatter_about(streams_of[1], (N_DOM * SLOTS, WINDOW, PROJS), WINDOW ** -0.5, 0.25, ((0, 32),), jnp.float32)
    window_start = with_ends(jax.random.randint(streams_of[2], (N_DOM * SLOTS,), 0, CELLS - WINDOW + 1), jax.random.fold_in(streams_of[2], 1), 0, CELLS - WINDOW).astype(jnp.int32)
    slot_atom = draw_slot_atom(jax.random.fold_in(streams_of[7], 71), 0)
    atom_home = draw_atom_home(jax.random.fold_in(streams_of[7], 71), 0)
    atom_matrices = scatter_about(streams_of[5], (ATOMS, PROJS, PROJS), (8 * PROJS) ** -0.5, 0.1875, ((0, 32),), jnp.float32)
    rotation = scatter_about(streams_of[6], (BANDS, BANDS), BANDS ** -0.5, 0.1875, ((0, 4),), jnp.float32)
    return dict(orbitals=orbitals, projectors=projectors, window_start=window_start, slot_atom=slot_atom, atom_home=atom_home, atom_matrices=atom_matrices, rotation=rotation)


HIGHEST = lax.Precision.HIGHEST


def reference(orbitals, projectors, window_start, slot_atom, atom_home, atom_matrices, rotation):
    atom_ids = jnp.arange(ATOMS, dtype=jnp.int32)

    def domain_pieces(domain):
        domain = domain.astype(jnp.int32)
        block = lax.dynamic_slice_in_dim(orbitals, domain * CELLS, CELLS, 1)
        starts = lax.dynamic_slice_in_dim(window_start, domain * SLOTS, SLOTS, 0)
        tiles = lax.dynamic_slice_in_dim(projectors, domain * SLOTS, SLOTS, 0)
        members = lax.dynamic_index_in_dim(slot_atom, domain, 0, keepdims=False)
        return block, starts, tiles, members

    def accumulate(domain, totals):
        block, starts, tiles, members = domain_pieces(domain)
        windows = jax.vmap(lambda offset: lax.dynamic_slice_in_dim(block, offset, WINDOW, 1))(starts)
        partials = jnp.einsum("sbw,swp->sbp", windows, tiles, precision=HIGHEST)
        matching = (atom_ids[:, None] == members[None, :]).astype(jnp.float32)
        return totals + jnp.einsum("as,sbp->abp", matching, partials, precision=HIGHEST)

    atom_sums = lax.fori_loop(0, N_DOM, accumulate, jnp.zeros((ATOMS, BANDS, PROJS), jnp.float32))
    matrices = atom_matrices[atom_home]
    factors = jnp.einsum("abp,apq->abq", atom_sums, matrices, precision=HIGHEST)

    def correct(domain):
        block, starts, tiles, members = domain_pieces(domain)
        slot_factors = factors[members]
        updates = jnp.einsum("sbq,swq->sbw", slot_factors, tiles, precision=HIGHEST)

        def add_window(slot_index, current):
            offset = starts[slot_index]
            previous = lax.dynamic_slice_in_dim(current, offset, WINDOW, 1)
            return lax.dynamic_update_slice_in_dim(current, previous + updates[slot_index], offset, 1)

        return lax.fori_loop(0, SLOTS, add_window, block)

    corrected_blocks = lax.map(correct, jnp.arange(N_DOM, dtype=jnp.int32))
    corrected = jnp.transpose(corrected_blocks, (1, 0, 2)).reshape(BANDS, GRID)
    return jnp.dot(rotation, corrected, precision=HIGHEST, preferred_element_type=jnp.float32)
```

```python
import functools

import jax
import jax.numpy as jnp
from jax import lax
from jax.experimental import pallas as pl
from jax.experimental.pallas import tpu as pltpu
from jax.sharding import PartitionSpec as P

HIGH = lax.Precision.HIGH
LANES = 128
GROUP = 4


def split(value):
    high = value.astype(jnp.bfloat16)
    low = (value - high.astype(jnp.float32)).astype(jnp.bfloat16)
    return high, low


def dot(a, b):
    return jnp.dot(a, b, preferred_element_type=jnp.float32)


def dot_nt(a, b):
    return lax.dot_general(a, b, (((1,), (1,)), ((), ())), preferred_element_type=jnp.float32)


def place(start, cells, wide):
    tile = jnp.minimum(start // LANES, (cells - wide) // LANES)
    return pl.multiple_of(tile * LANES, LANES), start - tile * LANES


def shifted(projector, pad, shift, window, wide):
    pad[pl.ds(LANES, window), :] = projector
    return split(pad[pl.ds(LANES - shift, wide), :])


def clear(pad, window):
    edge = jnp.zeros((LANES, pad.shape[1]), jnp.float32)
    pad[pl.ds(0, LANES), :] = edge
    pad[pl.ds(LANES + window, LANES), :] = edge


def project_kernel(dom, start, slot_atom, home, orbitals, projectors, sums, high, low, *pads):
    step = pl.program_id(0)
    group, window, _ = projectors.shape
    cells = orbitals.shape[1]
    wide = window + LANES

    @pl.when(step == 0)
    def _():
        for pad in pads:
            clear(pad, window)
        sums[...] = jnp.zeros_like(sums)
        value = orbitals[...]
        top, rest = split(value)
        high[...] = top
        low[...] = rest

    for k in range(group):
        slot = step * group + k
        row = home[slot_atom[dom[0], slot]]
        cell, shift = place(start[slot], cells, wide)
        p_high, p_low = shifted(projectors[k], pads[k], shift, window, wide)
        o_high = high[:, pl.ds(cell, wide)]
        o_low = low[:, pl.ds(cell, wide)]
        both = dot(o_high, jnp.concatenate([p_high, p_low], axis=1))
        projs = p_high.shape[1]
        sums[row] += both[:, :projs] + both[:, projs:] + dot(o_low, p_high)


def project(dom, start, slot_atom, home, orbitals, projectors):
    slots, window, projs = projectors.shape
    bands, cells = orbitals.shape
    atoms = home.shape[0]
    return pl.pallas_call(
        project_kernel,
        out_shape=jax.ShapeDtypeStruct((atoms, bands, projs), jnp.float32),
        grid_spec=pltpu.PrefetchScalarGridSpec(
            num_scalar_prefetch=4,
            grid=(slots // GROUP,),
            in_specs=[
                pl.BlockSpec((bands, cells), lambda i, *_: (0, 0), pipeline_mode=pl.Buffered(1)),
                pl.BlockSpec((GROUP, window, projs), lambda i, *_: (i, 0, 0)),
            ],
            out_specs=pl.BlockSpec(
                (atoms, bands, projs), lambda i, *_: (0, 0, 0), pipeline_mode=pl.Buffered(1)
            ),
            scratch_shapes=[pltpu.VMEM((bands, cells), jnp.bfloat16)] * 2
            + [pltpu.VMEM((window + 2 * LANES, projs), jnp.float32)] * GROUP,
        ),
        cost_estimate=pl.CostEstimate(
            flops=6 * slots * window * bands * projs, bytes_accessed=28 << 20, transcendentals=0
        ),
        compiler_params=pltpu.CompilerParams(vmem_limit_bytes=40 << 20),
        name="project",
    )(dom, start, slot_atom, home, orbitals, projectors)


def update_kernel(dom, start, slot_atom, home, *refs):
    group = GROUP
    factors = refs[:group]
    projectors, rotated, out = refs[group : group + 3]
    pads = refs[group + 3 :]
    step = pl.program_id(0)
    _, window, _ = projectors.shape
    cells = out.shape[1]
    wide = window + LANES

    @pl.when(step == 0)
    def _():
        for pad in pads:
            clear(pad, window)
        out[...] = rotated[...]

    for k in range(group):
        slot = step * group + k
        cell, shift = place(start[slot], cells, wide)
        p_high, p_low = shifted(projectors[k], pads[k], shift, window, wide)
        f_high, f_low = split(factors[k][0])
        update = dot_nt(
            jnp.concatenate([f_high, f_low, f_high], axis=1),
            jnp.concatenate([p_high, p_high, p_low], axis=1),
        )
        out[:, pl.ds(cell, wide)] += update


def update(dom, start, slot_atom, home, factors, projectors, rotated):
    slots, window, projs = projectors.shape
    bands, cells = rotated.shape

    def factor_spec(k):
        return pl.BlockSpec(
            (1, bands, projs),
            lambda i, d, s, a, h: (h[a[d[0], i * GROUP + k]], 0, 0),
        )

    return pl.pallas_call(
        update_kernel,
        out_shape=jax.ShapeDtypeStruct((bands, cells), jnp.float32),
        grid_spec=pltpu.PrefetchScalarGridSpec(
            num_scalar_prefetch=4,
            grid=(slots // GROUP,),
            in_specs=[factor_spec(k) for k in range(GROUP)]
            + [
                pl.BlockSpec((GROUP, window, projs), lambda i, *_: (i, 0, 0)),
                pl.BlockSpec((bands, cells), lambda i, *_: (0, 0), pipeline_mode=pl.Buffered(1)),
            ],
            out_specs=pl.BlockSpec(
                (bands, cells), lambda i, *_: (0, 0), pipeline_mode=pl.Buffered(1)
            ),
            scratch_shapes=[pltpu.VMEM((window + 2 * LANES, projs), jnp.float32)] * GROUP,
        ),
        cost_estimate=pl.CostEstimate(
            flops=6 * slots * window * bands * projs, bytes_accessed=20 << 20, transcendentals=0
        ),
        compiler_params=pltpu.CompilerParams(vmem_limit_bytes=40 << 20),
        name="update",
    )(dom, start, slot_atom, home, *([factors] * GROUP), projectors, rotated)


def per_device(orbitals, projectors, window_start, slot_atom, atom_home, atom_matrices, rotation):
    dom = lax.axis_index("dom").astype(jnp.int32).reshape(1)
    every = lax.all_gather(orbitals, "band", axis=0, tiled=True)
    sums = project(dom, window_start, slot_atom, atom_home, orbitals, projectors)
    owned = lax.psum_scatter(sums, "dom", scatter_dimension=0, tiled=True)
    owned = lax.all_gather(owned, "band", axis=1, tiled=True)
    owned = jnp.einsum("cb,abp->acp", rotation, owned, precision=HIGH)
    owned = jnp.einsum("acp,apq->acq", owned, atom_matrices, precision=HIGH)
    factors = lax.all_gather(owned, "dom", axis=0, tiled=True)
    rotated = jnp.dot(rotation, every, precision=HIGH, preferred_element_type=jnp.float32)
    return update(dom, window_start, slot_atom, atom_home, factors, projectors, rotated)


def solution(mesh):
    in_specs = (
        P("band", "dom"),
        P("dom", None, None),
        P("dom"),
        P(),
        P(),
        P("dom", None, None),
        P("band", None),
    )
    out_specs = P("band", "dom")
    return jax.shard_map(
        per_device, mesh=mesh, in_specs=in_specs, out_specs=out_specs, check_vma=False
    )
```

```python
import jax
import jax.numpy as jnp
from jax import lax
from jax.experimental import pallas as pl
from jax.experimental.pallas import tpu as pltpu
from jax.sharding import PartitionSpec as P

LANES = 128
GROUP = 4


def split(value):
    high = value.astype(jnp.bfloat16)
    low = (value - high.astype(jnp.float32)).astype(jnp.bfloat16)
    return high, low


def dot(a, b):
    return jnp.dot(a, b, preferred_element_type=jnp.float32)


def dot_nt(a, b):
    return lax.dot_general(a, b, (((1,), (1,)), ((), ())), preferred_element_type=jnp.float32)


def place(start, cells, wide):
    tile = jnp.minimum(start // LANES, (cells - wide) // LANES)
    return pl.multiple_of(tile * LANES, LANES), start - tile * LANES


def shifted(projector, pad, shift, window, wide):
    pad[pl.ds(LANES, window), :] = projector
    return split(pad[pl.ds(LANES - shift, wide), :])


def clear(pad, window):
    edge = jnp.zeros((LANES, pad.shape[1]), jnp.float32)
    pad[pl.ds(0, LANES), :] = edge
    pad[pl.ds(LANES + window, LANES), :] = edge


def project_kernel(dom, start, slot_atom, home, orbitals, projectors, sums, high, low, *pads):
    step = pl.program_id(0)
    group, window, _ = projectors.shape
    cells = orbitals.shape[1]
    wide = window + LANES

    @pl.when(step == 0)
    def _():
        for pad in pads:
            clear(pad, window)
        sums[...] = jnp.zeros_like(sums)
        value = orbitals[...]
        top, rest = split(value)
        high[...] = top
        low[...] = rest

    for k in range(group):
        slot = step * group + k
        row = home[slot_atom[dom[0], slot]]
        cell, shift = place(start[slot], cells, wide)
        p_high, p_low = shifted(projectors[k], pads[k], shift, window, wide)
        o_high = high[:, pl.ds(cell, wide)]
        o_low = low[:, pl.ds(cell, wide)]
        both = dot(o_high, jnp.concatenate([p_high, p_low], axis=1))
        projs = p_high.shape[1]
        sums[row] += both[:, :projs] + both[:, projs:] + dot(o_low, p_high)


def project(dom, start, slot_atom, home, orbitals, projectors):
    slots, window, projs = projectors.shape
    bands, cells = orbitals.shape
    atoms = home.shape[0]
    return pl.pallas_call(
        project_kernel,
        out_shape=jax.ShapeDtypeStruct((atoms, bands, projs), jnp.float32),
        grid_spec=pltpu.PrefetchScalarGridSpec(
            num_scalar_prefetch=4,
            grid=(slots // GROUP,),
            in_specs=[
                pl.BlockSpec((bands, cells), lambda i, *_: (0, 0), pipeline_mode=pl.Buffered(1)),
                pl.BlockSpec((GROUP, window, projs), lambda i, *_: (i, 0, 0)),
            ],
            out_specs=pl.BlockSpec(
                (atoms, bands, projs), lambda i, *_: (0, 0, 0), pipeline_mode=pl.Buffered(1)
            ),
            scratch_shapes=[pltpu.VMEM((bands, cells), jnp.bfloat16)] * 2
            + [pltpu.VMEM((window + 2 * LANES, projs), jnp.float32)] * GROUP,
        ),
        cost_estimate=pl.CostEstimate(
            flops=6 * slots * window * bands * projs, bytes_accessed=28 << 20, transcendentals=0
        ),
        compiler_params=pltpu.CompilerParams(vmem_limit_bytes=40 << 20),
        name="project",
    )(dom, start, slot_atom, home, orbitals, projectors)


def update_kernel(dom, start, slot_atom, home, *refs):
    group = GROUP
    factors = refs[:group]
    projectors, rotated, out = refs[group : group + 3]
    pads = refs[group + 3 :]
    step = pl.program_id(0)
    _, window, _ = projectors.shape
    cells = out.shape[1]
    wide = window + LANES

    @pl.when(step == 0)
    def _():
        for pad in pads:
            clear(pad, window)
        out[...] = rotated[...]

    for k in range(group):
        slot = step * group + k
        cell, shift = place(start[slot], cells, wide)
        p_high, p_low = shifted(projectors[k], pads[k], shift, window, wide)
        f_high, f_low = split(factors[k][0])
        update = dot_nt(
            jnp.concatenate([f_high, f_low, f_high], axis=1),
            jnp.concatenate([p_high, p_high, p_low], axis=1),
        )
        out[:, pl.ds(cell, wide)] += update


def update(dom, start, slot_atom, home, factors, projectors, rotated):
    slots, window, projs = projectors.shape
    bands, cells = rotated.shape

    def factor_spec(k):
        return pl.BlockSpec(
            (1, bands, projs),
            lambda i, d, s, a, h: (h[a[d[0], i * GROUP + k]], 0, 0),
        )

    return pl.pallas_call(
        update_kernel,
        out_shape=jax.ShapeDtypeStruct((bands, cells), jnp.float32),
        grid_spec=pltpu.PrefetchScalarGridSpec(
            num_scalar_prefetch=4,
            grid=(slots // GROUP,),
            in_specs=[factor_spec(k) for k in range(GROUP)]
            + [
                pl.BlockSpec((GROUP, window, projs), lambda i, *_: (i, 0, 0)),
                pl.BlockSpec((bands, cells), lambda i, *_: (0, 0), pipeline_mode=pl.Buffered(1)),
            ],
            out_specs=pl.BlockSpec(
                (bands, cells), lambda i, *_: (0, 0), pipeline_mode=pl.Buffered(1)
            ),
            scratch_shapes=[pltpu.VMEM((window + 2 * LANES, projs), jnp.float32)] * GROUP,
        ),
        cost_estimate=pl.CostEstimate(
            flops=6 * slots * window * bands * projs, bytes_accessed=20 << 20, transcendentals=0
        ),
        compiler_params=pltpu.CompilerParams(vmem_limit_bytes=40 << 20),
        name="update",
    )(dom, start, slot_atom, home, *([factors] * GROUP), projectors, rotated)


MESH = pl.DeviceIdType.MESH
RING = 4
ORDER = (2, 1, 3, 0)


def ring(position, offset):
    return lax.rem(position + offset, RING)


def tile_of(index, size):
    return pl.ds(pl.multiple_of(index * size, size), size)


class Links:
    def __init__(self):
        self.band = lax.axis_index("band")
        dom = lax.axis_index("dom")
        self.core = lax.rem(dom, 2)
        self.z = lax.rem(dom // 2, RING)
        self.x = dom // (2 * RING)

    def place(self, band, x, z, core):
        return (band, (x * RING + z) * 2 + core)

    def at_band(self, offset):
        return self.place(ring(self.band, offset), self.x, self.z, self.core)

    def at_x(self, offset):
        return self.place(self.band, ring(self.x, offset), self.z, self.core)

    def at_z(self, offset):
        return self.place(self.band, self.x, ring(self.z, offset), self.core)

    def partner(self):
        return self.place(self.band, self.x, self.z, 1 - self.core)


def exchange_kernel(
    sums, orbitals, rotation, matrices, factors, rotated,
    cells_in, cells_out, full, r_high, r_low, total, mate, hop1, hop2, hop3, hop4, gathered, owned,
    sem_load, sem_keep, sem_own, *sems
):
    link = Links()
    b, x, z, c = link.band, link.x, link.z, link.core
    names = ("yin", "yout", "r1", "r2", "r3", "s0", "one", "two", "sum", "ag1", "ag2", "agf", "core")
    send = dict(zip(names, sems[0::2]))
    recv = dict(zip(names, sems[1::2]))
    bands, cells = orbitals.shape
    quarter = cells // RING
    parts = cells_in.shape[0]
    width = quarter // parts
    half = bands // 2
    sub = half // 2
    started = []

    def push(src, dst, kind, index, device):
        copy = pltpu.make_async_remote_copy(
            src_ref=src, dst_ref=dst, send_sem=send[kind].at[index], recv_sem=recv[kind].at[index],
            device_id=device, device_id_type=MESH,
        )
        copy.start()
        started.append(copy)
        return copy

    def keep(src, dst, sem):
        copy = pltpu.make_async_copy(src, dst, sem)
        copy.start()
        return copy

    barrier = pltpu.get_barrier_semaphore()
    peers = [f(o) for f in (link.at_band, link.at_x, link.at_z) for o in (1, 2, 3)] + [link.partner()]
    for peer in peers:
        pl.semaphore_signal(barrier, inc=1, device_id=peer, device_id_type=MESH)
    pl.semaphore_wait(barrier, len(peers))

    first = (x, z)
    second = (z, x)
    at_first = (link.at_x, link.at_z)
    at_second = (link.at_z, link.at_x)

    def sums_at(h, t, core):
        rows = pl.ds(h * half, half)
        if h == 0:
            return sums.at[t, :, core, :, rows, :]
        return sums.at[:, t, core, :, rows, :]

    def factor_at(h, t, u, core, low=0, size=None):
        rows = pl.ds(h * half + low, half if size is None else size)
        if h == 0:
            return factors.at[t, u, core, :, rows, :]
        return factors.at[u, t, core, :, rows, :]

    mates, loads = {}, {}
    for o in ORDER:
        for h in range(2):
            t = ring(first[h], o)
            mates[h, o] = push(sums_at(h, t, 1 - c), mate.at[h, t], "s0", (h, o), link.partner())
            loads[h, o] = keep(sums_at(h, t, c), total.at[h, t], sem_load.at[h, o])
    r1 = {}
    for o in (1, 2, 3):
        for h in range(2):
            piece = (h, first[h], c)
            r1[o, h] = push(rotation.at[piece], full.at[(b,) + piece], "r1", (o - 1, h), link.at_band(o))
    own_rows = keep(rotation, full.at[b], sem_own.at[0])
    yin, own_cells = {}, []
    for i in range(parts):
        for o in (1, 2, 3):
            src = orbitals.at[:, tile_of(ring(b, o) * parts + i, width)]
            yin[i, o] = push(src, cells_in.at[i, b], "yin", (i, o - 1), link.at_band(o))
        own_cells.append(keep(orbitals.at[:, tile_of(b * parts + i, width)], cells_in.at[i, b], sem_keep.at[i]))

    one, two = {}, {}

    def gather_mate(h, o):
        t = ring(first[h], o)
        loads[h, o].wait()
        mates[h, o].wait_recv()

        def body(u, carry):
            total[h, t, u] += mate[h, t, u]
            return carry

        lax.fori_loop(0, RING, body, 0)

    low2, high2 = pl.ds(0, 2), pl.ds(2, 2)
    for h in range(2):
        gather_mate(h, 2)
        t = ring(first[h], 2)
        one[h, 0, 0] = push(total.at[h, t, low2], hop1.at[h, 0], "one", (h, 0, 0), at_first[h](1))
        one[h, 1, 0] = push(total.at[h, t, high2], hop1.at[h, 1], "one", (h, 1, 0), at_first[h](3))
    for h in range(2):
        gather_mate(h, 1)
        t = ring(first[h], 1)
        one[h, 0, 1] = push(total.at[h, t, high2], hop2.at[h, 0, high2], "one", (h, 0, 1), at_first[h](1))
        gather_mate(h, 3)
        t = ring(first[h], 3)
        one[h, 1, 1] = push(total.at[h, t, low2], hop2.at[h, 1, low2], "one", (h, 1, 1), at_first[h](3))

    r2 = {}
    for o in (1, 2, 3):
        k = ring(b, RING - o)
        for h in range(2):
            r1[o, h].wait_recv()
            piece = (k, h, first[h], c)
            for p in (1, 2, 3):
                r2[o, p, h] = push(full.at[piece], full.at[piece], "r2", (o - 1, p - 1, h), at_first[h](p))

    for h in range(2):
        gather_mate(h, 0)

    def add_rows(h, t, start, source):
        def body(u, carry):
            total[h, t, start + u] += source[h, start // 2, u]
            return carry

        lax.fori_loop(0, 2, body, 0)

    for h in range(2):
        one[h, 0, 0].wait_recv()
        t = ring(first[h], 1)
        add_rows(h, t, 0, hop1)
        one[h, 0, 2] = push(total.at[h, t, low2], hop2.at[h, 0, low2], "one", (h, 0, 2), at_first[h](1))
        one[h, 1, 0].wait_recv()
        t = ring(first[h], 3)
        add_rows(h, t, 2, hop1)
        one[h, 1, 2] = push(total.at[h, t, high2], hop2.at[h, 1, high2], "one", (h, 1, 2), at_first[h](3))

    r3 = {}
    for o in (1, 2, 3):
        k = ring(b, RING - o)
        for h in range(2):
            for p in (1, 2, 3):
                r2[o, p, h].wait_recv()
        mine = full.at[k, :, :, c]
        r3[o] = push(mine, mine, "r3", (o - 1,), link.partner())

    own_rows.wait()
    for o in (1, 2, 3):
        r3[o].wait_recv()

    def split_rows(k, carry):
        top, rest = split(full[k].reshape(bands, full.shape[-1]))
        r_high[k] = top
        r_low[k] = rest
        return carry

    lax.fori_loop(0, RING, split_rows, 0)

    yout, own_out = {}, []

    def rotate(i):
        for o in (1, 2, 3):
            yin[i, o].wait_recv()
        own_cells[i].wait()
        high, low = split(cells_in[i].reshape(RING * bands, width))
        pair = jnp.concatenate([high, low], axis=1)

        def body(k, carry):
            both = dot(r_high[k], pair)
            cells_out[i, k] = both[:, :width] + both[:, width:] + dot(r_low[k], high)
            return carry

        lax.fori_loop(0, RING, body, 0)
        columns = tile_of(b * parts + i, width)
        for o in (1, 2, 3):
            src = cells_out.at[i, ring(b, o)]
            yout[i, o] = push(src, rotated.at[:, columns], "yout", (i, o - 1), link.at_band(o))
        own_out.append(keep(cells_out.at[i, b], rotated.at[:, columns], sem_keep.at[parts + i]))

    rotate(0)

    for h in range(2):
        t = first[h]
        one[h, 0, 1].wait_recv()
        one[h, 1, 1].wait_recv()
        one[h, 0, 2].wait_recv()
        one[h, 1, 2].wait_recv()

        def finish(u, carry, h=h, t=t):
            total[h, t, u] += hop2[h, 0, u] + hop2[h, 1, u]
            return carry

        lax.fori_loop(0, RING, finish, 0)
        lower, upper = pl.ds(0, sub), pl.ds(sub, sub)
        s = second[h]
        far, nxt, prv = ring(s, 2), ring(s, 1), ring(s, 3)
        two[h, 0, 0] = push(total.at[h, t, far, :, lower], hop3.at[h, 0], "two", (h, 0, 0), at_second[h](1))
        two[h, 1, 0] = push(total.at[h, t, far, :, upper], hop3.at[h, 1], "two", (h, 1, 0), at_second[h](3))
        two[h, 0, 1] = push(
            total.at[h, t, nxt, :, upper], hop4.at[h, 0, :, upper], "two", (h, 0, 1), at_second[h](1)
        )
        two[h, 1, 1] = push(
            total.at[h, t, prv, :, lower], hop4.at[h, 1, :, lower], "two", (h, 1, 1), at_second[h](3)
        )

    for h in range(2):
        t, s = first[h], second[h]
        nxt, prv = ring(s, 1), ring(s, 3)
        two[h, 0, 0].wait_recv()
        total[h, t, nxt, :, lower] += hop3[h, 0]
        two[h, 0, 2] = push(
            total.at[h, t, nxt, :, lower], hop4.at[h, 0, :, lower], "two", (h, 0, 2), at_second[h](1)
        )
        two[h, 1, 0].wait_recv()
        total[h, t, prv, :, upper] += hop3[h, 1]
        two[h, 1, 2] = push(
            total.at[h, t, prv, :, upper], hop4.at[h, 1, :, upper], "two", (h, 1, 2), at_second[h](3)
        )

    rotate(1)

    for h in range(2):
        t, s = first[h], second[h]
        for d in range(2):
            two[h, d, 1].wait_recv()
            two[h, d, 2].wait_recv()
        gathered[b, :, pl.ds(h * half, half), :] = total[h, t, s] + hop4[h, 0] + hop4[h, 1]
    swap = {}
    for o in (1, 2, 3):
        swap[o] = push(gathered.at[b], gathered.at[b], "sum", (o - 1,), link.at_band(o))

    rotate(2)

    for o in (1, 2, 3):
        swap[o].wait_recv()
    projs = matrices.shape[-1]
    for atom in range(matrices.shape[0]):
        high, low = split(gathered[:, atom].reshape(RING * bands, projs))
        both = dot(r_high[b], jnp.concatenate([high, low], axis=1))
        turned = both[:, :projs] + both[:, projs:] + dot(r_low[b], high)
        t_high, t_low = split(turned)
        m_high, m_low = split(matrices[atom])
        both = dot(t_high, jnp.concatenate([m_high, m_low], axis=1))
        owned[atom] = both[:, :projs] + both[:, projs:] + dot(t_low, m_high)

    own_factor = keep(owned, factors.at[x, z, c], sem_own.at[1])
    mate_core = []

    def to_mate(src, h, t, u, index):
        mate_core.append(push(src, factor_at(h, t, u, c), "core", (h, index), link.partner()))

    ag1, ag2, agf = {}, {}, {}
    for h in range(2):
        t, s = first[h], second[h]
        for d, peer, order in ((0, 1, (0, 1)), (1, 3, (1, 0))):
            for m, part in enumerate(order):
                rows = pl.ds(h * half + part * sub, sub)
                ag1[h, d, m] = push(
                    owned.at[:, rows], factor_at(h, t, s, c, part * sub, sub), "ag1", (h, d, m), at_second[h](peer)
                )
    def spread(h, r, src, u):
        t = first[h]
        for d, peer in ((0, 1), (1, 3)):
            ag2[h, d, r] = push(src, factor_at(h, t, u, c), "ag2", (h, d, r), at_first[h](peer))
        to_mate(src, h, t, u, r)

    lines = (0, 3, 1, 2)
    for h in range(2):
        spread(h, 0, owned.at[:, pl.ds(h * half, half)], second[h])
    for h in range(2):
        t, s = first[h], second[h]
        for d, back, peer in ((0, 3, 1), (1, 1, 3)):
            ag1[h, d, 0].wait_recv()
            piece = factor_at(h, t, ring(s, back), c, d * sub, sub)
            ag1[h, d, 2] = push(piece, piece, "ag1", (h, d, 2), at_second[h](peer))
    for h in range(2):
        t, s = first[h], second[h]
        for d, r in ((0, 1), (1, 2)):
            ag1[h, d, 1].wait_recv()
            u = ring(s, lines[r])
            spread(h, r, factor_at(h, t, u, c), u)
    for h in range(2):
        t, s = first[h], second[h]
        ag1[h, 0, 2].wait_recv()
        ag1[h, 1, 2].wait_recv()
        u = ring(s, 2)
        spread(h, 3, factor_at(h, t, u, c), u)

    rotate(3)

    for r in range(RING):
        for h in range(2):
            u = ring(second[h], lines[r])
            for d, back, peer in ((0, 3, 1), (1, 1, 3)):
                ag2[h, d, r].wait_recv()
                t = ring(first[h], back)
                piece = factor_at(h, t, u, c)
                if (r < 2) == (d == 0):
                    agf[h, r] = push(piece, piece, "agf", (h, r), at_first[h](peer))
                to_mate(piece, h, t, u, RING * (1 + d) + r)
    for r in range(RING):
        for h in range(2):
            u = ring(second[h], lines[r])
            agf[h, r].wait_recv()
            t = ring(first[h], 2)
            to_mate(factor_at(h, t, u, c), h, t, u, RING * 3 + r)

    for copy in mate_core:
        copy.wait_recv()
    for copy in yout.values():
        copy.wait_recv()
    for copy in own_out:
        copy.wait()
    own_factor.wait()
    for copy in started:
        copy.wait_send()


PARTS = 4


def exchange(sums, orbitals, rotation, matrices):
    atoms, bands, projs = sums.shape
    cells = orbitals.shape[1]
    all_bands = rotation.shape[1]
    group = atoms // (2 * RING * RING)
    width = cells // RING // PARTS
    half = bands // 2
    sub = half // 2
    rows = bands // (4 * RING)
    f32, bf16 = jnp.float32, jnp.bfloat16
    counts = [
        (PARTS, 3), (PARTS, 3), (3, 2), (3, 3, 2), (3,), (2, RING), (2, 2, 3), (2, 2, 3), (3,),
        (2, 2, 3), (2, 2, RING), (2, RING), (2, 4 * RING),
    ]
    dma = pltpu.SemaphoreType.DMA
    factors, rotated = pl.pallas_call(
        exchange_kernel,
        out_shape=(
            jax.ShapeDtypeStruct((RING, RING, 2, group, bands, projs), f32),
            jax.ShapeDtypeStruct((bands, cells), f32),
        ),
        in_specs=[pl.BlockSpec(memory_space=pl.ANY)] * 3 + [pl.BlockSpec(memory_space=pltpu.VMEM)],
        out_specs=[pl.BlockSpec(memory_space=pl.ANY)] * 2,
        scratch_shapes=[
            pltpu.VMEM((PARTS, RING, bands, width), f32),
            pltpu.VMEM((PARTS, RING, bands, width), f32),
            pltpu.VMEM((RING, 2, RING, 2, rows, all_bands), f32),
            pltpu.VMEM((RING, bands, all_bands), bf16),
            pltpu.VMEM((RING, bands, all_bands), bf16),
            pltpu.VMEM((2, RING, RING, group, half, projs), f32),
            pltpu.VMEM((2, RING, RING, group, half, projs), f32),
            pltpu.VMEM((2, 2, 2, group, half, projs), f32),
            pltpu.VMEM((2, 2, RING, group, half, projs), f32),
            pltpu.VMEM((2, 2, group, sub, projs), f32),
            pltpu.VMEM((2, 2, group, half, projs), f32),
            pltpu.VMEM((RING, group, bands, projs), f32),
            pltpu.VMEM((group, bands, projs), f32),
            dma((2, RING)),
            dma((2 * PARTS,)),
            dma((2,)),
        ]
        + [dma(shape) for shape in counts for _ in range(2)],
        compiler_params=pltpu.CompilerParams(
            collective_id=0, has_side_effects=True, vmem_limit_bytes=52 << 20
        ),
        name="exchange",
    )(
        sums.reshape(RING, RING, 2, group, bands, projs),
        orbitals,
        rotation.reshape(2, RING, 2, rows, all_bands),
        matrices,
    )
    return factors.reshape(atoms, bands, projs), rotated


def per_device(orbitals, projectors, window_start, slot_atom, atom_home, atom_matrices, rotation):
    dom = lax.axis_index("dom").astype(jnp.int32).reshape(1)
    sums = project(dom, window_start, slot_atom, atom_home, orbitals, projectors)
    factors, rotated = exchange(sums, orbitals, rotation, atom_matrices)
    return update(dom, window_start, slot_atom, atom_home, factors, projectors, rotated)


def solution(mesh):
    in_specs = (
        P("band", "dom"),
        P("dom", None, None),
        P("dom"),
        P(),
        P(),
        P("dom", None, None),
        P("band", None),
    )
    out_specs = P("band", "dom")
    return jax.shard_map(
        per_device, mesh=mesh, in_specs=in_specs, out_specs=out_specs, check_vma=False
    )
```

```python
import functools

import jax
import jax.numpy as jnp
from jax import lax
from jax.experimental import pallas as pl
from jax.experimental.pallas import tpu as pltpu
from jax.sharding import PartitionSpec as P

LANES = 128
GROUP = 4


def split(value):
    high = value.astype(jnp.bfloat16)
    low = (value - high.astype(jnp.float32)).astype(jnp.bfloat16)
    return high, low


def dot(a, b):
    return jnp.dot(a, b, preferred_element_type=jnp.float32)


def dot_nt(a, b):
    return lax.dot_general(a, b, (((1,), (1,)), ((), ())), preferred_element_type=jnp.float32)


def shifted(projector, pad, shift, window, wide):
    pad[pl.ds(LANES, window), :] = projector
    return split(pad[pl.ds(LANES - shift, wide), :])


def clear(pad, window):
    edge = jnp.zeros((LANES, pad.shape[1]), jnp.float32)
    pad[pl.ds(0, LANES), :] = edge
    pad[pl.ds(LANES + window, LANES), :] = edge


TILE, SHIFT, ROW, WHERE = 0, 1, 2, 3
TABLE_ROWS = 16


def list_kernel(dom, start, slot_atom, home, table, weights, *, group, cells, wide):
    lane = lax.broadcasted_iota(jnp.int32, (1, LANES), 1)
    blank = jnp.zeros((1, LANES), jnp.int32)
    none = jnp.full((1, LANES), -1, jnp.int32)
    core = lax.rem(dom[0], 2)

    def enter(domain):
        def body(slot, carry):
            row_of, where0, local0, where1, local1 = carry
            row = home[slot_atom[domain, slot]]
            owner = row // group
            local = row - owner * group
            here = lane == owner
            taken = here & (local0 >= 0)
            fresh = here & (local0 < 0)
            where1 = jnp.where(taken, slot, where1)
            local1 = jnp.where(taken, local, local1)
            where0 = jnp.where(fresh, slot, where0)
            local0 = jnp.where(fresh, local, local0)
            return jnp.where(lane == slot, row, row_of), where0, local0, where1, local1

        return lax.fori_loop(0, start.shape[0], body, (blank, blank, none, blank, none))

    def locate(slot, carry):
        tile = jnp.minimum(start[slot] // LANES, (cells - wide) // LANES)
        cell_of, shift_of = carry
        cell_of = jnp.where(lane == slot, tile, cell_of)
        return cell_of, jnp.where(lane == slot, start[slot] - tile * LANES, shift_of)

    cell_of, shift_of = lax.fori_loop(0, start.shape[0], locate, (blank, blank))
    row_of, own0, own_local0, own1, own_local1 = enter(dom[0])
    _, mate0, mate_local0, mate1, mate_local1 = enter(dom[0] + 1 - 2 * core)
    rows = [cell_of, shift_of, row_of, own0, own1, mate0, mate1]
    for index, row in enumerate(rows):
        table[index : index + 1, :] = row
    for index, local in enumerate([own_local0, own_local1, mate_local0, mate_local1]):
        for atom in range(group):
            at = index * group + atom
            weights[at : at + 1, :] = (local == atom).astype(jnp.float32)


def list_slots(dom, start, slot_atom, home, group, cells, wide):
    return pl.pallas_call(
        functools.partial(list_kernel, group=group, cells=cells, wide=wide),
        out_shape=[jax.ShapeDtypeStruct((TABLE_ROWS, LANES), kind) for kind in (jnp.int32, jnp.float32)],
        in_specs=[pl.BlockSpec(memory_space=pltpu.SMEM)] * 4,
        out_specs=[pl.BlockSpec(memory_space=pltpu.VMEM)] * 2,
        compiler_params=pltpu.CompilerParams(vmem_limit_bytes=60 << 20),
        name="list_slots",
    )(dom, start, slot_atom, home)


def update_kernel(table, *refs):
    group = GROUP
    factors = refs[:group]
    projectors, rotated, out = refs[group : group + 3]
    pads = refs[group + 3 : -1]
    step = pl.program_id(0)
    fetch = pltpu.make_async_copy(rotated, out, refs[-1])
    _, window, _ = projectors.shape
    cells = out.shape[1]
    wide = window + LANES

    @pl.when(step == 0)
    def _():
        fetch.start()
        for pad in pads:
            clear(pad, window)
        fetch.wait()

    for k in range(group):
        slot = step * group + k
        cell, shift = pl.multiple_of(table[TILE, slot] * LANES, LANES), table[SHIFT, slot]
        p_high, p_low = shifted(projectors[k], pads[k], shift, window, wide)
        f_high, f_low = split(factors[k][0])
        update = dot_nt(
            jnp.concatenate([f_high, f_low, f_high], axis=1),
            jnp.concatenate([p_high, p_high, p_low], axis=1),
        )
        out[:, pl.ds(cell, wide)] += update


def update(table, factors, projectors, rotated):
    slots, window, projs = projectors.shape
    bands, cells = rotated.shape

    def factor_spec(k):
        return pl.BlockSpec(
            (1, bands, projs),
            lambda i, table: (table[ROW, i * GROUP + k], 0, 0),
        )

    return pl.pallas_call(
        update_kernel,
        out_shape=jax.ShapeDtypeStruct((bands, cells), jnp.float32),
        grid_spec=pltpu.PrefetchScalarGridSpec(
            num_scalar_prefetch=1,
            grid=(slots // GROUP,),
            in_specs=[factor_spec(k) for k in range(GROUP)]
            + [
                pl.BlockSpec((GROUP, window, projs), lambda i, *_: (i, 0, 0)),
                pl.BlockSpec(memory_space=pltpu.MemorySpace.HBM),
            ],
            out_specs=pl.BlockSpec(
                (bands, cells), lambda i, *_: (0, 0), pipeline_mode=pl.Buffered(1)
            ),
            scratch_shapes=[pltpu.VMEM((window + 2 * LANES, projs), jnp.float32)] * GROUP
            + [pltpu.SemaphoreType.DMA],
        ),
        cost_estimate=pl.CostEstimate(
            flops=6 * slots * window * bands * projs, bytes_accessed=20 << 20, transcendentals=0
        ),
        compiler_params=pltpu.CompilerParams(vmem_limit_bytes=60 << 20),
        name="update",
    )(table, *([factors] * GROUP), projectors, rotated)


MESH = pl.DeviceIdType.MESH
RING = 4
ORDER = (2, 1, 3, 0)


def ring(position, offset):
    return lax.rem(position + offset, RING)


def tile_of(index, size):
    return pl.ds(pl.multiple_of(index * size, size), size)


class Links:
    def __init__(self):
        self.band = lax.axis_index("band")
        dom = lax.axis_index("dom")
        self.core = lax.rem(dom, 2)
        self.z = lax.rem(dom // 2, RING)
        self.x = dom // (2 * RING)

    def place(self, band, x, z, core):
        return (band, (x * RING + z) * 2 + core)

    def at_band(self, offset):
        return self.place(ring(self.band, offset), self.x, self.z, self.core)

    def at_x(self, offset):
        return self.place(self.band, ring(self.x, offset), self.z, self.core)

    def at_z(self, offset):
        return self.place(self.band, self.x, ring(self.z, offset), self.core)

    def partner(self):
        return self.place(self.band, self.x, self.z, 1 - self.core)


def exchange_kernel(
    table, weights, orbitals, projectors, rotation, matrices, factors, rotated,
    cells_in, cells_out, full, high_rows, low_rows, high_cells, low_cells, tiles, windows, mate, total, hop1, hop2, hop3, hop4,
    turn, turn_in, turn_out, turned, owned, pads,
    sem_load, sem_keep, sem_own, *sems
):
    link = Links()
    b, x, z, c = link.band, link.x, link.z, link.core
    names = ("yin", "yout", "r1", "r2", "r3", "s0", "one", "two", "sum", "back", "ag1", "ag2", "agf", "core")
    send = dict(zip(names, sems[0::2]))
    recv = dict(zip(names, sems[1::2]))
    bands, cells = orbitals.shape
    slots, window, projs = projectors.shape
    wide = window + LANES
    group = matrices.shape[0]
    quarter = cells // RING
    parts = cells_in.shape[0]
    width = quarter // parts
    half = bands // 2
    sub = half // 2
    strip = turn.shape[0] // RING
    started = []

    def push(src, dst, kind, index, device):
        copy = pltpu.make_async_remote_copy(
            src_ref=src, dst_ref=dst, send_sem=send[kind].at[index], recv_sem=recv[kind].at[index],
            device_id=device, device_id_type=MESH,
        )
        copy.start()
        started.append(copy)
        return copy

    def keep(src, dst, sem):
        copy = pltpu.make_async_copy(src, dst, sem)
        copy.start()
        return copy

    barrier = pltpu.get_barrier_semaphore()
    peers = [f(o) for f in (link.at_band, link.at_x, link.at_z) for o in (1, 2, 3)] + [link.partner()]
    for peer in peers:
        pl.semaphore_signal(barrier, inc=1, device_id=peer, device_id_type=MESH)
    pl.semaphore_wait(barrier, len(peers))

    first = (x, z)
    second = (z, x)
    at_first = (link.at_x, link.at_z)
    at_second = (link.at_z, link.at_x)

    def factor_at(h, t, u, core, low=0, size=None):
        rows = pl.ds(h * half + low, half if size is None else size)
        if h == 0:
            return factors.at[t, u, core, :, rows, :]
        return factors.at[u, t, core, :, rows, :]

    stage = [keep(orbitals.at[:, tile_of(q, quarter)], cells_out.at[q], sem_load.at[q]) for q in range(RING)]
    eighth = slots // RING
    stage_tiles = [
        keep(projectors.at[pl.ds(q * eighth, eighth)], tiles.at[pl.ds(q * eighth, eighth)], sem_load.at[RING + q])
        for q in range(RING)
    ]
    r1 = {}
    for o in (1, 2, 3):
        for h in range(2):
            piece = (h, first[h], c)
            r1[o, h] = push(rotation.at[piece], full.at[(b,) + piece], "r1", (o - 1, h), link.at_band(o))
    own_rows = keep(rotation, full.at[b], sem_own.at[0])
    yin, own_cells = {}, []
    for i in range(parts):
        for o in (1, 2, 3):
            src = orbitals.at[:, tile_of(ring(b, o) * parts + i, width)]
            yin[i, o] = push(src, cells_in.at[i, b], "yin", (i, o - 1), link.at_band(o))
        own_cells.append(keep(orbitals.at[:, tile_of(b * parts + i, width)], cells_in.at[i, b], sem_keep.at[i]))

    for k in range(GROUP):
        clear(pads.at[k], window)
    for q in range(RING):
        stage[q].wait()
        top, rest = split(cells_out[q])
        for m in range(quarter // LANES):
            high_cells[q * (quarter // LANES) + m] = top[:, m * LANES : (m + 1) * LANES]
            low_cells[q * (quarter // LANES) + m] = rest[:, m * LANES : (m + 1) * LANES]
    for copy in stage_tiles:
        copy.wait()

    def to_mate(step):
        group_at = pl.ds(step * GROUP, GROUP)
        return pltpu.make_async_remote_copy(
            src_ref=windows.at[group_at], dst_ref=mate.at[group_at],
            send_sem=send["s0"].at[step], recv_sem=recv["s0"].at[step],
            device_id=link.partner(), device_id_type=MESH,
        )

    def take(step, carry):
        for k in range(GROUP):
            index = step * GROUP + k
            tile, shift = table[TILE, index], table[SHIFT, index]
            o_high, o_low = [
                jnp.concatenate([ref[tile + m] for m in range(wide // LANES)], axis=1) for ref in (high_cells, low_cells)
            ]
            p_high, p_low = shifted(tiles[index], pads.at[k], shift, window, wide)
            both = dot(o_high, jnp.concatenate([p_high, p_low], axis=1))
            windows[index] = both[:, :projs] + both[:, projs:] + dot(o_low, p_high)
        to_mate(step).start()
        return carry

    one, two = {}, {}

    def assemble(h, o):
        t = ring(first[h], o)
        rows = pl.ds(h * half, half)

        def body(u, carry):
            owner = (t * RING + u if h == 0 else u * RING + t) * 2 + c
            values = [
                ref[table[WHERE + k, owner], rows, :] for k, ref in enumerate((windows, windows, mate, mate))
            ]
            for atom in range(group):
                a, d, e, f = [value * weights[k * group + atom, owner] for k, value in enumerate(values)]
                total[h, t, u, atom] = (a + d) + (e + f)
            return carry

        lax.fori_loop(0, RING, body, 0)
        return t

    low2, high2 = pl.ds(0, 2), pl.ds(2, 2)

    def send_far(h):
        t = assemble(h, 2)
        one[h, 0, 0] = push(total.at[h, t, low2], hop1.at[h, 0], "one", (h, 0, 0), at_first[h](1))
        one[h, 1, 0] = push(total.at[h, t, high2], hop1.at[h, 1], "one", (h, 1, 0), at_first[h](3))

    steps = slots // GROUP
    lax.fori_loop(0, steps // 4, take, 0)

    r2 = {}
    for o in (1, 2, 3):
        k = ring(b, RING - o)
        for h in range(2):
            r1[o, h].wait_recv()
            piece = (k, h, first[h], c)
            for p in (1, 2, 3):
                r2[o, p, h] = push(full.at[piece], full.at[piece], "r2", (o - 1, p - 1, h), at_first[h](p))

    lax.fori_loop(steps // 4, steps, take, 0)
    for step in range(steps):
        to_mate(step).wait_recv()
    for h in range(2):
        send_far(h)
    for h in range(2):
        t = assemble(h, 1)
        one[h, 0, 1] = push(total.at[h, t, high2], hop2.at[h, 0, high2], "one", (h, 0, 1), at_first[h](1))
    for h in range(2):
        t = assemble(h, 3)
        one[h, 1, 1] = push(total.at[h, t, low2], hop2.at[h, 1, low2], "one", (h, 1, 1), at_first[h](3))
    for h in range(2):
        assemble(h, 0)

    def add_rows(h, t, start, source):
        def body(u, carry):
            total[h, t, start + u] += source[h, start // 2, u]
            return carry

        lax.fori_loop(0, 2, body, 0)

    for h in range(2):
        one[h, 0, 0].wait_recv()
        t = ring(first[h], 1)
        add_rows(h, t, 0, hop1)
        one[h, 0, 2] = push(total.at[h, t, low2], hop2.at[h, 0, low2], "one", (h, 0, 2), at_first[h](1))
        one[h, 1, 0].wait_recv()
        t = ring(first[h], 3)
        add_rows(h, t, 2, hop1)
        one[h, 1, 2] = push(total.at[h, t, high2], hop2.at[h, 1, high2], "one", (h, 1, 2), at_first[h](3))

    r3 = {}
    for o in (1, 2, 3):
        k = ring(b, RING - o)
        for h in range(2):
            for p in (1, 2, 3):
                r2[o, p, h].wait_recv()
        mine = full.at[k, :, :, c]
        r3[o] = push(mine, mine, "r3", (o - 1,), link.partner())

    own_rows.wait()
    for o in (1, 2, 3):
        r3[o].wait_recv()

    def split_rows(k, carry):
        top, rest = split(full[k].reshape(bands, full.shape[-1]))
        columns = tile_of(k, full.shape[-1])
        high_rows[:, columns] = top
        low_rows[:, columns] = rest
        return carry

    lax.fori_loop(0, RING, split_rows, 0)

    yout, own_out = {}, []

    def rotate(i):
        for o in (1, 2, 3):
            yin[i, o].wait_recv()
        own_cells[i].wait()
        high, low = split(cells_in[i].reshape(RING * bands, width))
        pair = jnp.concatenate([high, low], axis=1)

        def body(k, carry):
            columns = tile_of(k, full.shape[-1])
            both = dot(high_rows[:, columns], pair)
            here = both[:, :width] + both[:, width:] + dot(low_rows[:, columns], high)
            cells_out[k, :, pl.ds(i * width, width)] = here
            return carry

        lax.fori_loop(0, RING, body, 0)
    def give(i):
        columns = tile_of(b * parts + i, width)
        for o in (1, 2, 3):
            src = cells_out.at[ring(b, o), :, pl.ds(i * width, width)]
            yout[i, o] = push(src, rotated.at[:, columns], "yout", (i, o - 1), link.at_band(o))
        own_out.append(keep(cells_out.at[b, :, pl.ds(i * width, width)], rotated.at[:, columns], sem_keep.at[parts + i]))

    for i in range(parts // 2):
        rotate(i)
    give(0)

    for h in range(2):
        t = first[h]
        one[h, 0, 1].wait_recv()
        one[h, 1, 1].wait_recv()
        one[h, 0, 2].wait_recv()
        one[h, 1, 2].wait_recv()

        def finish(u, carry, h=h, t=t):
            total[h, t, u] += hop2[h, 0, u] + hop2[h, 1, u]
            return carry

        lax.fori_loop(0, RING, finish, 0)
        lower, upper = pl.ds(0, sub), pl.ds(sub, sub)
        s = second[h]
        far, nxt, prv = ring(s, 2), ring(s, 1), ring(s, 3)
        two[h, 0, 0] = push(total.at[h, t, far, :, lower], hop3.at[h, 0], "two", (h, 0, 0), at_second[h](1))
        two[h, 1, 0] = push(total.at[h, t, far, :, upper], hop3.at[h, 1], "two", (h, 1, 0), at_second[h](3))
        two[h, 0, 1] = push(
            total.at[h, t, nxt, :, upper], hop4.at[h, 0, :, upper], "two", (h, 0, 1), at_second[h](1)
        )
        two[h, 1, 1] = push(
            total.at[h, t, prv, :, lower], hop4.at[h, 1, :, lower], "two", (h, 1, 1), at_second[h](3)
        )

    for h in range(2):
        t, s = first[h], second[h]
        nxt, prv = ring(s, 1), ring(s, 3)
        two[h, 0, 0].wait_recv()
        total[h, t, nxt, :, lower] += hop3[h, 0]
        two[h, 0, 2] = push(
            total.at[h, t, nxt, :, lower], hop4.at[h, 0, :, lower], "two", (h, 0, 2), at_second[h](1)
        )
        two[h, 1, 0].wait_recv()
        total[h, t, prv, :, upper] += hop3[h, 1]
        two[h, 1, 2] = push(
            total.at[h, t, prv, :, upper], hop4.at[h, 1, :, upper], "two", (h, 1, 2), at_second[h](3)
        )

    rotate(parts // 2)
    rotate(parts // 2 + 1)

    for h in range(2):
        t, s = first[h], second[h]
        for d in range(2):
            two[h, d, 1].wait_recv()
            two[h, d, 2].wait_recv()
        for atom in range(group):
            value = total[h, t, s, atom] + hop4[h, 0, atom] + hop4[h, 1, atom]
            turn[pl.ds(atom * projs, projs), pl.ds(h * half, half)] = value.T

    def strip_at(index):
        return pl.ds(pl.multiple_of(index * strip, 8), strip)

    swap, back = {}, {}
    for o in (1, 2, 3):
        swap[o] = push(turn.at[strip_at(ring(b, o))], turn_in.at[b], "sum", (o - 1,), link.at_band(o))
    turn_in[b] = turn[strip_at(b), :]
    give(1)

    for o in (1, 2, 3):
        swap[o].wait_recv()
    high, low = split(jnp.concatenate([turn_in[k] for k in range(RING)], axis=1))
    pair = jnp.concatenate([high, low], axis=0)

    def turn_rows(k, carry):
        columns = tile_of(k, full.shape[-1])
        both = dot_nt(pair, high_rows[:, columns])
        turn_out[k] = both[:strip] + both[strip:] + dot_nt(high, low_rows[:, columns])
        return carry

    lax.fori_loop(0, RING, turn_rows, 0)
    for o in (1, 2, 3):
        back[o] = push(turn_out.at[ring(b, o)], turned.at[strip_at(b)], "back", (o - 1,), link.at_band(o))
    turned[strip_at(b), :] = turn_out[b]

    for i in range(2, parts // 2 + 2):
        give(i)
    for i in range(parts // 2 + 2, parts):
        rotate(i)
        give(i)

    for o in (1, 2, 3):
        back[o].wait_recv()
    for atom in range(group):
        t_high, t_low = split(turned[pl.ds(atom * projs, projs), :].T)
        m_high, m_low = split(matrices[atom])
        both = dot(t_high, jnp.concatenate([m_high, m_low], axis=1))
        owned[atom] = both[:, :projs] + both[:, projs:] + dot(t_low, m_high)

    own_factor = keep(owned, factors.at[x, z, c], sem_own.at[1])
    mate_core = []

    def to_core(src, h, t, u, index):
        mate_core.append(push(src, factor_at(h, t, u, c), "core", (h, index), link.partner()))

    ag1, ag2, agf = {}, {}, {}
    for h in range(2):
        t, s = first[h], second[h]
        for d, peer, order in ((0, 1, (0, 1)), (1, 3, (1, 0))):
            for m, part in enumerate(order):
                rows = pl.ds(h * half + part * sub, sub)
                ag1[h, d, m] = push(
                    owned.at[:, rows], factor_at(h, t, s, c, part * sub, sub), "ag1", (h, d, m), at_second[h](peer)
                )
    def spread(h, r, src, u):
        t = first[h]
        for d, peer in ((0, 1), (1, 3)):
            ag2[h, d, r] = push(src, factor_at(h, t, u, c), "ag2", (h, d, r), at_first[h](peer))
        to_core(src, h, t, u, r)

    lines = (0, 3, 1, 2)
    for h in range(2):
        spread(h, 0, owned.at[:, pl.ds(h * half, half)], second[h])
    for h in range(2):
        t, s = first[h], second[h]
        for d, back, peer in ((0, 3, 1), (1, 1, 3)):
            ag1[h, d, 0].wait_recv()
            piece = factor_at(h, t, ring(s, back), c, d * sub, sub)
            ag1[h, d, 2] = push(piece, piece, "ag1", (h, d, 2), at_second[h](peer))
    for h in range(2):
        t, s = first[h], second[h]
        for d, r in ((0, 1), (1, 2)):
            ag1[h, d, 1].wait_recv()
            u = ring(s, lines[r])
            spread(h, r, factor_at(h, t, u, c), u)
    for h in range(2):
        t, s = first[h], second[h]
        ag1[h, 0, 2].wait_recv()
        ag1[h, 1, 2].wait_recv()
        u = ring(s, 2)
        spread(h, 3, factor_at(h, t, u, c), u)

    for r in range(RING):
        for h in range(2):
            u = ring(second[h], lines[r])
            for d, back, peer in ((0, 3, 1), (1, 1, 3)):
                ag2[h, d, r].wait_recv()
                t = ring(first[h], back)
                piece = factor_at(h, t, u, c)
                if (r < 2) == (d == 0):
                    agf[h, r] = push(piece, piece, "agf", (h, r), at_first[h](peer))
                to_core(piece, h, t, u, RING * (1 + d) + r)
    for r in range(RING):
        for h in range(2):
            u = ring(second[h], lines[r])
            agf[h, r].wait_recv()
            t = ring(first[h], 2)
            to_core(factor_at(h, t, u, c), h, t, u, RING * 3 + r)

    for copy in mate_core:
        copy.wait_recv()
    for copy in yout.values():
        copy.wait_recv()
    for copy in own_out:
        copy.wait()
    own_factor.wait()
    for copy in started:
        copy.wait_send()
    for step in range(slots // GROUP):
        to_mate(step).wait_send()


PARTS = 8


def exchange(table, weights, orbitals, projectors, rotation, matrices):
    bands, cells = orbitals.shape
    slots, window, projs = projectors.shape
    all_bands = rotation.shape[1]
    group = matrices.shape[0]
    atoms = 2 * RING * RING * group
    width = cells // RING // PARTS
    half = bands // 2
    sub = half // 2
    rows = bands // (4 * RING)
    strip = group * projs // RING
    f32, bf16 = jnp.float32, jnp.bfloat16
    counts = [
        (PARTS, 3), (PARTS, 3), (3, 2), (3, 3, 2), (3,), (slots // GROUP,), (2, 2, 3), (2, 2, 3), (3,), (3,),
        (2, 2, 3), (2, 2, RING), (2, RING), (2, 4 * RING),
    ]
    dma = pltpu.SemaphoreType.DMA
    in_hbm = pl.BlockSpec(memory_space=pltpu.MemorySpace.HBM)
    factors, rotated = pl.pallas_call(
        exchange_kernel,
        out_shape=(
            jax.ShapeDtypeStruct((RING, RING, 2, group, bands, projs), f32),
            jax.ShapeDtypeStruct((bands, cells), f32),
        ),
        in_specs=[pl.BlockSpec(memory_space=pltpu.SMEM)] * 2
        + [in_hbm] * 3
        + [pl.BlockSpec(memory_space=pltpu.VMEM)],
        out_specs=[in_hbm] * 2,
        scratch_shapes=[
            pltpu.VMEM((PARTS, RING, bands, width), f32),
            pltpu.VMEM((RING, bands, cells // RING), f32),
            pltpu.VMEM((RING, 2, RING, 2, rows, all_bands), f32),
            pltpu.VMEM((bands, RING * all_bands), bf16),
            pltpu.VMEM((bands, RING * all_bands), bf16),
            pltpu.VMEM((cells // LANES, bands, LANES), bf16),
            pltpu.VMEM((cells // LANES, bands, LANES), bf16),
            pltpu.VMEM((slots, window, projs), f32),
            pltpu.VMEM((slots, bands, projs), f32),
            pltpu.VMEM((slots, bands, projs), f32),
            pltpu.VMEM((2, RING, RING, group, half, projs), f32),
            pltpu.VMEM((2, 2, 2, group, half, projs), f32),
            pltpu.VMEM((2, 2, RING, group, half, projs), f32),
            pltpu.VMEM((2, 2, group, sub, projs), f32),
            pltpu.VMEM((2, 2, group, half, projs), f32),
            pltpu.VMEM((group * projs, bands), f32),
            pltpu.VMEM((RING, strip, bands), f32),
            pltpu.VMEM((RING, strip, bands), f32),
            pltpu.VMEM((group * projs, bands), f32),
            pltpu.VMEM((group, bands, projs), f32),
            pltpu.VMEM((GROUP, window + 2 * LANES, projs), f32),
            dma((2 * RING,)),
            dma((2 * PARTS,)),
            dma((2,)),
        ]
        + [dma(shape) for shape in counts for _ in range(2)],
        compiler_params=pltpu.CompilerParams(
            collective_id=0, has_side_effects=True, vmem_limit_bytes=60 << 20
        ),
        name="exchange",
    )(
        table, weights, orbitals, projectors, rotation.reshape(2, RING, 2, rows, all_bands), matrices
    )
    return factors.reshape(atoms, bands, projs), rotated


def per_device(orbitals, projectors, window_start, slot_atom, atom_home, atom_matrices, rotation):
    dom = lax.axis_index("dom").astype(jnp.int32).reshape(1)
    window = projectors.shape[1]
    table, weights = list_slots(
        dom, window_start, slot_atom, atom_home, atom_matrices.shape[0], orbitals.shape[1], window + LANES
    )
    factors, rotated = exchange(table, weights, orbitals, projectors, rotation, atom_matrices)
    return update(table, factors, projectors, rotated)


def solution(mesh):
    in_specs = (
        P("band", "dom"),
        P("dom", None, None),
        P("dom"),
        P(),
        P(),
        P("dom", None, None),
        P("band", None),
    )
    out_specs = P("band", "dom")
    return jax.shard_map(
        per_device, mesh=mesh, in_specs=in_specs, out_specs=out_specs, check_vma=False
    )
```

```python
import functools

import jax
import jax.numpy as jnp
from jax import lax
from jax.experimental import pallas as pl
from jax.experimental.pallas import tpu as pltpu
from jax.sharding import PartitionSpec as P

LANES = 128
GROUP = 4
UPDATE_GROUP = 8


def split(value):
    high = value.astype(jnp.bfloat16)
    low = (value - high.astype(jnp.float32)).astype(jnp.bfloat16)
    return high, low


def dot(a, b):
    return jnp.dot(a, b, preferred_element_type=jnp.float32)


def dot_nt(a, b):
    return lax.dot_general(a, b, (((1,), (1,)), ((), ())), preferred_element_type=jnp.float32)


def shifted(projector, pad, shift, window, wide):
    pad[pl.ds(LANES, window), :] = projector
    return split(pad[pl.ds(LANES - shift, wide), :])


def clear(pad, window):
    edge = jnp.zeros((LANES, pad.shape[1]), jnp.float32)
    pad[pl.ds(0, LANES), :] = edge
    pad[pl.ds(LANES + window, LANES), :] = edge


TILE, SHIFT, ROW, WHERE = 0, 1, 2, 3
TABLE_ROWS = 16


def list_kernel(dom, start, slot_atom, home, table, weights, *, group, cells, wide):
    lane = lax.broadcasted_iota(jnp.int32, (1, LANES), 1)
    blank = jnp.zeros((1, LANES), jnp.int32)
    none = jnp.full((1, LANES), -1, jnp.int32)
    core = lax.rem(dom[0], 2)

    def enter(domain):
        def body(slot, carry):
            row_of, where0, local0, where1, local1 = carry
            row = home[slot_atom[domain, slot]]
            owner = row // group
            local = row - owner * group
            here = lane == owner
            taken = here & (local0 >= 0)
            fresh = here & (local0 < 0)
            where1 = jnp.where(taken, slot, where1)
            local1 = jnp.where(taken, local, local1)
            where0 = jnp.where(fresh, slot, where0)
            local0 = jnp.where(fresh, local, local0)
            return jnp.where(lane == slot, row, row_of), where0, local0, where1, local1

        return lax.fori_loop(0, start.shape[0], body, (blank, blank, none, blank, none), unroll=8)

    def locate(slot, carry):
        tile = jnp.minimum(start[slot] // LANES, (cells - wide) // LANES)
        cell_of, shift_of = carry
        cell_of = jnp.where(lane == slot, tile, cell_of)
        return cell_of, jnp.where(lane == slot, start[slot] - tile * LANES, shift_of)

    cell_of, shift_of = lax.fori_loop(0, start.shape[0], locate, (blank, blank), unroll=8)
    row_of, own0, own_local0, own1, own_local1 = enter(dom[0])
    _, mate0, mate_local0, mate1, mate_local1 = enter(dom[0] + 1 - 2 * core)
    rows = [cell_of, shift_of, row_of, own0, own1, mate0, mate1]
    for index, row in enumerate(rows):
        table[index : index + 1, :] = row
    for index, local in enumerate([own_local0, own_local1, mate_local0, mate_local1]):
        for atom in range(group):
            at = index * group + atom
            weights[at : at + 1, :] = (local == atom).astype(jnp.float32)


def list_slots(dom, start, slot_atom, home, group, cells, wide):
    return pl.pallas_call(
        functools.partial(list_kernel, group=group, cells=cells, wide=wide),
        out_shape=[jax.ShapeDtypeStruct((TABLE_ROWS, LANES), kind) for kind in (jnp.int32, jnp.float32)],
        in_specs=[pl.BlockSpec(memory_space=pltpu.SMEM)] * 4,
        out_specs=[pl.BlockSpec(memory_space=pltpu.VMEM)] * 2,
        compiler_params=pltpu.CompilerParams(vmem_limit_bytes=60 << 20),
        name="list_slots",
    )(dom, start, slot_atom, home)


def update_kernel(table, *refs):
    group = UPDATE_GROUP
    factors = refs[:group]
    projectors, rotated, out = refs[group : group + 3]
    pads, base = refs[group + 3 : -2], refs[-2]
    step = pl.program_id(0)
    fetch = pltpu.make_async_copy(rotated, base, refs[-1])
    _, window, _ = projectors.shape
    cells = out.shape[1]
    wide = window + LANES

    @pl.when(step == 0)
    def _():
        fetch.start()
        for pad in pads:
            clear(pad, window)
        out[...] = jnp.zeros_like(out)

    for k in range(group):
        slot = step * group + k
        cell, shift = pl.multiple_of(table[TILE, slot] * LANES, LANES), table[SHIFT, slot]
        p_high, p_low = shifted(projectors[k], pads[k], shift, window, wide)
        f_high, f_low = split(factors[k][0])
        update = dot_nt(
            jnp.concatenate([f_high, f_low, f_high], axis=1),
            jnp.concatenate([p_high, p_high, p_low], axis=1),
        )
        out[:, pl.ds(cell, wide)] += update

    @pl.when(step == pl.num_programs(0) - 1)
    def _():
        fetch.wait()
        out[...] += base[...]


def update(table, factors, projectors, rotated):
    slots, window, projs = projectors.shape
    bands, cells = rotated.shape

    def factor_spec(k):
        return pl.BlockSpec(
            (1, bands, projs),
            lambda i, table: (table[ROW, i * UPDATE_GROUP + k], 0, 0),
        )

    return pl.pallas_call(
        update_kernel,
        out_shape=jax.ShapeDtypeStruct((bands, cells), jnp.float32),
        grid_spec=pltpu.PrefetchScalarGridSpec(
            num_scalar_prefetch=1,
            grid=(slots // UPDATE_GROUP,),
            in_specs=[factor_spec(k) for k in range(UPDATE_GROUP)]
            + [
                pl.BlockSpec((UPDATE_GROUP, window, projs), lambda i, *_: (i, 0, 0)),
                pl.BlockSpec(memory_space=pltpu.MemorySpace.HBM),
            ],
            out_specs=pl.BlockSpec(
                (bands, cells), lambda i, *_: (0, 0), pipeline_mode=pl.Buffered(1)
            ),
            scratch_shapes=[pltpu.VMEM((window + 2 * LANES, projs), jnp.float32)] * UPDATE_GROUP
            + [pltpu.VMEM((bands, cells), jnp.float32), pltpu.SemaphoreType.DMA],
        ),
        cost_estimate=pl.CostEstimate(
            flops=6 * slots * window * bands * projs, bytes_accessed=20 << 20, transcendentals=0
        ),
        compiler_params=pltpu.CompilerParams(vmem_limit_bytes=60 << 20),
        name="update",
    )(table, *([factors] * UPDATE_GROUP), projectors, rotated)


MESH = pl.DeviceIdType.MESH
RING = 4
ORDER = (2, 1, 3, 0)


def ring(position, offset):
    return lax.rem(position + offset, RING)


def tile_of(index, size):
    return pl.ds(pl.multiple_of(index * size, size), size)


class Links:
    def __init__(self):
        self.band = lax.axis_index("band")
        dom = lax.axis_index("dom")
        self.core = lax.rem(dom, 2)
        self.z = lax.rem(dom // 2, RING)
        self.x = dom // (2 * RING)

    def place(self, band, x, z, core):
        return (band, (x * RING + z) * 2 + core)

    def at_band(self, offset):
        return self.place(ring(self.band, offset), self.x, self.z, self.core)

    def at_x(self, offset):
        return self.place(self.band, ring(self.x, offset), self.z, self.core)

    def at_z(self, offset):
        return self.place(self.band, self.x, ring(self.z, offset), self.core)

    def partner(self):
        return self.place(self.band, self.x, self.z, 1 - self.core)


def exchange_kernel(
    table, weights, orbitals, projectors, rotation, matrices, factors, rotated,
    cells_in, cells_out, full, high_rows, low_rows, high_cells, low_cells, tiles, windows, mate, total, hop1, hop2, hop3, hop4,
    turn, turn_in, turn_out, turned, owned, pads,
    sem_load, sem_keep, sem_own, *sems
):
    link = Links()
    b, x, z, c = link.band, link.x, link.z, link.core
    names = ("yin", "yout", "r1", "r2", "r3", "r4", "s0", "one", "two", "sum", "back", "ag1", "ag2", "agf", "core")
    send = dict(zip(names, sems[0::2]))
    recv = dict(zip(names, sems[1::2]))
    bands, cells = orbitals.shape
    slots, window, projs = projectors.shape
    wide = window + LANES
    group = matrices.shape[0]
    quarter = cells // RING
    parts = cells_in.shape[0]
    width = quarter // parts
    half = bands // 2
    sub = half // 2
    strip = turn.shape[0] // RING
    started = []

    def push(src, dst, kind, index, device):
        copy = pltpu.make_async_remote_copy(
            src_ref=src, dst_ref=dst, send_sem=send[kind].at[index], recv_sem=recv[kind].at[index],
            device_id=device, device_id_type=MESH,
        )
        copy.start()
        started.append(copy)
        return copy

    def keep(src, dst, sem):
        copy = pltpu.make_async_copy(src, dst, sem)
        copy.start()
        return copy

    barrier = pltpu.get_barrier_semaphore()
    peers = [f(o) for f in (link.at_band, link.at_x, link.at_z) for o in (1, 2, 3)] + [link.partner()]
    for peer in peers:
        pl.semaphore_signal(barrier, inc=1, device_id=peer, device_id_type=MESH)
    pl.semaphore_wait(barrier, len(peers))

    first = (x, z)
    second = (z, x)
    at_first = (link.at_x, link.at_z)
    at_second = (link.at_z, link.at_x)

    def factor_at(h, t, u, core, low=0, size=None):
        rows = pl.ds(h * half + low, half if size is None else size)
        if h == 0:
            return factors.at[t, u, core, :, rows, :]
        return factors.at[u, t, core, :, rows, :]

    stage = [keep(orbitals.at[:, tile_of(q, quarter)], cells_out.at[q], sem_load.at[q]) for q in range(RING)]
    eighth = slots // RING
    stage_tiles = [
        keep(projectors.at[pl.ds(q * eighth, eighth)], tiles.at[pl.ds(q * eighth, eighth)], sem_load.at[RING + q])
        for q in range(RING)
    ]
    r1 = {}
    for o in (1, 2, 3):
        r1[o] = push(rotation.at[x, z, c], full.at[b, x, z, c], "r1", (o - 1,), link.at_band(o))
    own_rows = keep(rotation, full.at[b], sem_own.at[0])
    yin, own_cells = {}, []
    for i in range(parts):
        for o in (1, 2, 3):
            src = orbitals.at[:, tile_of(ring(b, o) * parts + i, width)]
            yin[i, o] = push(src, cells_in.at[i, b], "yin", (i, o - 1), link.at_band(o))
        own_cells.append(keep(orbitals.at[:, tile_of(b * parts + i, width)], cells_in.at[i, b], sem_keep.at[i]))

    for k in range(GROUP):
        clear(pads.at[k], window)
    r2, r3, r4 = {}, {}, {}
    columns_of = [pl.ds(h * (full.shape[-1] // 2), full.shape[-1] // 2) for h in range(2)]
    for o in (1, 2, 3):
        r1[o].wait_recv()
        for h in range(2):
            piece = full.at[ring(b, RING - o), x, z, c, :, columns_of[h]]
            for p in (1, 2, 3):
                r2[o, p, h] = push(piece, piece, "r2", (o - 1, p - 1, h), at_first[h](p))
    for q in range(RING):
        stage[q].wait()
        top, rest = split(cells_out[q])
        for m in range(quarter // LANES):
            high_cells[q * (quarter // LANES) + m] = top[:, m * LANES : (m + 1) * LANES]
            low_cells[q * (quarter // LANES) + m] = rest[:, m * LANES : (m + 1) * LANES]
    for o in (1, 2, 3):
        k = ring(b, RING - o)
        for h in range(2):
            for p in (1, 2, 3):
                r2[o, p, h].wait_recv()
            if h == 0:
                piece = full.at[k, :, z, c, :, columns_of[h]]
            else:
                piece = full.at[k, x, :, c, :, columns_of[h]]
            for p in (1, 2, 3):
                r3[o, p, h] = push(piece, piece, "r3", (o - 1, p - 1, h), at_second[h](p))

    def to_mate(step):
        group_at = pl.ds(step * GROUP, GROUP)
        return pltpu.make_async_remote_copy(
            src_ref=windows.at[group_at], dst_ref=mate.at[group_at],
            send_sem=send["s0"].at[step], recv_sem=recv["s0"].at[step],
            device_id=link.partner(), device_id_type=MESH,
        )

    def take(step, carry):
        for k in range(GROUP):
            index = step * GROUP + k
            tile, shift = table[TILE, index], table[SHIFT, index]
            o_high, o_low = [
                jnp.concatenate([ref[tile + m] for m in range(wide // LANES)], axis=1) for ref in (high_cells, low_cells)
            ]
            p_high, p_low = shifted(tiles[index], pads.at[k], shift, window, wide)
            both = dot(o_high, jnp.concatenate([p_high, p_low], axis=1))
            windows[index] = both[:, :projs] + both[:, projs:] + dot(o_low, p_high)
        to_mate(step).start()
        return carry

    one, two = {}, {}

    def assemble(h, o):
        t = ring(first[h], o)
        rows = pl.ds(h * half, half)

        def body(u, carry):
            owner = (t * RING + u if h == 0 else u * RING + t) * 2 + c
            values = [
                ref[table[WHERE + k, owner], rows, :] for k, ref in enumerate((windows, windows, mate, mate))
            ]
            for atom in range(group):
                a, d, e, f = [value * weights[k * group + atom, owner] for k, value in enumerate(values)]
                total[h, t, u, atom] = (a + d) + (e + f)
            return carry

        lax.fori_loop(0, RING, body, 0)
        return t

    low2, high2 = pl.ds(0, 2), pl.ds(2, 2)

    def send_far(h):
        t = assemble(h, 2)
        one[h, 0, 0] = push(total.at[h, t, low2], hop1.at[h, 0], "one", (h, 0, 0), at_first[h](1))
        one[h, 1, 0] = push(total.at[h, t, high2], hop1.at[h, 1], "one", (h, 1, 0), at_first[h](3))

    steps = slots // GROUP
    for q in range(RING):
        stage_tiles[q].wait()
        lax.fori_loop(q * steps // RING, (q + 1) * steps // RING, take, 0)
    for step in range(steps):
        to_mate(step).wait_recv()
    for h in range(2):
        send_far(h)
    for h in range(2):
        t = assemble(h, 1)
        one[h, 0, 1] = push(total.at[h, t, high2], hop2.at[h, 0, high2], "one", (h, 0, 1), at_first[h](1))
    for h in range(2):
        t = assemble(h, 3)
        one[h, 1, 1] = push(total.at[h, t, low2], hop2.at[h, 1, low2], "one", (h, 1, 1), at_first[h](3))
    for h in range(2):
        assemble(h, 0)

    def add_rows(h, t, start, source):
        def body(u, carry):
            total[h, t, start + u] += source[h, start // 2, u]
            return carry

        lax.fori_loop(0, 2, body, 0)

    for h in range(2):
        one[h, 0, 0].wait_recv()
        t = ring(first[h], 1)
        add_rows(h, t, 0, hop1)
        one[h, 0, 2] = push(total.at[h, t, low2], hop2.at[h, 0, low2], "one", (h, 0, 2), at_first[h](1))
        one[h, 1, 0].wait_recv()
        t = ring(first[h], 3)
        add_rows(h, t, 2, hop1)
        one[h, 1, 2] = push(total.at[h, t, high2], hop2.at[h, 1, high2], "one", (h, 1, 2), at_first[h](3))

    for o in (1, 2, 3):
        for h in range(2):
            for p in (1, 2, 3):
                r3[o, p, h].wait_recv()
        mine = full.at[ring(b, RING - o), :, :, c]
        r4[o] = push(mine, mine, "r4", (o - 1,), link.partner())

    own_rows.wait()
    for o in (1, 2, 3):
        r4[o].wait_recv()

    def split_rows(k, carry):
        top, rest = split(full[k].reshape(bands, full.shape[-1]))
        columns = tile_of(k, full.shape[-1])
        high_rows[:, columns] = top
        low_rows[:, columns] = rest
        return carry

    lax.fori_loop(0, RING, split_rows, 0)

    yout, own_out = {}, []

    def rotate(i):
        for o in (1, 2, 3):
            yin[i, o].wait_recv()
        own_cells[i].wait()
        high, low = split(cells_in[i].reshape(RING * bands, width))
        pair = jnp.concatenate([high, low], axis=1)

        def body(k, carry):
            columns = tile_of(k, full.shape[-1])
            both = dot(high_rows[:, columns], pair)
            here = both[:, :width] + both[:, width:] + dot(low_rows[:, columns], high)
            cells_out[k, :, pl.ds(i * width, width)] = here
            return carry

        lax.fori_loop(0, RING, body, 0)
    def give(i):
        columns = tile_of(b * parts + i, width)
        for o in (1, 2, 3):
            src = cells_out.at[ring(b, o), :, pl.ds(i * width, width)]
            yout[i, o] = push(src, rotated.at[:, columns], "yout", (i, o - 1), link.at_band(o))
        own_out.append(keep(cells_out.at[b, :, pl.ds(i * width, width)], rotated.at[:, columns], sem_keep.at[parts + i]))

    for i in range(parts // 2):
        rotate(i)
    give(0)

    for h in range(2):
        t = first[h]
        one[h, 0, 1].wait_recv()
        one[h, 1, 1].wait_recv()
        one[h, 0, 2].wait_recv()
        one[h, 1, 2].wait_recv()

        def finish(u, carry, h=h, t=t):
            total[h, t, u] += hop2[h, 0, u] + hop2[h, 1, u]
            return carry

        lax.fori_loop(0, RING, finish, 0)
        lower, upper = pl.ds(0, sub), pl.ds(sub, sub)
        s = second[h]
        far, nxt, prv = ring(s, 2), ring(s, 1), ring(s, 3)
        two[h, 0, 0] = push(total.at[h, t, far, :, lower], hop3.at[h, 0], "two", (h, 0, 0), at_second[h](1))
        two[h, 1, 0] = push(total.at[h, t, far, :, upper], hop3.at[h, 1], "two", (h, 1, 0), at_second[h](3))
        two[h, 0, 1] = push(
            total.at[h, t, nxt, :, upper], hop4.at[h, 0, :, upper], "two", (h, 0, 1), at_second[h](1)
        )
        two[h, 1, 1] = push(
            total.at[h, t, prv, :, lower], hop4.at[h, 1, :, lower], "two", (h, 1, 1), at_second[h](3)
        )

    for h in range(2):
        t, s = first[h], second[h]
        nxt, prv = ring(s, 1), ring(s, 3)
        two[h, 0, 0].wait_recv()
        total[h, t, nxt, :, lower] += hop3[h, 0]
        two[h, 0, 2] = push(
            total.at[h, t, nxt, :, lower], hop4.at[h, 0, :, lower], "two", (h, 0, 2), at_second[h](1)
        )
        two[h, 1, 0].wait_recv()
        total[h, t, prv, :, upper] += hop3[h, 1]
        two[h, 1, 2] = push(
            total.at[h, t, prv, :, upper], hop4.at[h, 1, :, upper], "two", (h, 1, 2), at_second[h](3)
        )

    rotate(parts // 2)
    rotate(parts // 2 + 1)

    for h in range(2):
        t, s = first[h], second[h]
        for d in range(2):
            two[h, d, 1].wait_recv()
            two[h, d, 2].wait_recv()
        for atom in range(group):
            value = total[h, t, s, atom] + hop4[h, 0, atom] + hop4[h, 1, atom]
            turn[pl.ds(atom * projs, projs), pl.ds(h * half, half)] = value.T

    def strip_at(index):
        return pl.ds(pl.multiple_of(index * strip, 8), strip)

    swap, back = {}, {}
    for o in (1, 2, 3):
        swap[o] = push(turn.at[strip_at(ring(b, o))], turn_in.at[b], "sum", (o - 1,), link.at_band(o))
    turn_in[b] = turn[strip_at(b), :]
    give(1)

    for o in (1, 2, 3):
        swap[o].wait_recv()
    high, low = split(jnp.concatenate([turn_in[k] for k in range(RING)], axis=1))
    pair = jnp.concatenate([high, low], axis=0)

    def turn_rows(k, carry):
        columns = tile_of(k, full.shape[-1])
        both = dot_nt(pair, high_rows[:, columns])
        turn_out[k] = both[:strip] + both[strip:] + dot_nt(high, low_rows[:, columns])
        return carry

    lax.fori_loop(0, RING, turn_rows, 0)
    for o in (1, 2, 3):
        back[o] = push(turn_out.at[ring(b, o)], turned.at[strip_at(b)], "back", (o - 1,), link.at_band(o))
    turned[strip_at(b), :] = turn_out[b]

    for i in range(2, parts // 2 + 2):
        give(i)
    for i in range(parts // 2 + 2, parts):
        rotate(i)
        give(i)

    for o in (1, 2, 3):
        back[o].wait_recv()
    for atom in range(group):
        t_high, t_low = split(turned[pl.ds(atom * projs, projs), :].T)
        m_high, m_low = split(matrices[atom])
        both = dot(t_high, jnp.concatenate([m_high, m_low], axis=1))
        owned[atom] = both[:, :projs] + both[:, projs:] + dot(t_low, m_high)

    own_factor = keep(owned, factors.at[x, z, c], sem_own.at[1])
    mate_core = []

    def to_core(src, h, t, u, index):
        mate_core.append(push(src, factor_at(h, t, u, c), "core", (h, index), link.partner()))

    ag1, ag2, agf = {}, {}, {}
    for h in range(2):
        t, s = first[h], second[h]
        for d, peer, order in ((0, 1, (0, 1)), (1, 3, (1, 0))):
            for m, part in enumerate(order):
                rows = pl.ds(h * half + part * sub, sub)
                ag1[h, d, m] = push(
                    owned.at[:, rows], factor_at(h, t, s, c, part * sub, sub), "ag1", (h, d, m), at_second[h](peer)
                )
    def spread(h, r, src, u):
        t = first[h]
        for d, peer in ((0, 1), (1, 3)):
            ag2[h, d, r] = push(src, factor_at(h, t, u, c), "ag2", (h, d, r), at_first[h](peer))
        to_core(src, h, t, u, r)

    lines = (0, 3, 1, 2)
    for h in range(2):
        spread(h, 0, owned.at[:, pl.ds(h * half, half)], second[h])
    for h in range(2):
        t, s = first[h], second[h]
        for d, back, peer in ((0, 3, 1), (1, 1, 3)):
            ag1[h, d, 0].wait_recv()
            piece = factor_at(h, t, ring(s, back), c, d * sub, sub)
            ag1[h, d, 2] = push(piece, piece, "ag1", (h, d, 2), at_second[h](peer))
    for h in range(2):
        t, s = first[h], second[h]
        for d, r in ((0, 1), (1, 2)):
            ag1[h, d, 1].wait_recv()
            u = ring(s, lines[r])
            spread(h, r, factor_at(h, t, u, c), u)
    for h in range(2):
        t, s = first[h], second[h]
        ag1[h, 0, 2].wait_recv()
        ag1[h, 1, 2].wait_recv()
        u = ring(s, 2)
        spread(h, 3, factor_at(h, t, u, c), u)

    for r in range(RING):
        for h in range(2):
            u = ring(second[h], lines[r])
            for d, back, peer in ((0, 3, 1), (1, 1, 3)):
                ag2[h, d, r].wait_recv()
                t = ring(first[h], back)
                piece = factor_at(h, t, u, c)
                if (r < 2) == (d == 0):
                    agf[h, r] = push(piece, piece, "agf", (h, r), at_first[h](peer))
                to_core(piece, h, t, u, RING * (1 + d) + r)
    for r in range(RING):
        for h in range(2):
            u = ring(second[h], lines[r])
            agf[h, r].wait_recv()
            t = ring(first[h], 2)
            to_core(factor_at(h, t, u, c), h, t, u, RING * 3 + r)

    for copy in mate_core:
        copy.wait_recv()
    for copy in yout.values():
        copy.wait_recv()
    for copy in own_out:
        copy.wait()
    own_factor.wait()
    for copy in started:
        copy.wait_send()
    for step in range(slots // GROUP):
        to_mate(step).wait_send()


PARTS = 8


def exchange(table, weights, orbitals, projectors, rotation, matrices):
    bands, cells = orbitals.shape
    slots, window, projs = projectors.shape
    all_bands = rotation.shape[1]
    group = matrices.shape[0]
    atoms = 2 * RING * RING * group
    width = cells // RING // PARTS
    half = bands // 2
    sub = half // 2
    rows = bands // (2 * RING * RING)
    strip = group * projs // RING
    f32, bf16 = jnp.float32, jnp.bfloat16
    counts = [
        (PARTS, 3), (PARTS, 3), (3,), (3, 3, 2), (3, 3, 2), (3,), (slots // GROUP,), (2, 2, 3), (2, 2, 3), (3,), (3,),
        (2, 2, 3), (2, 2, RING), (2, RING), (2, 4 * RING),
    ]
    dma = pltpu.SemaphoreType.DMA
    in_hbm = pl.BlockSpec(memory_space=pltpu.MemorySpace.HBM)
    factors, rotated = pl.pallas_call(
        exchange_kernel,
        out_shape=(
            jax.ShapeDtypeStruct((RING, RING, 2, group, bands, projs), f32),
            jax.ShapeDtypeStruct((bands, cells), f32),
        ),
        in_specs=[pl.BlockSpec(memory_space=pltpu.SMEM)] * 2
        + [in_hbm] * 3
        + [pl.BlockSpec(memory_space=pltpu.VMEM)],
        out_specs=[in_hbm] * 2,
        scratch_shapes=[
            pltpu.VMEM((PARTS, RING, bands, width), f32),
            pltpu.VMEM((RING, bands, cells // RING), f32),
            pltpu.VMEM((RING, RING, RING, 2, rows, all_bands), f32),
            pltpu.VMEM((bands, RING * all_bands), bf16),
            pltpu.VMEM((bands, RING * all_bands), bf16),
            pltpu.VMEM((cells // LANES, bands, LANES), bf16),
            pltpu.VMEM((cells // LANES, bands, LANES), bf16),
            pltpu.VMEM((slots, window, projs), f32),
            pltpu.VMEM((slots, bands, projs), f32),
            pltpu.VMEM((slots, bands, projs), f32),
            pltpu.VMEM((2, RING, RING, group, half, projs), f32),
            pltpu.VMEM((2, 2, 2, group, half, projs), f32),
            pltpu.VMEM((2, 2, RING, group, half, projs), f32),
            pltpu.VMEM((2, 2, group, sub, projs), f32),
            pltpu.VMEM((2, 2, group, half, projs), f32),
            pltpu.VMEM((group * projs, bands), f32),
            pltpu.VMEM((RING, strip, bands), f32),
            pltpu.VMEM((RING, strip, bands), f32),
            pltpu.VMEM((group * projs, bands), f32),
            pltpu.VMEM((group, bands, projs), f32),
            pltpu.VMEM((GROUP, window + 2 * LANES, projs), f32),
            dma((2 * RING,)),
            dma((2 * PARTS,)),
            dma((2,)),
        ]
        + [dma(shape) for shape in counts for _ in range(2)],
        compiler_params=pltpu.CompilerParams(
            collective_id=0, has_side_effects=True, vmem_limit_bytes=60 << 20
        ),
        name="exchange",
    )(
        table, weights, orbitals, projectors, rotation.reshape(RING, RING, 2, rows, all_bands), matrices
    )
    return factors.reshape(atoms, bands, projs), rotated


def per_device(orbitals, projectors, window_start, slot_atom, atom_home, atom_matrices, rotation):
    dom = lax.axis_index("dom").astype(jnp.int32).reshape(1)
    window = projectors.shape[1]
    table, weights = list_slots(
        dom, window_start, slot_atom, atom_home, atom_matrices.shape[0], orbitals.shape[1], window + LANES
    )
    factors, rotated = exchange(table, weights, orbitals, projectors, rotation, atom_matrices)
    return update(table, factors, projectors, rotated)


def solution(mesh):
    in_specs = (
        P("band", "dom"),
        P("dom", None, None),
        P("dom"),
        P(),
        P(),
        P("dom", None, None),
        P("band", None),
    )
    out_specs = P("band", "dom")
    return jax.shard_map(
        per_device, mesh=mesh, in_specs=in_specs, out_specs=out_specs, check_vma=False
    )
```

```python
import functools

import jax
import jax.numpy as jnp
from jax import lax
from jax.experimental import pallas as pl
from jax.experimental.pallas import tpu as pltpu
from jax.sharding import PartitionSpec as P

LANES = 128
GROUP = 4
UPDATE_GROUP = 8


def split(value):
    high = value.astype(jnp.bfloat16)
    low = (value - high.astype(jnp.float32)).astype(jnp.bfloat16)
    return high, low


def dot(a, b):
    return jnp.dot(a, b, preferred_element_type=jnp.float32)


def dot_nt(a, b):
    return lax.dot_general(a, b, (((1,), (1,)), ((), ())), preferred_element_type=jnp.float32)


def shifted(projector, pad, shift, window, wide):
    pad[pl.ds(LANES, window), :] = projector
    return split(pad[pl.ds(LANES - shift, wide), :])


def clear(pad, window):
    edge = jnp.zeros((LANES, pad.shape[1]), jnp.float32)
    pad[pl.ds(0, LANES), :] = edge
    pad[pl.ds(LANES + window, LANES), :] = edge


TILE, SHIFT, ROW, WHERE = 0, 1, 2, 3
TABLE_ROWS = 16


def list_kernel(dom, start, slot_atom, home, table, weights, *, group, cells, wide):
    lane = lax.broadcasted_iota(jnp.int32, (1, LANES), 1)
    blank = jnp.zeros((1, LANES), jnp.int32)
    none = jnp.full((1, LANES), -1, jnp.int32)
    core = lax.rem(dom[0], 2)

    def enter(domain):
        def body(slot, carry):
            row_of, where0, local0, where1, local1 = carry
            row = home[slot_atom[domain, slot]]
            owner = row // group
            local = row - owner * group
            here = lane == owner
            taken = here & (local0 >= 0)
            fresh = here & (local0 < 0)
            where1 = jnp.where(taken, slot, where1)
            local1 = jnp.where(taken, local, local1)
            where0 = jnp.where(fresh, slot, where0)
            local0 = jnp.where(fresh, local, local0)
            return jnp.where(lane == slot, row, row_of), where0, local0, where1, local1

        return lax.fori_loop(0, start.shape[0], body, (blank, blank, none, blank, none), unroll=8)

    def locate(slot, carry):
        tile = jnp.minimum(start[slot] // LANES, (cells - wide) // LANES)
        cell_of, shift_of = carry
        cell_of = jnp.where(lane == slot, tile, cell_of)
        return cell_of, jnp.where(lane == slot, start[slot] - tile * LANES, shift_of)

    cell_of, shift_of = lax.fori_loop(0, start.shape[0], locate, (blank, blank), unroll=8)
    row_of, own0, own_local0, own1, own_local1 = enter(dom[0])
    _, mate0, mate_local0, mate1, mate_local1 = enter(dom[0] + 1 - 2 * core)
    rows = [cell_of, shift_of, row_of, own0, own1, mate0, mate1]
    for index, row in enumerate(rows):
        table[index : index + 1, :] = row
    for index, local in enumerate([own_local0, own_local1, mate_local0, mate_local1]):
        for atom in range(group):
            at = index * group + atom
            weights[at : at + 1, :] = (local == atom).astype(jnp.float32)


def list_slots(dom, start, slot_atom, home, group, cells, wide):
    return pl.pallas_call(
        functools.partial(list_kernel, group=group, cells=cells, wide=wide),
        out_shape=[jax.ShapeDtypeStruct((TABLE_ROWS, LANES), kind) for kind in (jnp.int32, jnp.float32)],
        in_specs=[pl.BlockSpec(memory_space=pltpu.SMEM)] * 4,
        out_specs=[pl.BlockSpec(memory_space=pltpu.VMEM)] * 2,
        compiler_params=pltpu.CompilerParams(vmem_limit_bytes=60 << 20),
        name="list_slots",
    )(dom, start, slot_atom, home)


def update_kernel(table, *refs):
    group = UPDATE_GROUP
    factors = refs[:group]
    columns, rotated, out, base, sem = refs[group:]
    step = pl.program_id(0)
    _, both, wide = columns.shape
    projs = both // 2
    fetch = pltpu.make_async_copy(rotated, base, sem)

    @pl.when(step == 0)
    def _():
        fetch.start()
        out[...] = jnp.zeros_like(out)

    for k in range(group):
        slot = step * group + k
        cell = pl.multiple_of(table[TILE, slot] * LANES, LANES)
        f_high, f_low = split(factors[k][0])
        p_high, p_low = columns[k, :projs, :], columns[k, projs:, :]
        out[:, pl.ds(cell, wide)] += dot(
            jnp.concatenate([f_high, f_low, f_high], axis=1),
            jnp.concatenate([p_high, p_high, p_low], axis=0),
        )

    @pl.when(step == pl.num_programs(0) - 1)
    def _():
        fetch.wait()
        out[...] += base[...]


def update(table, factors, columns, rotated):
    slots, both, wide = columns.shape
    bands, cells = rotated.shape
    projs = both // 2

    def factor_spec(k):
        return pl.BlockSpec(
            (1, bands, projs),
            lambda i, table: (table[ROW, i * UPDATE_GROUP + k], 0, 0),
        )

    return pl.pallas_call(
        update_kernel,
        out_shape=jax.ShapeDtypeStruct((bands, cells), jnp.float32),
        grid_spec=pltpu.PrefetchScalarGridSpec(
            num_scalar_prefetch=1,
            grid=(slots // UPDATE_GROUP,),
            in_specs=[factor_spec(k) for k in range(UPDATE_GROUP)]
            + [
                pl.BlockSpec((UPDATE_GROUP, both, wide), lambda i, *_: (i, 0, 0)),
                pl.BlockSpec(memory_space=pltpu.MemorySpace.HBM),
            ],
            out_specs=pl.BlockSpec(
                (bands, cells), lambda i, *_: (0, 0), pipeline_mode=pl.Buffered(1)
            ),
            scratch_shapes=[pltpu.VMEM((bands, cells), jnp.float32), pltpu.SemaphoreType.DMA],
        ),
        cost_estimate=pl.CostEstimate(
            flops=6 * slots * wide * bands * projs, bytes_accessed=22 << 20, transcendentals=0
        ),
        compiler_params=pltpu.CompilerParams(vmem_limit_bytes=60 << 20),
        name="update",
    )(table, *([factors] * UPDATE_GROUP), columns, rotated)


MESH = pl.DeviceIdType.MESH
RING = 4
ORDER = (2, 1, 3, 0)


def ring(position, offset):
    return lax.rem(position + offset, RING)


def tile_of(index, size):
    return pl.ds(pl.multiple_of(index * size, size), size)


class Links:
    def __init__(self):
        self.band = lax.axis_index("band")
        dom = lax.axis_index("dom")
        self.core = lax.rem(dom, 2)
        self.z = lax.rem(dom // 2, RING)
        self.x = dom // (2 * RING)

    def place(self, band, x, z, core):
        return (band, (x * RING + z) * 2 + core)

    def at_band(self, offset):
        return self.place(ring(self.band, offset), self.x, self.z, self.core)

    def at_x(self, offset):
        return self.place(self.band, ring(self.x, offset), self.z, self.core)

    def at_z(self, offset):
        return self.place(self.band, self.x, ring(self.z, offset), self.core)

    def partner(self):
        return self.place(self.band, self.x, self.z, 1 - self.core)


def exchange_kernel(
    table, weights, orbitals, projectors, rotation, matrices, factors, rotated, columns,
    cells_in, cells_out, full, high_rows, low_rows, high_cells, low_cells, tiles, windows, mate, total, hop1, hop2, hop3, hop4,
    turn, turn_in, turn_out, turned, owned, pads, ready,
    sem_load, sem_keep, sem_own, sem_ready, *sems
):
    link = Links()
    b, x, z, c = link.band, link.x, link.z, link.core
    names = ("yin", "yout", "r1", "r2", "r3", "r4", "s0", "one", "two", "sum", "back", "ag1", "ag2", "agf", "core")
    send = dict(zip(names, sems[0::2]))
    recv = dict(zip(names, sems[1::2]))
    bands, cells = orbitals.shape
    slots, window, projs = projectors.shape
    wide = window + LANES
    group = matrices.shape[0]
    quarter = cells // RING
    parts = cells_in.shape[0]
    width = quarter // parts
    half = bands // 2
    sub = half // 2
    strip = turn.shape[0] // RING
    started = []

    def push(src, dst, kind, index, device):
        copy = pltpu.make_async_remote_copy(
            src_ref=src, dst_ref=dst, send_sem=send[kind].at[index], recv_sem=recv[kind].at[index],
            device_id=device, device_id_type=MESH,
        )
        copy.start()
        started.append(copy)
        return copy

    def keep(src, dst, sem):
        copy = pltpu.make_async_copy(src, dst, sem)
        copy.start()
        return copy

    barrier = pltpu.get_barrier_semaphore()
    peers = [f(o) for f in (link.at_band, link.at_x, link.at_z) for o in (1, 2, 3)] + [link.partner()]
    for peer in peers:
        pl.semaphore_signal(barrier, inc=1, device_id=peer, device_id_type=MESH)
    pl.semaphore_wait(barrier, len(peers))

    first = (x, z)
    second = (z, x)
    at_first = (link.at_x, link.at_z)
    at_second = (link.at_z, link.at_x)

    def factor_at(h, t, u, core, low=0, size=None):
        rows = pl.ds(h * half + low, half if size is None else size)
        if h == 0:
            return factors.at[t, u, core, :, rows, :]
        return factors.at[u, t, core, :, rows, :]

    r1 = {}
    for o in (1, 2, 3):
        r1[o] = push(rotation.at[x, z, c], full.at[b, x, z, c], "r1", (o - 1,), link.at_band(o))
    yin, own_cells = {}, []

    def send_cells(i):
        for o in (1, 2, 3):
            src = orbitals.at[:, tile_of(ring(b, o) * parts + i, width)]
            yin[i, o] = push(src, cells_in.at[i, b], "yin", (i, o - 1), link.at_band(o))

    send_cells(0)
    stage = [keep(orbitals.at[:, tile_of(q, quarter)], cells_out.at[q], sem_load.at[q]) for q in range(RING)]
    eighth = slots // RING
    stage_tiles = [
        keep(projectors.at[pl.ds(q * eighth, eighth)], tiles.at[pl.ds(q * eighth, eighth)], sem_load.at[RING + q])
        for q in range(RING)
    ]
    own_rows = keep(rotation, full.at[b], sem_own.at[0])
    for i in range(1, parts):
        send_cells(i)
    for i in range(parts):
        own_cells.append(keep(orbitals.at[:, tile_of(b * parts + i, width)], cells_in.at[i, b], sem_keep.at[i]))
    for k in range(GROUP):
        clear(pads.at[k], window)
    r2, r3, r4 = {}, {}, {}
    columns_of = [pl.ds(h * (full.shape[-1] // 2), full.shape[-1] // 2) for h in range(2)]
    for o in (1, 2, 3):
        r1[o].wait_recv()
        for h in range(2):
            piece = full.at[ring(b, RING - o), x, z, c, :, columns_of[h]]
            for p in (1, 2, 3):
                r2[o, p, h] = push(piece, piece, "r2", (o - 1, p - 1, h), at_first[h](p))
    for q in range(RING):
        stage[q].wait()
        top, rest = split(cells_out[q])
        for m in range(quarter // LANES):
            high_cells[q * (quarter // LANES) + m] = top[:, m * LANES : (m + 1) * LANES]
            low_cells[q * (quarter // LANES) + m] = rest[:, m * LANES : (m + 1) * LANES]
    for o in (1, 2, 3):
        k = ring(b, RING - o)
        for h in range(2):
            for p in (1, 2, 3):
                r2[o, p, h].wait_recv()
            if h == 0:
                piece = full.at[k, :, z, c, :, columns_of[h]]
            else:
                piece = full.at[k, x, :, c, :, columns_of[h]]
            for p in (1, 2, 3):
                r3[o, p, h] = push(piece, piece, "r3", (o - 1, p - 1, h), at_second[h](p))

    def to_mate(step):
        group_at = pl.ds(step * GROUP, GROUP)
        return pltpu.make_async_remote_copy(
            src_ref=windows.at[group_at], dst_ref=mate.at[group_at],
            send_sem=send["s0"].at[step], recv_sem=recv["s0"].at[step],
            device_id=link.partner(), device_id_type=MESH,
        )

    def take(step, carry):
        for k in range(GROUP):
            index = step * GROUP + k
            tile, shift = table[TILE, index], table[SHIFT, index]
            o_high, o_low = [
                jnp.concatenate([ref[tile + m] for m in range(wide // LANES)], axis=1) for ref in (high_cells, low_cells)
            ]
            p_high, p_low = shifted(tiles[index], pads.at[k], shift, window, wide)
            both = dot(o_high, jnp.concatenate([p_high, p_low], axis=1))
            windows[index] = both[:, :projs] + both[:, projs:] + dot(o_low, p_high)
        to_mate(step).start()
        return carry

    one, two = {}, {}

    def assemble(h, o):
        t = ring(first[h], o)
        rows = pl.ds(h * half, half)

        def body(u, carry):
            owner = (t * RING + u if h == 0 else u * RING + t) * 2 + c
            values = [
                ref[table[WHERE + k, owner], rows, :] for k, ref in enumerate((windows, windows, mate, mate))
            ]
            for atom in range(group):
                a, d, e, f = [value * weights[k * group + atom, owner] for k, value in enumerate(values)]
                total[h, t, u, atom] = (a + d) + (e + f)
            return carry

        lax.fori_loop(0, RING, body, 0)
        return t

    low2, high2 = pl.ds(0, 2), pl.ds(2, 2)

    def send_far(h):
        t = assemble(h, 2)
        one[h, 0, 0] = push(total.at[h, t, low2], hop1.at[h, 0], "one", (h, 0, 0), at_first[h](1))
        one[h, 1, 0] = push(total.at[h, t, high2], hop1.at[h, 1], "one", (h, 1, 0), at_first[h](3))

    steps = slots // GROUP
    for q in range(RING):
        stage_tiles[q].wait()
        lax.fori_loop(q * steps // RING, (q + 1) * steps // RING, take, 0)
    for step in range(steps):
        to_mate(step).wait_recv()
    for h in range(2):
        send_far(h)
    for h in range(2):
        t = assemble(h, 1)
        one[h, 0, 1] = push(total.at[h, t, high2], hop2.at[h, 0, high2], "one", (h, 0, 1), at_first[h](1))
    for h in range(2):
        t = assemble(h, 3)
        one[h, 1, 1] = push(total.at[h, t, low2], hop2.at[h, 1, low2], "one", (h, 1, 1), at_first[h](3))
    for h in range(2):
        assemble(h, 0)

    def add_rows(h, t, start, source):
        def body(u, carry):
            total[h, t, start + u] += source[h, start // 2, u]
            return carry

        lax.fori_loop(0, 2, body, 0)

    for h in range(2):
        one[h, 0, 0].wait_recv()
        t = ring(first[h], 1)
        add_rows(h, t, 0, hop1)
        one[h, 0, 2] = push(total.at[h, t, low2], hop2.at[h, 0, low2], "one", (h, 0, 2), at_first[h](1))
        one[h, 1, 0].wait_recv()
        t = ring(first[h], 3)
        add_rows(h, t, 2, hop1)
        one[h, 1, 2] = push(total.at[h, t, high2], hop2.at[h, 1, high2], "one", (h, 1, 2), at_first[h](3))

    for o in (1, 2, 3):
        for h in range(2):
            for p in (1, 2, 3):
                r3[o, p, h].wait_recv()
        mine = full.at[ring(b, RING - o), :, :, c]
        r4[o] = push(mine, mine, "r4", (o - 1,), link.partner())

    own_rows.wait()
    for o in (1, 2, 3):
        r4[o].wait_recv()

    def split_rows(k, carry):
        top, rest = split(full[k].reshape(bands, full.shape[-1]))
        columns = tile_of(k, full.shape[-1])
        high_rows[:, columns] = top
        low_rows[:, columns] = rest
        return carry

    lax.fori_loop(0, RING, split_rows, 0)

    yout, own_out = {}, []

    def rotate(i):
        for o in (1, 2, 3):
            yin[i, o].wait_recv()
        own_cells[i].wait()
        high, low = split(cells_in[i].reshape(RING * bands, width))
        pair = jnp.concatenate([high, low], axis=1)

        def body(k, carry):
            columns = tile_of(k, full.shape[-1])
            both = dot(high_rows[:, columns], pair)
            here = both[:, :width] + both[:, width:] + dot(low_rows[:, columns], high)
            cells_out[k, :, pl.ds(i * width, width)] = here
            return carry

        lax.fori_loop(0, RING, body, 0)
    def give(i, offsets=(1, 2, 3)):
        columns = tile_of(b * parts + i, width)
        for o in offsets:
            src = cells_out.at[ring(b, o), :, pl.ds(i * width, width)]
            yout[i, o] = push(src, rotated.at[:, columns], "yout", (i, o - 1), link.at_band(o))
        if 2 in offsets:
            own_out.append(
                keep(cells_out.at[b, :, pl.ds(i * width, width)], rotated.at[:, columns], sem_keep.at[parts + i])
            )

    for i in range(parts // 2):
        rotate(i)

    for h in range(2):
        t = first[h]
        one[h, 0, 1].wait_recv()
        one[h, 1, 1].wait_recv()
        one[h, 0, 2].wait_recv()
        one[h, 1, 2].wait_recv()

        def finish(u, carry, h=h, t=t):
            total[h, t, u] += hop2[h, 0, u] + hop2[h, 1, u]
            return carry

        lax.fori_loop(0, RING, finish, 0)
        lower, upper = pl.ds(0, sub), pl.ds(sub, sub)
        s = second[h]
        far, nxt, prv = ring(s, 2), ring(s, 1), ring(s, 3)
        two[h, 0, 0] = push(total.at[h, t, far, :, lower], hop3.at[h, 0], "two", (h, 0, 0), at_second[h](1))
        two[h, 1, 0] = push(total.at[h, t, far, :, upper], hop3.at[h, 1], "two", (h, 1, 0), at_second[h](3))
        two[h, 0, 1] = push(
            total.at[h, t, nxt, :, upper], hop4.at[h, 0, :, upper], "two", (h, 0, 1), at_second[h](1)
        )
        two[h, 1, 1] = push(
            total.at[h, t, prv, :, lower], hop4.at[h, 1, :, lower], "two", (h, 1, 1), at_second[h](3)
        )

    for h in range(2):
        t, s = first[h], second[h]
        nxt, prv = ring(s, 1), ring(s, 3)
        two[h, 0, 0].wait_recv()
        total[h, t, nxt, :, lower] += hop3[h, 0]
        two[h, 0, 2] = push(
            total.at[h, t, nxt, :, lower], hop4.at[h, 0, :, lower], "two", (h, 0, 2), at_second[h](1)
        )
        two[h, 1, 0].wait_recv()
        total[h, t, prv, :, upper] += hop3[h, 1]
        two[h, 1, 2] = push(
            total.at[h, t, prv, :, upper], hop4.at[h, 1, :, upper], "two", (h, 1, 2), at_second[h](3)
        )

    rotate(parts // 2)
    rotate(parts // 2 + 1)

    for h in range(2):
        t, s = first[h], second[h]
        for d in range(2):
            two[h, d, 1].wait_recv()
            two[h, d, 2].wait_recv()
        for atom in range(group):
            value = total[h, t, s, atom] + hop4[h, 0, atom] + hop4[h, 1, atom]
            turn[pl.ds(atom * projs, projs), pl.ds(h * half, half)] = value.T

    def strip_at(index):
        return pl.ds(pl.multiple_of(index * strip, 8), strip)

    swap, back = {}, {}
    for o in (1, 2, 3):
        swap[o] = push(turn.at[strip_at(ring(b, o))], turn_in.at[b], "sum", (o - 1,), link.at_band(o))
    turn_in[b] = turn[strip_at(b), :]
    give(0, (1, 3))

    for o in (1, 2, 3):
        swap[o].wait_recv()
    high, low = split(jnp.concatenate([turn_in[k] for k in range(RING)], axis=1))
    pair = jnp.concatenate([high, low], axis=0)

    def turn_rows(k, carry):
        columns = tile_of(k, full.shape[-1])
        both = dot_nt(pair, high_rows[:, columns])
        turn_out[k] = both[:strip] + both[strip:] + dot_nt(high, low_rows[:, columns])
        return carry

    lax.fori_loop(0, RING, turn_rows, 0)
    for o in (1, 2, 3):
        back[o] = push(turn_out.at[ring(b, o)], turned.at[strip_at(b)], "back", (o - 1,), link.at_band(o))
    turned[strip_at(b), :] = turn_out[b]

    give(0, (2,))
    for i in range(1, parts // 2 + 2):
        give(i)
    for i in range(parts // 2 + 2, parts):
        rotate(i)
        give(i)

    for o in (1, 2, 3):
        back[o].wait_recv()
    for atom in range(group):
        t_high, t_low = split(turned[pl.ds(atom * projs, projs), :].T)
        m_high, m_low = split(matrices[atom])
        both = dot(t_high, jnp.concatenate([m_high, m_low], axis=1))
        owned[atom] = both[:, :projs] + both[:, projs:] + dot(t_low, m_high)

    own_factor = keep(owned, factors.at[x, z, c], sem_own.at[1])
    mate_core = []

    def to_core(src, h, t, u, index):
        mate_core.append(push(src, factor_at(h, t, u, c), "core", (h, index), link.partner()))

    pairs = ready.shape[0]

    def put(slot, index):
        return pltpu.make_async_copy(ready.at[slot], columns.at[index], sem_ready.at[slot])

    def prepare(low, high):
        def body(step, carry):
            for k in range(pairs):
                index = step * pairs + k

                @pl.when(step > 0)
                def _(k=k, index=index):
                    put(k, index).wait()

                pad = pads.at[k]
                pad[pl.ds(LANES, window), :] = tiles[index]
                high, low = split(pad[pl.ds(LANES - table[SHIFT, index], wide), :].T)
                ready[k, pl.ds(0, projs), :] = high
                ready[k, pl.ds(projs, projs), :] = low
                put(k, index).start()
            return carry

        lax.fori_loop(low, high, body, 0)

    share = slots // pairs // 8
    ag1, ag2, agf = {}, {}, {}
    for h in range(2):
        t, s = first[h], second[h]
        for d, peer, order in ((0, 1, (0, 1)), (1, 3, (1, 0))):
            for m, part in enumerate(order):
                rows = pl.ds(h * half + part * sub, sub)
                ag1[h, d, m] = push(
                    owned.at[:, rows], factor_at(h, t, s, c, part * sub, sub), "ag1", (h, d, m), at_second[h](peer)
                )
    def spread(h, r, src, u):
        t = first[h]
        for d, peer in ((0, 1), (1, 3)):
            ag2[h, d, r] = push(src, factor_at(h, t, u, c), "ag2", (h, d, r), at_first[h](peer))
        to_core(src, h, t, u, r)

    lines = (0, 3, 1, 2)
    for h in range(2):
        spread(h, 0, owned.at[:, pl.ds(h * half, half)], second[h])
    prepare(0, share)
    for h in range(2):
        t, s = first[h], second[h]
        for d, back, peer in ((0, 3, 1), (1, 1, 3)):
            ag1[h, d, 0].wait_recv()
            piece = factor_at(h, t, ring(s, back), c, d * sub, sub)
            ag1[h, d, 2] = push(piece, piece, "ag1", (h, d, 2), at_second[h](peer))
    prepare(share, 2 * share)
    for h in range(2):
        t, s = first[h], second[h]
        for d, r in ((0, 1), (1, 2)):
            ag1[h, d, 1].wait_recv()
            u = ring(s, lines[r])
            spread(h, r, factor_at(h, t, u, c), u)
    prepare(2 * share, 3 * share)
    for h in range(2):
        t, s = first[h], second[h]
        ag1[h, 0, 2].wait_recv()
        ag1[h, 1, 2].wait_recv()
        u = ring(s, 2)
        spread(h, 3, factor_at(h, t, u, c), u)
    prepare(3 * share, 4 * share)

    for r in range(RING):
        for h in range(2):
            u = ring(second[h], lines[r])
            for d, back, peer in ((0, 3, 1), (1, 1, 3)):
                ag2[h, d, r].wait_recv()
                t = ring(first[h], back)
                piece = factor_at(h, t, u, c)
                if (r < 2) == (d == 0):
                    agf[h, r] = push(piece, piece, "agf", (h, r), at_first[h](peer))
                to_core(piece, h, t, u, RING * (1 + d) + r)
        prepare((4 + r) * share, (5 + r) * share)
    for r in range(RING):
        for h in range(2):
            u = ring(second[h], lines[r])
            agf[h, r].wait_recv()
            t = ring(first[h], 2)
            to_core(factor_at(h, t, u, c), h, t, u, RING * 3 + r)

    for copy in mate_core:
        copy.wait_recv()
    for copy in yout.values():
        copy.wait_recv()
    for copy in own_out:
        copy.wait()
    own_factor.wait()
    for k in range(pairs):
        put(k, k).wait()
    for copy in started:
        copy.wait_send()
    for step in range(slots // GROUP):
        to_mate(step).wait_send()


PARTS = 8


def exchange(table, weights, orbitals, projectors, rotation, matrices):
    bands, cells = orbitals.shape
    slots, window, projs = projectors.shape
    all_bands = rotation.shape[1]
    group = matrices.shape[0]
    atoms = 2 * RING * RING * group
    width = cells // RING // PARTS
    half = bands // 2
    sub = half // 2
    rows = bands // (2 * RING * RING)
    strip = group * projs // RING
    f32, bf16 = jnp.float32, jnp.bfloat16
    counts = [
        (PARTS, 3), (PARTS, 3), (3,), (3, 3, 2), (3, 3, 2), (3,), (slots // GROUP,), (2, 2, 3), (2, 2, 3), (3,), (3,),
        (2, 2, 3), (2, 2, RING), (2, RING), (2, 4 * RING),
    ]
    dma = pltpu.SemaphoreType.DMA
    in_hbm = pl.BlockSpec(memory_space=pltpu.MemorySpace.HBM)
    factors, rotated, columns = pl.pallas_call(
        exchange_kernel,
        out_shape=(
            jax.ShapeDtypeStruct((RING, RING, 2, group, bands, projs), f32),
            jax.ShapeDtypeStruct((bands, cells), f32),
            jax.ShapeDtypeStruct((slots, 2 * projs, window + LANES), bf16),
        ),
        in_specs=[pl.BlockSpec(memory_space=pltpu.SMEM)] * 2
        + [in_hbm] * 3
        + [pl.BlockSpec(memory_space=pltpu.VMEM)],
        out_specs=[in_hbm] * 3,
        scratch_shapes=[
            pltpu.VMEM((PARTS, RING, bands, width), f32),
            pltpu.VMEM((RING, bands, cells // RING), f32),
            pltpu.VMEM((RING, RING, RING, 2, rows, all_bands), f32),
            pltpu.VMEM((bands, RING * all_bands), bf16),
            pltpu.VMEM((bands, RING * all_bands), bf16),
            pltpu.VMEM((cells // LANES, bands, LANES), bf16),
            pltpu.VMEM((cells // LANES, bands, LANES), bf16),
            pltpu.VMEM((slots, window, projs), f32),
            pltpu.VMEM((slots, bands, projs), f32),
            pltpu.VMEM((slots, bands, projs), f32),
            pltpu.VMEM((2, RING, RING, group, half, projs), f32),
            pltpu.VMEM((2, 2, 2, group, half, projs), f32),
            pltpu.VMEM((2, 2, RING, group, half, projs), f32),
            pltpu.VMEM((2, 2, group, sub, projs), f32),
            pltpu.VMEM((2, 2, group, half, projs), f32),
            pltpu.VMEM((group * projs, bands), f32),
            pltpu.VMEM((RING, strip, bands), f32),
            pltpu.VMEM((RING, strip, bands), f32),
            pltpu.VMEM((group * projs, bands), f32),
            pltpu.VMEM((group, bands, projs), f32),
            pltpu.VMEM((GROUP, window + 2 * LANES, projs), f32),
            pltpu.VMEM((2, 2 * projs, window + LANES), bf16),
            dma((2 * RING,)),
            dma((2 * PARTS,)),
            dma((2,)),
            dma((2,)),
        ]
        + [dma(shape) for shape in counts for _ in range(2)],
        compiler_params=pltpu.CompilerParams(
            collective_id=0, has_side_effects=True, vmem_limit_bytes=60 << 20
        ),
        name="exchange",
    )(
        table, weights, orbitals, projectors, rotation.reshape(RING, RING, 2, rows, all_bands), matrices
    )
    return factors.reshape(atoms, bands, projs), rotated, columns


def per_device(orbitals, projectors, window_start, slot_atom, atom_home, atom_matrices, rotation):
    dom = lax.axis_index("dom").astype(jnp.int32).reshape(1)
    window = projectors.shape[1]
    table, weights = list_slots(
        dom, window_start, slot_atom, atom_home, atom_matrices.shape[0], orbitals.shape[1], window + LANES
    )
    factors, rotated, columns = exchange(table, weights, orbitals, projectors, rotation, atom_matrices)
    return update(table, factors, columns, rotated)


def solution(mesh):
    in_specs = (
        P("band", "dom"),
        P("dom", None, None),
        P("dom"),
        P(),
        P(),
        P("dom", None, None),
        P("band", None),
    )
    out_specs = P("band", "dom")
    return jax.shard_map(
        per_device, mesh=mesh, in_specs=in_specs, out_specs=out_specs, check_vma=False
    )
```

```python
import functools

import jax
import jax.numpy as jnp
from jax import lax
from jax.experimental import pallas as pl
from jax.experimental.pallas import tpu as pltpu
from jax.sharding import PartitionSpec as P

LANES = 128
GROUP = 4
UPDATE_GROUP = 8


def split(value):
    high = value.astype(jnp.bfloat16)
    low = (value - high.astype(jnp.float32)).astype(jnp.bfloat16)
    return high, low


def dot(a, b):
    return jnp.dot(a, b, preferred_element_type=jnp.float32)


def dot_nt(a, b):
    return lax.dot_general(a, b, (((1,), (1,)), ((), ())), preferred_element_type=jnp.float32)


def shifted(projector, pad, shift, window, wide):
    pad[pl.ds(LANES, window), :] = projector
    return split(pad[pl.ds(LANES - shift, wide), :])


def clear(pad, window):
    edge = jnp.zeros((LANES, pad.shape[1]), jnp.float32)
    pad[pl.ds(0, LANES), :] = edge
    pad[pl.ds(LANES + window, LANES), :] = edge


TILE, SHIFT, ROW, WHERE = 0, 1, 2, 3
TABLE_ROWS = 16


def list_kernel(dom, start, slot_atom, home, table, weights, *, group, cells, wide):
    lane = lax.broadcasted_iota(jnp.int32, (1, LANES), 1)
    blank = jnp.zeros((1, LANES), jnp.int32)
    none = jnp.full((1, LANES), -1, jnp.int32)
    core = lax.rem(dom[0], 2)

    def enter(domain):
        def body(slot, carry):
            row_of, where0, local0, where1, local1 = carry
            row = home[slot_atom[domain, slot]]
            owner = row // group
            local = row - owner * group
            here = lane == owner
            taken = here & (local0 >= 0)
            fresh = here & (local0 < 0)
            where1 = jnp.where(taken, slot, where1)
            local1 = jnp.where(taken, local, local1)
            where0 = jnp.where(fresh, slot, where0)
            local0 = jnp.where(fresh, local, local0)
            return jnp.where(lane == slot, row, row_of), where0, local0, where1, local1

        return lax.fori_loop(0, start.shape[0], body, (blank, blank, none, blank, none), unroll=8)

    def locate(slot, carry):
        tile = jnp.minimum(start[slot] // LANES, (cells - wide) // LANES)
        cell_of, shift_of = carry
        cell_of = jnp.where(lane == slot, tile, cell_of)
        return cell_of, jnp.where(lane == slot, start[slot] - tile * LANES, shift_of)

    cell_of, shift_of = lax.fori_loop(0, start.shape[0], locate, (blank, blank), unroll=8)
    row_of, own0, own_local0, own1, own_local1 = enter(dom[0])
    _, mate0, mate_local0, mate1, mate_local1 = enter(dom[0] + 1 - 2 * core)
    rows = [cell_of, shift_of, row_of, own0, own1, mate0, mate1]
    for index, row in enumerate(rows):
        table[index : index + 1, :] = row
    for index, local in enumerate([own_local0, own_local1, mate_local0, mate_local1]):
        for atom in range(group):
            at = index * group + atom
            weights[at : at + 1, :] = (local == atom).astype(jnp.float32)


def list_slots(dom, start, slot_atom, home, group, cells, wide):
    return pl.pallas_call(
        functools.partial(list_kernel, group=group, cells=cells, wide=wide),
        out_shape=[jax.ShapeDtypeStruct((TABLE_ROWS, LANES), kind) for kind in (jnp.int32, jnp.float32)],
        in_specs=[pl.BlockSpec(memory_space=pltpu.SMEM)] * 4,
        out_specs=[pl.BlockSpec(memory_space=pltpu.VMEM)] * 2,
        compiler_params=pltpu.CompilerParams(vmem_limit_bytes=60 << 20),
        name="list_slots",
    )(dom, start, slot_atom, home)


def update_kernel(table, *refs):
    group = UPDATE_GROUP
    factors = refs[:group]
    columns, rotated, out, base, sem = refs[group:]
    step = pl.program_id(0)
    _, both, wide = columns.shape
    projs = both // 2
    fetch = pltpu.make_async_copy(rotated, base, sem)

    @pl.when(step == 0)
    def _():
        fetch.start()
        out[...] = jnp.zeros_like(out)

    for k in range(group):
        slot = step * group + k
        cell = pl.multiple_of(table[TILE, slot] * LANES, LANES)
        f_high, f_low = split(factors[k][0])
        p_high, p_low = columns[k, :projs, :], columns[k, projs:, :]
        out[:, pl.ds(cell, wide)] += dot(
            jnp.concatenate([f_high, f_low, f_high], axis=1),
            jnp.concatenate([p_high, p_high, p_low], axis=0),
        )

    @pl.when(step == pl.num_programs(0) - 1)
    def _():
        fetch.wait()
        out[...] += base[...]


def update(table, factors, columns, rotated):
    slots, both, wide = columns.shape
    bands, cells = rotated.shape
    projs = both // 2

    def factor_spec(k):
        return pl.BlockSpec(
            (1, bands, projs),
            lambda i, table: (table[ROW, i * UPDATE_GROUP + k], 0, 0),
        )

    return pl.pallas_call(
        update_kernel,
        out_shape=jax.ShapeDtypeStruct((bands, cells), jnp.float32),
        grid_spec=pltpu.PrefetchScalarGridSpec(
            num_scalar_prefetch=1,
            grid=(slots // UPDATE_GROUP,),
            in_specs=[factor_spec(k) for k in range(UPDATE_GROUP)]
            + [
                pl.BlockSpec((UPDATE_GROUP, both, wide), lambda i, *_: (i, 0, 0)),
                pl.BlockSpec(memory_space=pltpu.MemorySpace.HBM),
            ],
            out_specs=pl.BlockSpec(
                (bands, cells), lambda i, *_: (0, 0), pipeline_mode=pl.Buffered(1)
            ),
            scratch_shapes=[pltpu.VMEM((bands, cells), jnp.float32), pltpu.SemaphoreType.DMA],
        ),
        cost_estimate=pl.CostEstimate(
            flops=6 * slots * wide * bands * projs, bytes_accessed=22 << 20, transcendentals=0
        ),
        compiler_params=pltpu.CompilerParams(vmem_limit_bytes=60 << 20),
        name="update",
    )(table, *([factors] * UPDATE_GROUP), columns, rotated)


MESH = pl.DeviceIdType.MESH
RING = 4
ORDER = (2, 1, 3, 0)


def ring(position, offset):
    return lax.rem(position + offset, RING)


def tile_of(index, size):
    return pl.ds(pl.multiple_of(index * size, size), size)


class Links:
    def __init__(self):
        self.band = lax.axis_index("band")
        dom = lax.axis_index("dom")
        self.core = lax.rem(dom, 2)
        self.z = lax.rem(dom // 2, RING)
        self.x = dom // (2 * RING)

    def place(self, band, x, z, core):
        return (band, (x * RING + z) * 2 + core)

    def at_band(self, offset):
        return self.place(ring(self.band, offset), self.x, self.z, self.core)

    def at_x(self, offset):
        return self.place(self.band, ring(self.x, offset), self.z, self.core)

    def at_z(self, offset):
        return self.place(self.band, self.x, ring(self.z, offset), self.core)

    def partner(self):
        return self.place(self.band, self.x, self.z, 1 - self.core)


def exchange_kernel(
    table, weights, orbitals, projectors, rotation, matrices, factors, rotated, columns,
    cells_in, cells_out, full, high_rows, low_rows, high_cells, low_cells, tiles, windows, mate, total, hop1, hop2, hop3, hop4,
    turn, turn_in, turn_out, turned, owned, pads, ready,
    sem_load, sem_keep, sem_own, sem_ready, *sems
):
    link = Links()
    b, x, z, c = link.band, link.x, link.z, link.core
    names = ("yin", "yout", "r1", "r2", "r3", "r4", "s0", "one", "two", "sum", "back", "ag1", "ag2", "agf", "core")
    send = dict(zip(names, sems[0::2]))
    recv = dict(zip(names, sems[1::2]))
    bands, cells = orbitals.shape
    slots, window, projs = projectors.shape
    wide = window + LANES
    group = matrices.shape[0]
    quarter = cells // RING
    parts = cells_in.shape[0]
    width = quarter // parts
    half = bands // 2
    sub = half // 2
    strip = turn.shape[0] // RING
    started = []

    def push(src, dst, kind, index, device):
        copy = pltpu.make_async_remote_copy(
            src_ref=src, dst_ref=dst, send_sem=send[kind].at[index], recv_sem=recv[kind].at[index],
            device_id=device, device_id_type=MESH,
        )
        copy.start()
        started.append(copy)
        return copy

    def keep(src, dst, sem):
        copy = pltpu.make_async_copy(src, dst, sem)
        copy.start()
        return copy

    barrier = pltpu.get_barrier_semaphore()
    peers = [f(o) for f in (link.at_band, link.at_x, link.at_z) for o in (1, 2, 3)] + [link.partner()]
    for peer in peers:
        pl.semaphore_signal(barrier, inc=1, device_id=peer, device_id_type=MESH)
    stage = [keep(orbitals.at[:, tile_of(q, quarter)], cells_out.at[q], sem_load.at[q]) for q in range(RING)]
    eighth = slots // RING
    stage_tiles = [
        keep(projectors.at[pl.ds(q * eighth, eighth)], tiles.at[pl.ds(q * eighth, eighth)], sem_load.at[RING + q])
        for q in range(RING)
    ]
    own_rows = keep(rotation, full.at[b], sem_own.at[0])
    for k in range(GROUP):
        clear(pads.at[k], window)
    pl.semaphore_wait(barrier, len(peers))

    first = (x, z)
    second = (z, x)
    at_first = (link.at_x, link.at_z)
    at_second = (link.at_z, link.at_x)

    def factor_at(h, t, u, core, low=0, size=None):
        rows = pl.ds(h * half + low, half if size is None else size)
        if h == 0:
            return factors.at[t, u, core, :, rows, :]
        return factors.at[u, t, core, :, rows, :]

    r1 = {}
    for o in (1, 2, 3):
        r1[o] = push(rotation.at[x, z, c], full.at[b, x, z, c], "r1", (o - 1,), link.at_band(o))
    yin, own_cells = {}, []

    def send_cells(i):
        for o in (1, 2, 3):
            src = orbitals.at[:, tile_of(ring(b, o) * parts + i, width)]
            yin[i, o] = push(src, cells_in.at[i, b], "yin", (i, o - 1), link.at_band(o))

    send_cells(0)
    for i in range(1, parts):
        send_cells(i)
    for i in range(parts):
        own_cells.append(keep(orbitals.at[:, tile_of(b * parts + i, width)], cells_in.at[i, b], sem_keep.at[i]))
    r2, r3, r4 = {}, {}, {}
    columns_of = [pl.ds(h * (full.shape[-1] // 2), full.shape[-1] // 2) for h in range(2)]
    routes = [(1, 0, slice(None)), (2, 0, columns_of[0]), (2, 1, columns_of[1]), (3, 1, slice(None))]
    for q in range(RING):
        stage[q].wait()
        top, rest = split(cells_out[q])
        for m in range(quarter // LANES):
            high_cells[q * (quarter // LANES) + m] = top[:, m * LANES : (m + 1) * LANES]
            low_cells[q * (quarter // LANES) + m] = rest[:, m * LANES : (m + 1) * LANES]
    def to_mate(step):
        group_at = pl.ds(step * GROUP, GROUP)
        return pltpu.make_async_remote_copy(
            src_ref=windows.at[group_at], dst_ref=mate.at[group_at],
            send_sem=send["s0"].at[step], recv_sem=recv["s0"].at[step],
            device_id=link.partner(), device_id_type=MESH,
        )

    def take(step, carry):
        for k in range(GROUP):
            index = step * GROUP + k
            tile, shift = table[TILE, index], table[SHIFT, index]
            o_high, o_low = [
                jnp.concatenate([ref[tile + m] for m in range(wide // LANES)], axis=1) for ref in (high_cells, low_cells)
            ]
            p_high, p_low = shifted(tiles[index], pads.at[k], shift, window, wide)
            both = dot(o_high, jnp.concatenate([p_high, p_low], axis=1))
            windows[index] = both[:, :projs] + both[:, projs:] + dot(o_low, p_high)
        to_mate(step).start()
        return carry

    one, two = {}, {}

    def assemble(h, o):
        t = ring(first[h], o)
        rows = pl.ds(h * half, half)

        def body(u, carry):
            owner = (t * RING + u if h == 0 else u * RING + t) * 2 + c
            values = [
                ref[table[WHERE + k, owner], rows, :] for k, ref in enumerate((windows, windows, mate, mate))
            ]
            for atom in range(group):
                a, d, e, f = [value * weights[k * group + atom, owner] for k, value in enumerate(values)]
                total[h, t, u, atom] = (a + d) + (e + f)
            return carry

        lax.fori_loop(0, RING, body, 0)
        return t

    low2, high2 = pl.ds(0, 2), pl.ds(2, 2)

    def send_far(h):
        t = assemble(h, 2)
        one[h, 0, 0] = push(total.at[h, t, low2], hop1.at[h, 0], "one", (h, 0, 0), at_first[h](1))
        one[h, 1, 0] = push(total.at[h, t, high2], hop1.at[h, 1], "one", (h, 1, 0), at_first[h](3))

    steps = slots // GROUP
    for q in range(RING):
        stage_tiles[q].wait()
        lax.fori_loop(q * steps // RING, (q + 1) * steps // RING, take, 0)
        if q == 0:
            for o in (1, 2, 3):
                r1[o].wait_recv()
            for n, (o, h, span) in enumerate(routes):
                piece = full.at[ring(b, RING - o), x, z, c, :, span]
                for p in (1, 2, 3):
                    r2[n, p] = push(piece, piece, "r2", (n, p - 1), at_first[h](p))
        if q == 2:
            for n, (o, h, span) in enumerate(routes):
                k = ring(b, RING - o)
                for p in (1, 2, 3):
                    r2[n, p].wait_recv()
                piece = full.at[k, :, z, c, :, span] if h == 0 else full.at[k, x, :, c, :, span]
                for p in (1, 2, 3):
                    r3[n, p] = push(piece, piece, "r3", (n, p - 1), at_second[h](p))
    for step in range(steps):
        to_mate(step).wait_recv()
    for h in range(2):
        send_far(h)
    for h in range(2):
        t = assemble(h, 1)
        one[h, 0, 1] = push(total.at[h, t, high2], hop2.at[h, 0, high2], "one", (h, 0, 1), at_first[h](1))
    for h in range(2):
        t = assemble(h, 3)
        one[h, 1, 1] = push(total.at[h, t, low2], hop2.at[h, 1, low2], "one", (h, 1, 1), at_first[h](3))
    for h in range(2):
        assemble(h, 0)

    def add_rows(h, t, start, source):
        def body(u, carry):
            total[h, t, start + u] += source[h, start // 2, u]
            return carry

        lax.fori_loop(0, 2, body, 0)

    for h in range(2):
        one[h, 0, 0].wait_recv()
        t = ring(first[h], 1)
        add_rows(h, t, 0, hop1)
        one[h, 0, 2] = push(total.at[h, t, low2], hop2.at[h, 0, low2], "one", (h, 0, 2), at_first[h](1))
        one[h, 1, 0].wait_recv()
        t = ring(first[h], 3)
        add_rows(h, t, 2, hop1)
        one[h, 1, 2] = push(total.at[h, t, high2], hop2.at[h, 1, high2], "one", (h, 1, 2), at_first[h](3))

    for copy in r3.values():
        copy.wait_recv()
    for o in (1, 2, 3):
        mine = full.at[ring(b, RING - o), :, :, c]
        r4[o] = push(mine, mine, "r4", (o - 1,), link.partner())

    own_rows.wait()
    for o in (1, 2, 3):
        r4[o].wait_recv()

    def split_rows(k, carry):
        top, rest = split(full[k].reshape(bands, full.shape[-1]))
        columns = tile_of(k, full.shape[-1])
        high_rows[:, columns] = top
        low_rows[:, columns] = rest
        return carry

    lax.fori_loop(0, RING, split_rows, 0)

    yout, own_out = {}, []

    def rotate(i):
        for o in (1, 2, 3):
            yin[i, o].wait_recv()
        own_cells[i].wait()
        high, low = split(cells_in[i].reshape(RING * bands, width))
        pair = jnp.concatenate([high, low], axis=1)

        def body(k, carry):
            columns = tile_of(k, full.shape[-1])
            both = dot(high_rows[:, columns], pair)
            here = both[:, :width] + both[:, width:] + dot(low_rows[:, columns], high)
            cells_out[k, :, pl.ds(i * width, width)] = here
            return carry

        lax.fori_loop(0, RING, body, 0)
    def give(unit, offsets=(1, 2, 3)):
        i, lower = unit // 2, unit % 2
        rows, columns = pl.ds(lower * half, half), tile_of(b * parts + i, width)
        for o in offsets:
            src = cells_out.at[ring(b, o), rows, pl.ds(i * width, width)]
            yout[unit, o] = push(src, rotated.at[rows, columns], "yout", (unit, o - 1), link.at_band(o))
        if 2 in offsets:
            src = cells_out.at[b, rows, pl.ds(i * width, width)]
            own_out.append(keep(src, rotated.at[rows, columns], sem_keep.at[parts + unit]))

    rotate(0)
    rotate(1)
    give(0)

    for h in range(2):
        t = first[h]
        one[h, 0, 1].wait_recv()
        one[h, 1, 1].wait_recv()
        one[h, 0, 2].wait_recv()
        one[h, 1, 2].wait_recv()

        def finish(u, carry, h=h, t=t):
            total[h, t, u] += hop2[h, 0, u] + hop2[h, 1, u]
            return carry

        lax.fori_loop(0, RING, finish, 0)
        lower, upper = pl.ds(0, sub), pl.ds(sub, sub)
        s = second[h]
        far, nxt, prv = ring(s, 2), ring(s, 1), ring(s, 3)
        two[h, 0, 0] = push(total.at[h, t, far, :, lower], hop3.at[h, 0], "two", (h, 0, 0), at_second[h](1))
        two[h, 1, 0] = push(total.at[h, t, far, :, upper], hop3.at[h, 1], "two", (h, 1, 0), at_second[h](3))
        two[h, 0, 1] = push(
            total.at[h, t, nxt, :, upper], hop4.at[h, 0, :, upper], "two", (h, 0, 1), at_second[h](1)
        )
        two[h, 1, 1] = push(
            total.at[h, t, prv, :, lower], hop4.at[h, 1, :, lower], "two", (h, 1, 1), at_second[h](3)
        )

    for h in range(2):
        t, s = first[h], second[h]
        nxt, prv = ring(s, 1), ring(s, 3)
        two[h, 0, 0].wait_recv()
        total[h, t, nxt, :, lower] += hop3[h, 0]
        two[h, 0, 2] = push(
            total.at[h, t, nxt, :, lower], hop4.at[h, 0, :, lower], "two", (h, 0, 2), at_second[h](1)
        )
        two[h, 1, 0].wait_recv()
        total[h, t, prv, :, upper] += hop3[h, 1]
        two[h, 1, 2] = push(
            total.at[h, t, prv, :, upper], hop4.at[h, 1, :, upper], "two", (h, 1, 2), at_second[h](3)
        )

    rotate(2)

    for h in range(2):
        t, s = first[h], second[h]
        for d in range(2):
            two[h, d, 1].wait_recv()
            two[h, d, 2].wait_recv()
        for atom in range(group):
            value = total[h, t, s, atom] + hop4[h, 0, atom] + hop4[h, 1, atom]
            turn[pl.ds(atom * projs, projs), pl.ds(h * half, half)] = value.T

    def strip_at(index):
        return pl.ds(pl.multiple_of(index * strip, 8), strip)

    swap, back = {}, {}
    for o in (1, 2, 3):
        swap[o] = push(turn.at[strip_at(ring(b, o))], turn_in.at[b], "sum", (o - 1,), link.at_band(o))
    turn_in[b] = turn[strip_at(b), :]
    give(1, (1, 3))

    for o in (1, 2, 3):
        swap[o].wait_recv()
    high, low = split(jnp.concatenate([turn_in[k] for k in range(RING)], axis=1))
    pair = jnp.concatenate([high, low], axis=0)

    def turn_rows(k, carry):
        columns = tile_of(k, full.shape[-1])
        both = dot_nt(pair, high_rows[:, columns])
        turn_out[k] = both[:strip] + both[strip:] + dot_nt(high, low_rows[:, columns])
        return carry

    lax.fori_loop(0, RING, turn_rows, 0)
    for o in (1, 2, 3):
        back[o] = push(turn_out.at[ring(b, o)], turned.at[strip_at(b)], "back", (o - 1,), link.at_band(o))
    turned[strip_at(b), :] = turn_out[b]

    give(1, (2,))
    for unit in range(2, 6):
        give(unit)
    rotate(3)
    give(6)
    give(7)

    for o in (1, 2, 3):
        back[o].wait_recv()
    for atom in range(group):
        t_high, t_low = split(turned[pl.ds(atom * projs, projs), :].T)
        m_high, m_low = split(matrices[atom])
        both = dot(t_high, jnp.concatenate([m_high, m_low], axis=1))
        owned[atom] = both[:, :projs] + both[:, projs:] + dot(t_low, m_high)

    own_factor = keep(owned, factors.at[x, z, c], sem_own.at[1])
    mate_core = []

    def to_core(src, h, t, u, index):
        mate_core.append(push(src, factor_at(h, t, u, c), "core", (h, index), link.partner()))

    pairs = ready.shape[0]

    def put(slot, index):
        return pltpu.make_async_copy(ready.at[slot], columns.at[index], sem_ready.at[slot])

    def prepare(low, high):
        def body(step, carry):
            for k in range(pairs):
                index = step * pairs + k

                @pl.when(step > 0)
                def _(k=k, index=index):
                    put(k, index).wait()

                pad = pads.at[k]
                pad[pl.ds(LANES, window), :] = tiles[index]
                high, low = split(pad[pl.ds(LANES - table[SHIFT, index], wide), :].T)
                ready[k, pl.ds(0, projs), :] = high
                ready[k, pl.ds(projs, projs), :] = low
                put(k, index).start()
            return carry

        lax.fori_loop(low, high, body, 0)

    share = slots // pairs // 8
    ag1, ag2, agf = {}, {}, {}
    for h in range(2):
        t, s = first[h], second[h]
        for d, peer, order in ((0, 1, (0, 1)), (1, 3, (1, 0))):
            for m, part in enumerate(order):
                rows = pl.ds(h * half + part * sub, sub)
                ag1[h, d, m] = push(
                    owned.at[:, rows], factor_at(h, t, s, c, part * sub, sub), "ag1", (h, d, m), at_second[h](peer)
                )
    def spread(h, r, src, u):
        t = first[h]
        for d, peer in ((0, 1), (1, 3)):
            ag2[h, d, r] = push(src, factor_at(h, t, u, c), "ag2", (h, d, r), at_first[h](peer))
        to_core(src, h, t, u, r)

    lines = (0, 3, 1, 2)
    for h in range(2):
        spread(h, 0, owned.at[:, pl.ds(h * half, half)], second[h])
    prepare(0, share)
    for h in range(2):
        t, s = first[h], second[h]
        for d, back, peer in ((0, 3, 1), (1, 1, 3)):
            ag1[h, d, 0].wait_recv()
            piece = factor_at(h, t, ring(s, back), c, d * sub, sub)
            ag1[h, d, 2] = push(piece, piece, "ag1", (h, d, 2), at_second[h](peer))
    prepare(share, 2 * share)
    for h in range(2):
        t, s = first[h], second[h]
        for d, r in ((0, 1), (1, 2)):
            ag1[h, d, 1].wait_recv()
            u = ring(s, lines[r])
            spread(h, r, factor_at(h, t, u, c), u)
    prepare(2 * share, 3 * share)
    for h in range(2):
        t, s = first[h], second[h]
        ag1[h, 0, 2].wait_recv()
        ag1[h, 1, 2].wait_recv()
        u = ring(s, 2)
        spread(h, 3, factor_at(h, t, u, c), u)
    prepare(3 * share, 4 * share)

    for r in range(RING):
        for h in range(2):
            u = ring(second[h], lines[r])
            for d, back, peer in ((0, 3, 1), (1, 1, 3)):
                ag2[h, d, r].wait_recv()
                t = ring(first[h], back)
                piece = factor_at(h, t, u, c)
                if (r < 2) == (d == 0):
                    agf[h, r] = push(piece, piece, "agf", (h, r), at_first[h](peer))
                to_core(piece, h, t, u, RING * (1 + d) + r)
        prepare((4 + r) * share, (5 + r) * share)
    for r in range(RING):
        for h in range(2):
            u = ring(second[h], lines[r])
            agf[h, r].wait_recv()
            t = ring(first[h], 2)
            to_core(factor_at(h, t, u, c), h, t, u, RING * 3 + r)

    for copy in mate_core:
        copy.wait_recv()
    for copy in yout.values():
        copy.wait_recv()
    for copy in own_out:
        copy.wait()
    own_factor.wait()
    for k in range(pairs):
        put(k, k).wait()
    for copy in started:
        copy.wait_send()
    for step in range(slots // GROUP):
        to_mate(step).wait_send()


PARTS = 4


def exchange(table, weights, orbitals, projectors, rotation, matrices):
    bands, cells = orbitals.shape
    slots, window, projs = projectors.shape
    all_bands = rotation.shape[1]
    group = matrices.shape[0]
    atoms = 2 * RING * RING * group
    width = cells // RING // PARTS
    half = bands // 2
    sub = half // 2
    rows = bands // (2 * RING * RING)
    strip = group * projs // RING
    f32, bf16 = jnp.float32, jnp.bfloat16
    counts = [
        (PARTS, 3), (2 * PARTS, 3), (3,), (4, 3), (4, 3), (3,), (slots // GROUP,), (2, 2, 3), (2, 2, 3), (3,), (3,),
        (2, 2, 3), (2, 2, RING), (2, RING), (2, 4 * RING),
    ]
    dma = pltpu.SemaphoreType.DMA
    in_hbm = pl.BlockSpec(memory_space=pltpu.MemorySpace.HBM)
    factors, rotated, columns = pl.pallas_call(
        exchange_kernel,
        out_shape=(
            jax.ShapeDtypeStruct((RING, RING, 2, group, bands, projs), f32),
            jax.ShapeDtypeStruct((bands, cells), f32),
            jax.ShapeDtypeStruct((slots, 2 * projs, window + LANES), bf16),
        ),
        in_specs=[pl.BlockSpec(memory_space=pltpu.SMEM)] * 2
        + [in_hbm] * 3
        + [pl.BlockSpec(memory_space=pltpu.VMEM)],
        out_specs=[in_hbm] * 3,
        scratch_shapes=[
            pltpu.VMEM((PARTS, RING, bands, width), f32),
            pltpu.VMEM((RING, bands, cells // RING), f32),
            pltpu.VMEM((RING, RING, RING, 2, rows, all_bands), f32),
            pltpu.VMEM((bands, RING * all_bands), bf16),
            pltpu.VMEM((bands, RING * all_bands), bf16),
            pltpu.VMEM((cells // LANES, bands, LANES), bf16),
            pltpu.VMEM((cells // LANES, bands, LANES), bf16),
            pltpu.VMEM((slots, window, projs), f32),
            pltpu.VMEM((slots, bands, projs), f32),
            pltpu.VMEM((slots, bands, projs), f32),
            pltpu.VMEM((2, RING, RING, group, half, projs), f32),
            pltpu.VMEM((2, 2, 2, group, half, projs), f32),
            pltpu.VMEM((2, 2, RING, group, half, projs), f32),
            pltpu.VMEM((2, 2, group, sub, projs), f32),
            pltpu.VMEM((2, 2, group, half, projs), f32),
            pltpu.VMEM((group * projs, bands), f32),
            pltpu.VMEM((RING, strip, bands), f32),
            pltpu.VMEM((RING, strip, bands), f32),
            pltpu.VMEM((group * projs, bands), f32),
            pltpu.VMEM((group, bands, projs), f32),
            pltpu.VMEM((GROUP, window + 2 * LANES, projs), f32),
            pltpu.VMEM((2, 2 * projs, window + LANES), bf16),
            dma((2 * RING,)),
            dma((3 * PARTS,)),
            dma((2,)),
            dma((2,)),
        ]
        + [dma(shape) for shape in counts for _ in range(2)],
        compiler_params=pltpu.CompilerParams(
            collective_id=0, has_side_effects=True, vmem_limit_bytes=60 << 20
        ),
        name="exchange",
    )(
        table, weights, orbitals, projectors, rotation.reshape(RING, RING, 2, rows, all_bands), matrices
    )
    return factors.reshape(atoms, bands, projs), rotated, columns


def per_device(orbitals, projectors, window_start, slot_atom, atom_home, atom_matrices, rotation):
    dom = lax.axis_index("dom").astype(jnp.int32).reshape(1)
    window = projectors.shape[1]
    table, weights = list_slots(
        dom, window_start, slot_atom, atom_home, atom_matrices.shape[0], orbitals.shape[1], window + LANES
    )
    factors, rotated, columns = exchange(table, weights, orbitals, projectors, rotation, atom_matrices)
    return update(table, factors, columns, rotated)


def solution(mesh):
    in_specs = (
        P("band", "dom"),
        P("dom", None, None),
        P("dom"),
        P(),
        P(),
        P("dom", None, None),
        P("band", None),
    )
    out_specs = P("band", "dom")
    return jax.shard_map(
        per_device, mesh=mesh, in_specs=in_specs, out_specs=out_specs, check_vma=False
    )
```

```python
import functools

import jax
import jax.numpy as jnp
from jax import lax
from jax.experimental import pallas as pl
from jax.experimental.pallas import tpu as pltpu
from jax.sharding import PartitionSpec as P

LANES = 128
GROUP = 4
UPDATE_GROUP = 8


def split(value):
    high = value.astype(jnp.bfloat16)
    low = (value - high.astype(jnp.float32)).astype(jnp.bfloat16)
    return high, low


def dot(a, b):
    return jnp.dot(a, b, preferred_element_type=jnp.float32)


def dot_nt(a, b):
    return lax.dot_general(a, b, (((1,), (1,)), ((), ())), preferred_element_type=jnp.float32)


def shifted(projector, pad, shift, window, wide):
    pad[pl.ds(LANES, window), :] = projector
    return split(pad[pl.ds(LANES - shift, wide), :])


def clear(pad, window):
    edge = jnp.zeros((LANES, pad.shape[1]), jnp.float32)
    pad[pl.ds(0, LANES), :] = edge
    pad[pl.ds(LANES + window, LANES), :] = edge


TILE, SHIFT, ROW, WHERE = 0, 1, 2, 3
TABLE_ROWS = 16


def list_kernel(dom, start, slot_atom, home, table, weights, *, group, cells, wide):
    lane = lax.broadcasted_iota(jnp.int32, (1, LANES), 1)
    blank = jnp.zeros((1, LANES), jnp.int32)
    none = jnp.full((1, LANES), -1, jnp.int32)
    core = lax.rem(dom[0], 2)

    def enter(domain):
        def body(slot, carry):
            row_of, where0, local0, where1, local1 = carry
            row = home[slot_atom[domain, slot]]
            owner = row // group
            local = row - owner * group
            here = lane == owner
            taken = here & (local0 >= 0)
            fresh = here & (local0 < 0)
            where1 = jnp.where(taken, slot, where1)
            local1 = jnp.where(taken, local, local1)
            where0 = jnp.where(fresh, slot, where0)
            local0 = jnp.where(fresh, local, local0)
            return jnp.where(lane == slot, row, row_of), where0, local0, where1, local1

        return lax.fori_loop(0, start.shape[0], body, (blank, blank, none, blank, none), unroll=8)

    def locate(slot, carry):
        tile = jnp.minimum(start[slot] // LANES, (cells - wide) // LANES)
        cell_of, shift_of = carry
        cell_of = jnp.where(lane == slot, tile, cell_of)
        return cell_of, jnp.where(lane == slot, start[slot] - tile * LANES, shift_of)

    cell_of, shift_of = lax.fori_loop(0, start.shape[0], locate, (blank, blank), unroll=8)
    row_of, own0, own_local0, own1, own_local1 = enter(dom[0])
    _, mate0, mate_local0, mate1, mate_local1 = enter(dom[0] + 1 - 2 * core)
    rows = [cell_of, shift_of, row_of, own0, own1, mate0, mate1]
    for index, row in enumerate(rows):
        table[index : index + 1, :] = row
    for index, local in enumerate([own_local0, own_local1, mate_local0, mate_local1]):
        for atom in range(group):
            at = index * group + atom
            weights[at : at + 1, :] = (local == atom).astype(jnp.float32)


def list_slots(dom, start, slot_atom, home, group, cells, wide):
    return pl.pallas_call(
        functools.partial(list_kernel, group=group, cells=cells, wide=wide),
        out_shape=[jax.ShapeDtypeStruct((TABLE_ROWS, LANES), kind) for kind in (jnp.int32, jnp.float32)],
        in_specs=[pl.BlockSpec(memory_space=pltpu.SMEM)] * 4,
        out_specs=[pl.BlockSpec(memory_space=pltpu.VMEM)] * 2,
        compiler_params=pltpu.CompilerParams(vmem_limit_bytes=60 << 20),
        name="list_slots",
    )(dom, start, slot_atom, home)


def update_kernel(table, *refs):
    group = UPDATE_GROUP
    factors = refs[:group]
    columns, rotated, out, base, sem = refs[group:]
    step = pl.program_id(0)
    _, both, wide = columns.shape
    projs = both // 2
    fetch = pltpu.make_async_copy(rotated, base, sem)

    @pl.when(step == 0)
    def _():
        fetch.start()
        out[...] = jnp.zeros_like(out)

    for k in range(group):
        slot = step * group + k
        cell = pl.multiple_of(table[TILE, slot] * LANES, LANES)
        f_high, f_low = split(factors[k][0])
        p_high, p_low = columns[k, :projs, :], columns[k, projs:, :]
        out[:, pl.ds(cell, wide)] += dot(
            jnp.concatenate([f_high, f_low, f_high], axis=1),
            jnp.concatenate([p_high, p_high, p_low], axis=0),
        )

    @pl.when(step == pl.num_programs(0) - 1)
    def _():
        fetch.wait()
        out[...] += base[...]


def update(table, factors, columns, rotated):
    slots, both, wide = columns.shape
    bands, cells = rotated.shape
    projs = both // 2

    def factor_spec(k):
        return pl.BlockSpec(
            (1, bands, projs),
            lambda i, table: (table[ROW, i * UPDATE_GROUP + k], 0, 0),
        )

    return pl.pallas_call(
        update_kernel,
        out_shape=jax.ShapeDtypeStruct((bands, cells), jnp.float32),
        grid_spec=pltpu.PrefetchScalarGridSpec(
            num_scalar_prefetch=1,
            grid=(slots // UPDATE_GROUP,),
            in_specs=[factor_spec(k) for k in range(UPDATE_GROUP)]
            + [
                pl.BlockSpec((UPDATE_GROUP, both, wide), lambda i, *_: (i, 0, 0)),
                pl.BlockSpec(memory_space=pltpu.MemorySpace.HBM),
            ],
            out_specs=pl.BlockSpec(
                (bands, cells), lambda i, *_: (0, 0), pipeline_mode=pl.Buffered(1)
            ),
            scratch_shapes=[pltpu.VMEM((bands, cells), jnp.float32), pltpu.SemaphoreType.DMA],
        ),
        cost_estimate=pl.CostEstimate(
            flops=6 * slots * wide * bands * projs, bytes_accessed=22 << 20, transcendentals=0
        ),
        compiler_params=pltpu.CompilerParams(vmem_limit_bytes=60 << 20),
        name="update",
    )(table, *([factors] * UPDATE_GROUP), columns, rotated)


MESH = pl.DeviceIdType.MESH
RING = 4
ORDER = (2, 1, 3, 0)


def ring(position, offset):
    return lax.rem(position + offset, RING)


def tile_of(index, size):
    return pl.ds(pl.multiple_of(index * size, size), size)


class Links:
    def __init__(self):
        self.band = lax.axis_index("band")
        dom = lax.axis_index("dom")
        self.core = lax.rem(dom, 2)
        self.z = lax.rem(dom // 2, RING)
        self.x = dom // (2 * RING)

    def place(self, band, x, z, core):
        return (band, (x * RING + z) * 2 + core)

    def at_band(self, offset):
        return self.place(ring(self.band, offset), self.x, self.z, self.core)

    def at_x(self, offset):
        return self.place(self.band, ring(self.x, offset), self.z, self.core)

    def at_z(self, offset):
        return self.place(self.band, self.x, ring(self.z, offset), self.core)

    def partner(self):
        return self.place(self.band, self.x, self.z, 1 - self.core)


def exchange_kernel(
    table, weights, orbitals, projectors, rotation, matrices, factors, rotated, columns,
    cells_in, cells_out, full, high_rows, low_rows, high_cells, low_cells, tiles, windows, mate, total, hop1, hop2, hop3, hop4,
    turn, turn_in, turn_out, turned, owned, pads, ready,
    sem_load, sem_keep, sem_own, sem_ready, *sems
):
    link = Links()
    b, x, z, c = link.band, link.x, link.z, link.core
    names = ("yin", "yout", "r1", "r2", "r3", "r4", "s0", "one", "two", "sum", "back", "ag1", "ag2", "agf", "core")
    send = dict(zip(names, sems[0::2]))
    recv = dict(zip(names, sems[1::2]))
    bands, cells = orbitals.shape
    slots, window, projs = projectors.shape
    wide = window + LANES
    group = matrices.shape[0]
    quarter = cells // RING
    parts = cells_in.shape[0]
    width = quarter // parts
    half = bands // 2
    sub = half // 2
    strip = turn.shape[0] // RING
    started = []

    def push(src, dst, kind, index, device):
        copy = pltpu.make_async_remote_copy(
            src_ref=src, dst_ref=dst, send_sem=send[kind].at[index], recv_sem=recv[kind].at[index],
            device_id=device, device_id_type=MESH,
        )
        copy.start()
        started.append(copy)
        return copy

    def keep(src, dst, sem):
        copy = pltpu.make_async_copy(src, dst, sem)
        copy.start()
        return copy

    barrier = pltpu.get_barrier_semaphore()
    peers = [f(o) for f in (link.at_band, link.at_x, link.at_z) for o in (1, 2, 3)] + [link.partner()]
    for peer in peers:
        pl.semaphore_signal(barrier, inc=1, device_id=peer, device_id_type=MESH)
    stage = [keep(orbitals.at[:, tile_of(q, quarter)], cells_out.at[q], sem_load.at[q]) for q in range(RING)]
    eighth = slots // RING
    stage_tiles = [
        keep(projectors.at[pl.ds(q * eighth, eighth)], tiles.at[pl.ds(q * eighth, eighth)], sem_load.at[RING + q])
        for q in range(RING)
    ]
    own_rows = keep(rotation, full.at[b], sem_own.at[0])
    for k in range(GROUP):
        clear(pads.at[k], window)
    pl.semaphore_wait(barrier, len(peers))

    first = (x, z)
    second = (z, x)
    at_first = (link.at_x, link.at_z)
    at_second = (link.at_z, link.at_x)

    def factor_at(h, t, u, core, low=0, size=None):
        rows = pl.ds(h * half + low, half if size is None else size)
        if h == 0:
            return factors.at[t, u, core, :, rows, :]
        return factors.at[u, t, core, :, rows, :]

    r1 = {}
    for o in (1, 2, 3):
        r1[o] = push(rotation.at[x, z, c], full.at[b, x, z, c], "r1", (o - 1,), link.at_band(o))
    yin, own_cells = {}, []

    def send_cells(i):
        for o in (1, 2, 3):
            src = orbitals.at[:, tile_of(ring(b, o) * parts + i, width)]
            yin[i, o] = push(src, cells_in.at[i, b], "yin", (i, o - 1), link.at_band(o))

    send_cells(0)
    for i in range(1, parts):
        send_cells(i)
    for i in range(parts):
        own_cells.append(keep(orbitals.at[:, tile_of(b * parts + i, width)], cells_in.at[i, b], sem_keep.at[i]))
    r2, r3, r4 = {}, {}, {}
    columns_of = [pl.ds(h * (full.shape[-1] // 2), full.shape[-1] // 2) for h in range(2)]
    routes = [(1, 0, slice(None)), (2, 0, columns_of[0]), (2, 1, columns_of[1]), (3, 1, slice(None))]
    for q in range(RING):
        stage[q].wait()
        top, rest = split(cells_out[q])
        for m in range(quarter // LANES):
            high_cells[q * (quarter // LANES) + m] = top[:, m * LANES : (m + 1) * LANES]
            low_cells[q * (quarter // LANES) + m] = rest[:, m * LANES : (m + 1) * LANES]
    def to_mate(step):
        group_at = pl.ds(step * GROUP, GROUP)
        return pltpu.make_async_remote_copy(
            src_ref=windows.at[group_at], dst_ref=mate.at[group_at],
            send_sem=send["s0"].at[step], recv_sem=recv["s0"].at[step],
            device_id=link.partner(), device_id_type=MESH,
        )

    def take(step, carry):
        for k in range(GROUP):
            index = step * GROUP + k
            tile, shift = table[TILE, index], table[SHIFT, index]
            o_high, o_low = [
                jnp.concatenate([ref[tile + m] for m in range(wide // LANES)], axis=1) for ref in (high_cells, low_cells)
            ]
            p_high, p_low = shifted(tiles[index], pads.at[k], shift, window, wide)
            both = dot(o_high, jnp.concatenate([p_high, p_low], axis=1))
            windows[index] = both[:, :projs] + both[:, projs:] + dot(o_low, p_high)
        to_mate(step).start()
        return carry

    one, two = {}, {}

    def assemble(h, o):
        t = ring(first[h], o)
        rows = pl.ds(h * half, half)

        def body(u, carry):
            owner = (t * RING + u if h == 0 else u * RING + t) * 2 + c
            values = [
                ref[table[WHERE + k, owner], rows, :] for k, ref in enumerate((windows, windows, mate, mate))
            ]
            for atom in range(group):
                a, d, e, f = [value * weights[k * group + atom, owner] for k, value in enumerate(values)]
                total[h, t, u, atom] = (a + d) + (e + f)
            return carry

        lax.fori_loop(0, RING, body, 0)
        return t

    low2, high2 = pl.ds(0, 2), pl.ds(2, 2)

    def send_far(h):
        t = assemble(h, 2)
        one[h, 0, 0] = push(total.at[h, t, low2], hop1.at[h, 0], "one", (h, 0, 0), at_first[h](1))
        one[h, 1, 0] = push(total.at[h, t, high2], hop1.at[h, 1], "one", (h, 1, 0), at_first[h](3))

    steps = slots // GROUP
    for q in range(RING):
        stage_tiles[q].wait()
        lax.fori_loop(q * steps // RING, (q + 1) * steps // RING, take, 0)
        if q == 1:
            for o in (1, 2, 3):
                r1[o].wait_recv()
            for n, (o, h, span) in enumerate(routes):
                piece = full.at[ring(b, RING - o), x, z, c, :, span]
                for p in (1, 2, 3):
                    r2[n, p] = push(piece, piece, "r2", (n, p - 1), at_first[h](p))
        if q == 3:
            for n, (o, h, span) in enumerate(routes):
                k = ring(b, RING - o)
                for p in (1, 2, 3):
                    r2[n, p].wait_recv()
                piece = full.at[k, :, z, c, :, span] if h == 0 else full.at[k, x, :, c, :, span]
                for p in (1, 2, 3):
                    r3[n, p] = push(piece, piece, "r3", (n, p - 1), at_second[h](p))
    for step in range(steps):
        to_mate(step).wait_recv()
    for h in range(2):
        send_far(h)
    for h in range(2):
        t = assemble(h, 1)
        one[h, 0, 1] = push(total.at[h, t, high2], hop2.at[h, 0, high2], "one", (h, 0, 1), at_first[h](1))
    for h in range(2):
        t = assemble(h, 3)
        one[h, 1, 1] = push(total.at[h, t, low2], hop2.at[h, 1, low2], "one", (h, 1, 1), at_first[h](3))
    for h in range(2):
        assemble(h, 0)

    def add_rows(h, t, start, source):
        def body(u, carry):
            total[h, t, start + u] += source[h, start // 2, u]
            return carry

        lax.fori_loop(0, 2, body, 0)

    for h in range(2):
        one[h, 0, 0].wait_recv()
        t = ring(first[h], 1)
        add_rows(h, t, 0, hop1)
        one[h, 0, 2] = push(total.at[h, t, low2], hop2.at[h, 0, low2], "one", (h, 0, 2), at_first[h](1))
        one[h, 1, 0].wait_recv()
        t = ring(first[h], 3)
        add_rows(h, t, 2, hop1)
        one[h, 1, 2] = push(total.at[h, t, high2], hop2.at[h, 1, high2], "one", (h, 1, 2), at_first[h](3))

    for copy in r3.values():
        copy.wait_recv()
    for o in (1, 2, 3):
        mine = full.at[ring(b, RING - o), :, :, c]
        r4[o] = push(mine, mine, "r4", (o - 1,), link.partner())

    own_rows.wait()
    for o in (1, 2, 3):
        r4[o].wait_recv()

    def split_rows(k, carry):
        top, rest = split(full[k].reshape(bands, full.shape[-1]))
        columns = tile_of(k, full.shape[-1])
        high_rows[:, columns] = top
        low_rows[:, columns] = rest
        return carry

    lax.fori_loop(0, RING, split_rows, 0)

    yout, own_out = {}, []

    def rotate(i):
        for o in (1, 2, 3):
            yin[i, o].wait_recv()
        own_cells[i].wait()
        high, low = split(cells_in[i].reshape(RING * bands, width))
        pair = jnp.concatenate([high, low], axis=1)

        def body(k, carry):
            columns = tile_of(k, full.shape[-1])
            both = dot(high_rows[:, columns], pair)
            here = both[:, :width] + both[:, width:] + dot(low_rows[:, columns], high)
            cells_out[k, :, pl.ds(i * width, width)] = here
            return carry

        lax.fori_loop(0, RING, body, 0)
    def give(unit, offsets=(1, 2, 3)):
        i, lower = unit // 2, unit % 2
        rows, columns = pl.ds(lower * half, half), tile_of(b * parts + i, width)
        for o in offsets:
            src = cells_out.at[ring(b, o), rows, pl.ds(i * width, width)]
            yout[unit, o] = push(src, rotated.at[rows, columns], "yout", (unit, o - 1), link.at_band(o))
        if 2 in offsets:
            src = cells_out.at[b, rows, pl.ds(i * width, width)]
            own_out.append(keep(src, rotated.at[rows, columns], sem_keep.at[parts + unit]))

    rotate(0)
    rotate(1)
    give(0)

    for h in range(2):
        t = first[h]
        one[h, 0, 1].wait_recv()
        one[h, 1, 1].wait_recv()
        one[h, 0, 2].wait_recv()
        one[h, 1, 2].wait_recv()

        def finish(u, carry, h=h, t=t):
            total[h, t, u] += hop2[h, 0, u] + hop2[h, 1, u]
            return carry

        lax.fori_loop(0, RING, finish, 0)
        lower, upper = pl.ds(0, sub), pl.ds(sub, sub)
        s = second[h]
        far, nxt, prv = ring(s, 2), ring(s, 1), ring(s, 3)
        two[h, 0, 0] = push(total.at[h, t, far, :, lower], hop3.at[h, 0], "two", (h, 0, 0), at_second[h](1))
        two[h, 1, 0] = push(total.at[h, t, far, :, upper], hop3.at[h, 1], "two", (h, 1, 0), at_second[h](3))
        two[h, 0, 1] = push(
            total.at[h, t, nxt, :, upper], hop4.at[h, 0, :, upper], "two", (h, 0, 1), at_second[h](1)
        )
        two[h, 1, 1] = push(
            total.at[h, t, prv, :, lower], hop4.at[h, 1, :, lower], "two", (h, 1, 1), at_second[h](3)
        )

    for h in range(2):
        t, s = first[h], second[h]
        nxt, prv = ring(s, 1), ring(s, 3)
        two[h, 0, 0].wait_recv()
        total[h, t, nxt, :, lower] += hop3[h, 0]
        two[h, 0, 2] = push(
            total.at[h, t, nxt, :, lower], hop4.at[h, 0, :, lower], "two", (h, 0, 2), at_second[h](1)
        )
        two[h, 1, 0].wait_recv()
        total[h, t, prv, :, upper] += hop3[h, 1]
        two[h, 1, 2] = push(
            total.at[h, t, prv, :, upper], hop4.at[h, 1, :, upper], "two", (h, 1, 2), at_second[h](3)
        )

    rotate(2)

    for h in range(2):
        t, s = first[h], second[h]
        for d in range(2):
            two[h, d, 1].wait_recv()
            two[h, d, 2].wait_recv()
        for atom in range(group):
            value = total[h, t, s, atom] + hop4[h, 0, atom] + hop4[h, 1, atom]
            turn[pl.ds(atom * projs, projs), pl.ds(h * half, half)] = value.T

    def strip_at(index):
        return pl.ds(pl.multiple_of(index * strip, 8), strip)

    swap, back = {}, {}
    for o in (1, 2, 3):
        swap[o] = push(turn.at[strip_at(ring(b, o))], turn_in.at[b], "sum", (o - 1,), link.at_band(o))
    turn_in[b] = turn[strip_at(b), :]
    give(1, (1, 3))

    for o in (1, 2, 3):
        swap[o].wait_recv()
    high, low = split(jnp.concatenate([turn_in[k] for k in range(RING)], axis=1))
    pair = jnp.concatenate([high, low], axis=0)

    def turn_rows(k, carry):
        columns = tile_of(k, full.shape[-1])
        both = dot_nt(pair, high_rows[:, columns])
        turn_out[k] = both[:strip] + both[strip:] + dot_nt(high, low_rows[:, columns])
        return carry

    lax.fori_loop(0, RING, turn_rows, 0)
    for o in (1, 2, 3):
        back[o] = push(turn_out.at[ring(b, o)], turned.at[strip_at(b)], "back", (o - 1,), link.at_band(o))
    turned[strip_at(b), :] = turn_out[b]

    give(1, (2,))
    for unit in range(2, 6):
        give(unit)
    rotate(3)
    give(6)
    give(7)

    for o in (1, 2, 3):
        back[o].wait_recv()
    for atom in range(group):
        t_high, t_low = split(turned[pl.ds(atom * projs, projs), :].T)
        m_high, m_low = split(matrices[atom])
        both = dot(t_high, jnp.concatenate([m_high, m_low], axis=1))
        owned[atom] = both[:, :projs] + both[:, projs:] + dot(t_low, m_high)

    own_factor = keep(owned, factors.at[x, z, c], sem_own.at[1])
    mate_core = []

    def to_core(src, h, t, u, index):
        mate_core.append(push(src, factor_at(h, t, u, c), "core", (h, index), link.partner()))

    pairs = ready.shape[0]

    def put(slot, index):
        return pltpu.make_async_copy(ready.at[slot], columns.at[index], sem_ready.at[slot])

    def prepare(low, high):
        def body(step, carry):
            for k in range(pairs):
                index = step * pairs + k

                @pl.when(step > 0)
                def _(k=k, index=index):
                    put(k, index).wait()

                pad = pads.at[k]
                pad[pl.ds(LANES, window), :] = tiles[index]
                high, low = split(pad[pl.ds(LANES - table[SHIFT, index], wide), :].T)
                ready[k, pl.ds(0, projs), :] = high
                ready[k, pl.ds(projs, projs), :] = low
                put(k, index).start()
            return carry

        lax.fori_loop(low, high, body, 0)

    share = slots // pairs // 8
    ag1, ag2, agf = {}, {}, {}
    for h in range(2):
        t, s = first[h], second[h]
        for d, peer, order in ((0, 1, (0, 1)), (1, 3, (1, 0))):
            for m, part in enumerate(order):
                rows = pl.ds(h * half + part * sub, sub)
                ag1[h, d, m] = push(
                    owned.at[:, rows], factor_at(h, t, s, c, part * sub, sub), "ag1", (h, d, m), at_second[h](peer)
                )
    def spread(h, r, src, u):
        t = first[h]
        for d, peer in ((0, 1), (1, 3)):
            ag2[h, d, r] = push(src, factor_at(h, t, u, c), "ag2", (h, d, r), at_first[h](peer))
        to_core(src, h, t, u, r)

    lines = (0, 3, 1, 2)
    for h in range(2):
        spread(h, 0, owned.at[:, pl.ds(h * half, half)], second[h])
    prepare(0, share)
    for h in range(2):
        t, s = first[h], second[h]
        for d, back, peer in ((0, 3, 1), (1, 1, 3)):
            ag1[h, d, 0].wait_recv()
            piece = factor_at(h, t, ring(s, back), c, d * sub, sub)
            ag1[h, d, 2] = push(piece, piece, "ag1", (h, d, 2), at_second[h](peer))
    prepare(share, 2 * share)
    for h in range(2):
        t, s = first[h], second[h]
        for d, r in ((0, 1), (1, 2)):
            ag1[h, d, 1].wait_recv()
            u = ring(s, lines[r])
            spread(h, r, factor_at(h, t, u, c), u)
    prepare(2 * share, 3 * share)
    for h in range(2):
        t, s = first[h], second[h]
        ag1[h, 0, 2].wait_recv()
        ag1[h, 1, 2].wait_recv()
        u = ring(s, 2)
        spread(h, 3, factor_at(h, t, u, c), u)
    prepare(3 * share, 4 * share)

    for r in range(RING):
        for h in range(2):
            u = ring(second[h], lines[r])
            for d, back, peer in ((0, 3, 1), (1, 1, 3)):
                ag2[h, d, r].wait_recv()
                t = ring(first[h], back)
                piece = factor_at(h, t, u, c)
                if (r < 2) == (d == 0):
                    agf[h, r] = push(piece, piece, "agf", (h, r), at_first[h](peer))
                to_core(piece, h, t, u, RING * (1 + d) + r)
        prepare((4 + r) * share, (5 + r) * share)
    for r in range(RING):
        for h in range(2):
            u = ring(second[h], lines[r])
            agf[h, r].wait_recv()
            t = ring(first[h], 2)
            to_core(factor_at(h, t, u, c), h, t, u, RING * 3 + r)

    for copy in mate_core:
        copy.wait_recv()
    for copy in yout.values():
        copy.wait_recv()
    for copy in own_out:
        copy.wait()
    own_factor.wait()
    for k in range(pairs):
        put(k, k).wait()
    for copy in started:
        copy.wait_send()
    for step in range(slots // GROUP):
        to_mate(step).wait_send()


PARTS = 4


def exchange(table, weights, orbitals, projectors, rotation, matrices):
    bands, cells = orbitals.shape
    slots, window, projs = projectors.shape
    all_bands = rotation.shape[1]
    group = matrices.shape[0]
    atoms = 2 * RING * RING * group
    width = cells // RING // PARTS
    half = bands // 2
    sub = half // 2
    rows = bands // (2 * RING * RING)
    strip = group * projs // RING
    f32, bf16 = jnp.float32, jnp.bfloat16
    counts = [
        (PARTS, 3), (2 * PARTS, 3), (3,), (4, 3), (4, 3), (3,), (slots // GROUP,), (2, 2, 3), (2, 2, 3), (3,), (3,),
        (2, 2, 3), (2, 2, RING), (2, RING), (2, 4 * RING),
    ]
    dma = pltpu.SemaphoreType.DMA
    in_hbm = pl.BlockSpec(memory_space=pltpu.MemorySpace.HBM)
    factors, rotated, columns = pl.pallas_call(
        exchange_kernel,
        out_shape=(
            jax.ShapeDtypeStruct((RING, RING, 2, group, bands, projs), f32),
            jax.ShapeDtypeStruct((bands, cells), f32),
            jax.ShapeDtypeStruct((slots, 2 * projs, window + LANES), bf16),
        ),
        in_specs=[pl.BlockSpec(memory_space=pltpu.SMEM)] * 2
        + [in_hbm] * 3
        + [pl.BlockSpec(memory_space=pltpu.VMEM)],
        out_specs=[in_hbm] * 3,
        scratch_shapes=[
            pltpu.VMEM((PARTS, RING, bands, width), f32),
            pltpu.VMEM((RING, bands, cells // RING), f32),
            pltpu.VMEM((RING, RING, RING, 2, rows, all_bands), f32),
            pltpu.VMEM((bands, RING * all_bands), bf16),
            pltpu.VMEM((bands, RING * all_bands), bf16),
            pltpu.VMEM((cells // LANES, bands, LANES), bf16),
            pltpu.VMEM((cells // LANES, bands, LANES), bf16),
            pltpu.VMEM((slots, window, projs), f32),
            pltpu.VMEM((slots, bands, projs), f32),
            pltpu.VMEM((slots, bands, projs), f32),
            pltpu.VMEM((2, RING, RING, group, half, projs), f32),
            pltpu.VMEM((2, 2, 2, group, half, projs), f32),
            pltpu.VMEM((2, 2, RING, group, half, projs), f32),
            pltpu.VMEM((2, 2, group, sub, projs), f32),
            pltpu.VMEM((2, 2, group, half, projs), f32),
            pltpu.VMEM((group * projs, bands), f32),
            pltpu.VMEM((RING, strip, bands), f32),
            pltpu.VMEM((RING, strip, bands), f32),
            pltpu.VMEM((group * projs, bands), f32),
            pltpu.VMEM((group, bands, projs), f32),
            pltpu.VMEM((GROUP, window + 2 * LANES, projs), f32),
            pltpu.VMEM((2, 2 * projs, window + LANES), bf16),
            dma((2 * RING,)),
            dma((3 * PARTS,)),
            dma((2,)),
            dma((2,)),
        ]
        + [dma(shape) for shape in counts for _ in range(2)],
        compiler_params=pltpu.CompilerParams(
            collective_id=0, has_side_effects=True, vmem_limit_bytes=60 << 20
        ),
        name="exchange",
    )(
        table, weights, orbitals, projectors, rotation.reshape(RING, RING, 2, rows, all_bands), matrices
    )
    return factors.reshape(atoms, bands, projs), rotated, columns


def per_device(orbitals, projectors, window_start, slot_atom, atom_home, atom_matrices, rotation):
    dom = lax.axis_index("dom").astype(jnp.int32).reshape(1)
    window = projectors.shape[1]
    table, weights = list_slots(
        dom, window_start, slot_atom, atom_home, atom_matrices.shape[0], orbitals.shape[1], window + LANES
    )
    factors, rotated, columns = exchange(table, weights, orbitals, projectors, rotation, atom_matrices)
    return update(table, factors, columns, rotated)


def solution(mesh):
    in_specs = (
        P("band", "dom"),
        P("dom", None, None),
        P("dom"),
        P(),
        P(),
        P("dom", None, None),
        P("band", None),
    )
    out_specs = P("band", "dom")
    return jax.shard_map(
        per_device, mesh=mesh, in_specs=in_specs, out_specs=out_specs, check_vma=False
    )
```

```python
import functools

import jax
import jax.numpy as jnp
from jax import lax
from jax.experimental import pallas as pl
from jax.experimental.pallas import tpu as pltpu
from jax.sharding import PartitionSpec as P

LANES = 128
GROUP = 4
UPDATE_GROUP = 8


def split(value):
    high = value.astype(jnp.bfloat16)
    low = (value - high.astype(jnp.float32)).astype(jnp.bfloat16)
    return high, low


def dot(a, b):
    return jnp.dot(a, b, preferred_element_type=jnp.float32)


def dot_nt(a, b):
    return lax.dot_general(a, b, (((1,), (1,)), ((), ())), preferred_element_type=jnp.float32)


def shifted(projector, pad, shift, window, wide):
    pad[pl.ds(LANES, window), :] = projector
    return split(pad[pl.ds(LANES - shift, wide), :])


def clear(pad, window):
    edge = jnp.zeros((LANES, pad.shape[1]), jnp.float32)
    pad[pl.ds(0, LANES), :] = edge
    pad[pl.ds(LANES + window, LANES), :] = edge


TILE, SHIFT, ROW, WHERE = 0, 1, 2, 3
TABLE_ROWS = 16


def list_kernel(dom, start, slot_atom, home, table, weights, *, group, cells, wide):
    lane = lax.broadcasted_iota(jnp.int32, (1, LANES), 1)
    blank = jnp.zeros((1, LANES), jnp.int32)
    none = jnp.full((1, LANES), -1, jnp.int32)
    core = lax.rem(dom[0], 2)

    def enter(domain):
        def body(slot, carry):
            row_of, where0, local0, where1, local1 = carry
            row = home[slot_atom[domain, slot]]
            owner = row // group
            local = row - owner * group
            here = lane == owner
            taken = here & (local0 >= 0)
            fresh = here & (local0 < 0)
            where1 = jnp.where(taken, slot, where1)
            local1 = jnp.where(taken, local, local1)
            where0 = jnp.where(fresh, slot, where0)
            local0 = jnp.where(fresh, local, local0)
            return jnp.where(lane == slot, row, row_of), where0, local0, where1, local1

        return lax.fori_loop(0, start.shape[0], body, (blank, blank, none, blank, none), unroll=8)

    def locate(slot, carry):
        tile = jnp.minimum(start[slot] // LANES, (cells - wide) // LANES)
        cell_of, shift_of = carry
        cell_of = jnp.where(lane == slot, tile, cell_of)
        return cell_of, jnp.where(lane == slot, start[slot] - tile * LANES, shift_of)

    cell_of, shift_of = lax.fori_loop(0, start.shape[0], locate, (blank, blank), unroll=8)
    row_of, own0, own_local0, own1, own_local1 = enter(dom[0])
    _, mate0, mate_local0, mate1, mate_local1 = enter(dom[0] + 1 - 2 * core)
    rows = [cell_of, shift_of, row_of, own0, own1, mate0, mate1]
    for index, row in enumerate(rows):
        table[index : index + 1, :] = row
    for index, local in enumerate([own_local0, own_local1, mate_local0, mate_local1]):
        for atom in range(group):
            at = index * group + atom
            weights[at : at + 1, :] = (local == atom).astype(jnp.float32)


def list_slots(dom, start, slot_atom, home, group, cells, wide):
    return pl.pallas_call(
        functools.partial(list_kernel, group=group, cells=cells, wide=wide),
        out_shape=[jax.ShapeDtypeStruct((TABLE_ROWS, LANES), kind) for kind in (jnp.int32, jnp.float32)],
        in_specs=[pl.BlockSpec(memory_space=pltpu.SMEM)] * 4,
        out_specs=[pl.BlockSpec(memory_space=pltpu.VMEM)] * 2,
        compiler_params=pltpu.CompilerParams(vmem_limit_bytes=60 << 20),
        name="list_slots",
    )(dom, start, slot_atom, home)


def update_kernel(table, *refs):
    group = UPDATE_GROUP
    factors = refs[:group]
    columns, rotated, out, base, sem = refs[group:]
    step = pl.program_id(0)
    _, both, wide = columns.shape
    projs = both // 2
    fetch = pltpu.make_async_copy(rotated, base, sem)

    @pl.when(step == 0)
    def _():
        fetch.start()
        out[...] = jnp.zeros_like(out)

    for k in range(group):
        slot = step * group + k
        cell = pl.multiple_of(table[TILE, slot] * LANES, LANES)
        f_high, f_low = split(factors[k][0])
        p_high, p_low = columns[k, :projs, :], columns[k, projs:, :]
        out[:, pl.ds(cell, wide)] += dot(
            jnp.concatenate([f_high, f_low, f_high], axis=1),
            jnp.concatenate([p_high, p_high, p_low], axis=0),
        )

    @pl.when(step == pl.num_programs(0) - 1)
    def _():
        fetch.wait()
        out[...] += base[...]


def update(table, factors, columns, rotated):
    slots, both, wide = columns.shape
    bands, cells = rotated.shape
    projs = both // 2

    def factor_spec(k):
        return pl.BlockSpec(
            (1, bands, projs),
            lambda i, table: (table[ROW, i * UPDATE_GROUP + k], 0, 0),
        )

    return pl.pallas_call(
        update_kernel,
        out_shape=jax.ShapeDtypeStruct((bands, cells), jnp.float32),
        grid_spec=pltpu.PrefetchScalarGridSpec(
            num_scalar_prefetch=1,
            grid=(slots // UPDATE_GROUP,),
            in_specs=[factor_spec(k) for k in range(UPDATE_GROUP)]
            + [
                pl.BlockSpec((UPDATE_GROUP, both, wide), lambda i, *_: (i, 0, 0)),
                pl.BlockSpec(memory_space=pltpu.MemorySpace.HBM),
            ],
            out_specs=pl.BlockSpec(
                (bands, cells), lambda i, *_: (0, 0), pipeline_mode=pl.Buffered(1)
            ),
            scratch_shapes=[pltpu.VMEM((bands, cells), jnp.float32), pltpu.SemaphoreType.DMA],
        ),
        cost_estimate=pl.CostEstimate(
            flops=6 * slots * wide * bands * projs, bytes_accessed=22 << 20, transcendentals=0
        ),
        compiler_params=pltpu.CompilerParams(vmem_limit_bytes=60 << 20),
        name="update",
    )(table, *([factors] * UPDATE_GROUP), columns, rotated)


MESH = pl.DeviceIdType.MESH
RING = 4
ORDER = (2, 1, 3, 0)


def ring(position, offset):
    return lax.rem(position + offset, RING)


def tile_of(index, size):
    return pl.ds(pl.multiple_of(index * size, size), size)


class Links:
    def __init__(self):
        self.band = lax.axis_index("band")
        dom = lax.axis_index("dom")
        self.core = lax.rem(dom, 2)
        self.z = lax.rem(dom // 2, RING)
        self.x = dom // (2 * RING)

    def place(self, band, x, z, core):
        return (band, (x * RING + z) * 2 + core)

    def at_band(self, offset):
        return self.place(ring(self.band, offset), self.x, self.z, self.core)

    def at_x(self, offset):
        return self.place(self.band, ring(self.x, offset), self.z, self.core)

    def at_z(self, offset):
        return self.place(self.band, self.x, ring(self.z, offset), self.core)

    def partner(self):
        return self.place(self.band, self.x, self.z, 1 - self.core)


def exchange_kernel(
    table, weights, orbitals, projectors, rotation, matrices, factors, rotated, columns,
    cells_in, cells_out, full, high_rows, low_rows, high_cells, low_cells, tiles, windows, mate, total, hop1, hop2, hop3, hop4,
    turn, turn_in, turn_out, turned, owned, pads, ready,
    sem_load, sem_keep, sem_own, sem_ready, *sems
):
    link = Links()
    b, x, z, c = link.band, link.x, link.z, link.core
    names = ("yin", "yout", "r1", "r2", "r3", "r4", "s0", "one", "two", "sum", "back", "ag1", "ag2", "agf", "core")
    send = dict(zip(names, sems[0::2]))
    recv = dict(zip(names, sems[1::2]))
    bands, cells = orbitals.shape
    slots, window, projs = projectors.shape
    wide = window + LANES
    group = matrices.shape[0]
    quarter = cells // RING
    parts = cells_in.shape[0]
    width = quarter // parts
    half = bands // 2
    sub = half // 2
    strip = turn.shape[0] // RING
    started = []

    def push(src, dst, kind, index, device):
        copy = pltpu.make_async_remote_copy(
            src_ref=src, dst_ref=dst, send_sem=send[kind].at[index], recv_sem=recv[kind].at[index],
            device_id=device, device_id_type=MESH,
        )
        copy.start()
        started.append(copy)
        return copy

    def keep(src, dst, sem):
        copy = pltpu.make_async_copy(src, dst, sem)
        copy.start()
        return copy

    barrier = pltpu.get_barrier_semaphore()
    peers = [f(o) for f in (link.at_band, link.at_x, link.at_z) for o in (1, 2, 3)] + [link.partner()]
    for peer in peers:
        pl.semaphore_signal(barrier, inc=1, device_id=peer, device_id_type=MESH)
    stage = [keep(orbitals.at[:, tile_of(q, quarter)], cells_out.at[q], sem_load.at[q]) for q in range(RING)]
    eighth = slots // RING
    stage_tiles = [
        keep(projectors.at[pl.ds(q * eighth, eighth)], tiles.at[pl.ds(q * eighth, eighth)], sem_load.at[RING + q])
        for q in range(RING)
    ]
    own_rows = keep(rotation, full.at[b], sem_own.at[0])
    for k in range(GROUP):
        clear(pads.at[k], window)
    pl.semaphore_wait(barrier, len(peers))

    first = (x, z)
    second = (z, x)
    at_first = (link.at_x, link.at_z)
    at_second = (link.at_z, link.at_x)

    def factor_at(h, t, u, core, low=0, size=None):
        rows = pl.ds(h * half + low, half if size is None else size)
        if h == 0:
            return factors.at[t, u, core, :, rows, :]
        return factors.at[u, t, core, :, rows, :]

    r1 = {}
    for o in (1, 2, 3):
        r1[o] = push(rotation.at[x, z, c], full.at[b, x, z, c], "r1", (o - 1,), link.at_band(o))
    yin, own_cells = {}, []

    def send_cells(i):
        for o in (1, 2, 3):
            src = orbitals.at[:, tile_of(ring(b, o) * parts + i, width)]
            yin[i, o] = push(src, cells_in.at[i, b], "yin", (i, o - 1), link.at_band(o))

    send_cells(0)
    send_cells(1)
    for i in range(parts):
        own_cells.append(keep(orbitals.at[:, tile_of(b * parts + i, width)], cells_in.at[i, b], sem_keep.at[i]))
    r2, r3, r4 = {}, {}, {}
    columns_of = [pl.ds(h * (full.shape[-1] // 2), full.shape[-1] // 2) for h in range(2)]
    routes = [(1, 0, slice(None)), (2, 0, columns_of[0]), (2, 1, columns_of[1]), (3, 1, slice(None))]
    for q in range(RING):
        stage[q].wait()
        top, rest = split(cells_out[q])
        for m in range(quarter // LANES):
            high_cells[q * (quarter // LANES) + m] = top[:, m * LANES : (m + 1) * LANES]
            low_cells[q * (quarter // LANES) + m] = rest[:, m * LANES : (m + 1) * LANES]
    def to_mate(step):
        group_at = pl.ds(step * GROUP, GROUP)
        return pltpu.make_async_remote_copy(
            src_ref=windows.at[group_at], dst_ref=mate.at[group_at],
            send_sem=send["s0"].at[step], recv_sem=recv["s0"].at[step],
            device_id=link.partner(), device_id_type=MESH,
        )

    def take(step, carry):
        for k in range(GROUP):
            index = step * GROUP + k
            tile, shift = table[TILE, index], table[SHIFT, index]
            o_high, o_low = [
                jnp.concatenate([ref[tile + m] for m in range(wide // LANES)], axis=1) for ref in (high_cells, low_cells)
            ]
            p_high, p_low = shifted(tiles[index], pads.at[k], shift, window, wide)
            both = dot(o_high, jnp.concatenate([p_high, p_low], axis=1))
            windows[index] = both[:, :projs] + both[:, projs:] + dot(o_low, p_high)
        to_mate(step).start()
        return carry

    one, two = {}, {}

    def assemble(h, o):
        t = ring(first[h], o)
        rows = pl.ds(h * half, half)

        def body(u, carry):
            owner = (t * RING + u if h == 0 else u * RING + t) * 2 + c
            values = [
                ref[table[WHERE + k, owner], rows, :] for k, ref in enumerate((windows, windows, mate, mate))
            ]
            for atom in range(group):
                a, d, e, f = [value * weights[k * group + atom, owner] for k, value in enumerate(values)]
                total[h, t, u, atom] = (a + d) + (e + f)
            return carry

        lax.fori_loop(0, RING, body, 0)
        return t

    low2, high2 = pl.ds(0, 2), pl.ds(2, 2)

    def send_far(h):
        t = assemble(h, 2)
        one[h, 0, 0] = push(total.at[h, t, low2], hop1.at[h, 0], "one", (h, 0, 0), at_first[h](1))
        one[h, 1, 0] = push(total.at[h, t, high2], hop1.at[h, 1], "one", (h, 1, 0), at_first[h](3))

    steps = slots // GROUP
    for q in range(RING):
        stage_tiles[q].wait()
        lax.fori_loop(q * steps // RING, (q + 1) * steps // RING, take, 0)
        if q < 2:
            send_cells(2 + q)
        if q == 1:
            for o in (1, 2, 3):
                r1[o].wait_recv()
            for n, (o, h, span) in enumerate(routes):
                piece = full.at[ring(b, RING - o), x, z, c, :, span]
                for p in (1, 2, 3):
                    r2[n, p] = push(piece, piece, "r2", (n, p - 1), at_first[h](p))
        if q == 3:
            for n, (o, h, span) in enumerate(routes):
                k = ring(b, RING - o)
                for p in (1, 2, 3):
                    r2[n, p].wait_recv()
                piece = full.at[k, :, z, c, :, span] if h == 0 else full.at[k, x, :, c, :, span]
                for p in (1, 2, 3):
                    r3[n, p] = push(piece, piece, "r3", (n, p - 1), at_second[h](p))
    for step in range(steps):
        to_mate(step).wait_recv()
    for h in range(2):
        send_far(h)
    for h in range(2):
        t = assemble(h, 1)
        one[h, 0, 1] = push(total.at[h, t, high2], hop2.at[h, 0, high2], "one", (h, 0, 1), at_first[h](1))
    for h in range(2):
        t = assemble(h, 3)
        one[h, 1, 1] = push(total.at[h, t, low2], hop2.at[h, 1, low2], "one", (h, 1, 1), at_first[h](3))
    for h in range(2):
        assemble(h, 0)

    def add_rows(h, t, start, source):
        def body(u, carry):
            total[h, t, start + u] += source[h, start // 2, u]
            return carry

        lax.fori_loop(0, 2, body, 0)

    for h in range(2):
        one[h, 0, 0].wait_recv()
        t = ring(first[h], 1)
        add_rows(h, t, 0, hop1)
        one[h, 0, 2] = push(total.at[h, t, low2], hop2.at[h, 0, low2], "one", (h, 0, 2), at_first[h](1))
        one[h, 1, 0].wait_recv()
        t = ring(first[h], 3)
        add_rows(h, t, 2, hop1)
        one[h, 1, 2] = push(total.at[h, t, high2], hop2.at[h, 1, high2], "one", (h, 1, 2), at_first[h](3))

    for copy in r3.values():
        copy.wait_recv()
    for o in (1, 2, 3):
        mine = full.at[ring(b, RING - o), :, :, c]
        r4[o] = push(mine, mine, "r4", (o - 1,), link.partner())

    own_rows.wait()
    for o in (1, 2, 3):
        r4[o].wait_recv()

    def split_rows(k, carry):
        top, rest = split(full[k].reshape(bands, full.shape[-1]))
        columns = tile_of(k, full.shape[-1])
        high_rows[:, columns] = top
        low_rows[:, columns] = rest
        return carry

    lax.fori_loop(0, RING, split_rows, 0)

    yout, own_out = {}, []

    def rotate(i):
        for o in (1, 2, 3):
            yin[i, o].wait_recv()
        own_cells[i].wait()
        high, low = split(cells_in[i].reshape(RING * bands, width))
        pair = jnp.concatenate([high, low], axis=1)

        def body(k, carry):
            columns = tile_of(k, full.shape[-1])
            both = dot(high_rows[:, columns], pair)
            here = both[:, :width] + both[:, width:] + dot(low_rows[:, columns], high)
            cells_out[k, :, pl.ds(i * width, width)] = here
            return carry

        lax.fori_loop(0, RING, body, 0)
    def give(unit, offsets=(1, 2, 3)):
        i, lower = unit // 2, unit % 2
        rows, columns = pl.ds(lower * half, half), tile_of(b * parts + i, width)
        for o in offsets:
            src = cells_out.at[ring(b, o), rows, pl.ds(i * width, width)]
            yout[unit, o] = push(src, rotated.at[rows, columns], "yout", (unit, o - 1), link.at_band(o))
        if 2 in offsets:
            src = cells_out.at[b, rows, pl.ds(i * width, width)]
            own_out.append(keep(src, rotated.at[rows, columns], sem_keep.at[parts + unit]))

    rotate(0)
    rotate(1)
    give(0)

    for h in range(2):
        t = first[h]
        one[h, 0, 1].wait_recv()
        one[h, 1, 1].wait_recv()
        one[h, 0, 2].wait_recv()
        one[h, 1, 2].wait_recv()

        def finish(u, carry, h=h, t=t):
            total[h, t, u] += hop2[h, 0, u] + hop2[h, 1, u]
            return carry

        lax.fori_loop(0, RING, finish, 0)
        lower, upper = pl.ds(0, sub), pl.ds(sub, sub)
        s = second[h]
        far, nxt, prv = ring(s, 2), ring(s, 1), ring(s, 3)
        two[h, 0, 0] = push(total.at[h, t, far, :, lower], hop3.at[h, 0], "two", (h, 0, 0), at_second[h](1))
        two[h, 1, 0] = push(total.at[h, t, far, :, upper], hop3.at[h, 1], "two", (h, 1, 0), at_second[h](3))
        two[h, 0, 1] = push(
            total.at[h, t, nxt, :, upper], hop4.at[h, 0, :, upper], "two", (h, 0, 1), at_second[h](1)
        )
        two[h, 1, 1] = push(
            total.at[h, t, prv, :, lower], hop4.at[h, 1, :, lower], "two", (h, 1, 1), at_second[h](3)
        )

    for h in range(2):
        t, s = first[h], second[h]
        nxt, prv = ring(s, 1), ring(s, 3)
        two[h, 0, 0].wait_recv()
        total[h, t, nxt, :, lower] += hop3[h, 0]
        two[h, 0, 2] = push(
            total.at[h, t, nxt, :, lower], hop4.at[h, 0, :, lower], "two", (h, 0, 2), at_second[h](1)
        )
        two[h, 1, 0].wait_recv()
        total[h, t, prv, :, upper] += hop3[h, 1]
        two[h, 1, 2] = push(
            total.at[h, t, prv, :, upper], hop4.at[h, 1, :, upper], "two", (h, 1, 2), at_second[h](3)
        )

    rotate(2)

    for h in range(2):
        t, s = first[h], second[h]
        for d in range(2):
            two[h, d, 1].wait_recv()
            two[h, d, 2].wait_recv()
        for atom in range(group):
            value = total[h, t, s, atom] + hop4[h, 0, atom] + hop4[h, 1, atom]
            turn[pl.ds(atom * projs, projs), pl.ds(h * half, half)] = value.T

    def strip_at(index):
        return pl.ds(pl.multiple_of(index * strip, 8), strip)

    swap, back = {}, {}
    for o in (1, 2, 3):
        swap[o] = push(turn.at[strip_at(ring(b, o))], turn_in.at[b], "sum", (o - 1,), link.at_band(o))
    turn_in[b] = turn[strip_at(b), :]
    give(1, (1, 3))

    for o in (1, 2, 3):
        swap[o].wait_recv()
    high, low = split(jnp.concatenate([turn_in[k] for k in range(RING)], axis=1))
    pair = jnp.concatenate([high, low], axis=0)

    def turn_rows(k, carry):
        columns = tile_of(k, full.shape[-1])
        both = dot_nt(pair, high_rows[:, columns])
        turn_out[k] = both[:strip] + both[strip:] + dot_nt(high, low_rows[:, columns])
        return carry

    lax.fori_loop(0, RING, turn_rows, 0)
    for o in (1, 2, 3):
        back[o] = push(turn_out.at[ring(b, o)], turned.at[strip_at(b)], "back", (o - 1,), link.at_band(o))
    turned[strip_at(b), :] = turn_out[b]

    give(1, (2,))
    for unit in range(2, 6):
        give(unit)
    rotate(3)
    give(6)
    give(7)

    for o in (1, 2, 3):
        back[o].wait_recv()
    for atom in range(group):
        t_high, t_low = split(turned[pl.ds(atom * projs, projs), :].T)
        m_high, m_low = split(matrices[atom])
        both = dot(t_high, jnp.concatenate([m_high, m_low], axis=1))
        owned[atom] = both[:, :projs] + both[:, projs:] + dot(t_low, m_high)

    own_factor = keep(owned, factors.at[x, z, c], sem_own.at[1])
    mate_core = []

    def to_core(src, h, t, u, index):
        mate_core.append(push(src, factor_at(h, t, u, c), "core", (h, index), link.partner()))

    pairs = ready.shape[0]

    def put(slot, index):
        return pltpu.make_async_copy(ready.at[slot], columns.at[index], sem_ready.at[slot])

    def prepare(low, high):
        def body(step, carry):
            for k in range(pairs):
                index = step * pairs + k

                @pl.when(step > 0)
                def _(k=k, index=index):
                    put(k, index).wait()

                pad = pads.at[k]
                pad[pl.ds(LANES, window), :] = tiles[index]
                high, low = split(pad[pl.ds(LANES - table[SHIFT, index], wide), :].T)
                ready[k, pl.ds(0, projs), :] = high
                ready[k, pl.ds(projs, projs), :] = low
                put(k, index).start()
            return carry

        lax.fori_loop(low, high, body, 0)

    share = slots // pairs // 8
    ag1, ag2, agf = {}, {}, {}
    for h in range(2):
        t, s = first[h], second[h]
        for d, peer, order in ((0, 1, (0, 1)), (1, 3, (1, 0))):
            for m, part in enumerate(order):
                rows = pl.ds(h * half + part * sub, sub)
                ag1[h, d, m] = push(
                    owned.at[:, rows], factor_at(h, t, s, c, part * sub, sub), "ag1", (h, d, m), at_second[h](peer)
                )
    def spread(h, r, src, u):
        t = first[h]
        for d, peer in ((0, 1), (1, 3)):
            ag2[h, d, r] = push(src, factor_at(h, t, u, c), "ag2", (h, d, r), at_first[h](peer))
        to_core(src, h, t, u, r)

    lines = (0, 3, 1, 2)
    for h in range(2):
        spread(h, 0, owned.at[:, pl.ds(h * half, half)], second[h])
    prepare(0, share)
    for h in range(2):
        t, s = first[h], second[h]
        for d, back, peer in ((0, 3, 1), (1, 1, 3)):
            ag1[h, d, 0].wait_recv()
            piece = factor_at(h, t, ring(s, back), c, d * sub, sub)
            ag1[h, d, 2] = push(piece, piece, "ag1", (h, d, 2), at_second[h](peer))
    prepare(share, 2 * share)
    for h in range(2):
        t, s = first[h], second[h]
        for d, r in ((0, 1), (1, 2)):
            ag1[h, d, 1].wait_recv()
            u = ring(s, lines[r])
            spread(h, r, factor_at(h, t, u, c), u)
    prepare(2 * share, 3 * share)
    for h in range(2):
        t, s = first[h], second[h]
        ag1[h, 0, 2].wait_recv()
        ag1[h, 1, 2].wait_recv()
        u = ring(s, 2)
        spread(h, 3, factor_at(h, t, u, c), u)
    prepare(3 * share, 4 * share)

    for r in range(RING):
        for h in range(2):
            u = ring(second[h], lines[r])
            for d, back, peer in ((0, 3, 1), (1, 1, 3)):
                ag2[h, d, r].wait_recv()
                t = ring(first[h], back)
                piece = factor_at(h, t, u, c)
                if (r < 2) == (d == 0):
                    agf[h, r] = push(piece, piece, "agf", (h, r), at_first[h](peer))
                to_core(piece, h, t, u, RING * (1 + d) + r)
        prepare((4 + r) * share, (5 + r) * share)
    for r in range(RING):
        for h in range(2):
            u = ring(second[h], lines[r])
            agf[h, r].wait_recv()
            t = ring(first[h], 2)
            to_core(factor_at(h, t, u, c), h, t, u, RING * 3 + r)

    for copy in mate_core:
        copy.wait_recv()
    for copy in yout.values():
        copy.wait_recv()
    for copy in own_out:
        copy.wait()
    own_factor.wait()
    for k in range(pairs):
        put(k, k).wait()
    for copy in started:
        copy.wait_send()
    for step in range(slots // GROUP):
        to_mate(step).wait_send()


PARTS = 4


def exchange(table, weights, orbitals, projectors, rotation, matrices):
    bands, cells = orbitals.shape
    slots, window, projs = projectors.shape
    all_bands = rotation.shape[1]
    group = matrices.shape[0]
    atoms = 2 * RING * RING * group
    width = cells // RING // PARTS
    half = bands // 2
    sub = half // 2
    rows = bands // (2 * RING * RING)
    strip = group * projs // RING
    f32, bf16 = jnp.float32, jnp.bfloat16
    counts = [
        (PARTS, 3), (2 * PARTS, 3), (3,), (4, 3), (4, 3), (3,), (slots // GROUP,), (2, 2, 3), (2, 2, 3), (3,), (3,),
        (2, 2, 3), (2, 2, RING), (2, RING), (2, 4 * RING),
    ]
    dma = pltpu.SemaphoreType.DMA
    in_hbm = pl.BlockSpec(memory_space=pltpu.MemorySpace.HBM)
    factors, rotated, columns = pl.pallas_call(
        exchange_kernel,
        out_shape=(
            jax.ShapeDtypeStruct((RING, RING, 2, group, bands, projs), f32),
            jax.ShapeDtypeStruct((bands, cells), f32),
            jax.ShapeDtypeStruct((slots, 2 * projs, window + LANES), bf16),
        ),
        in_specs=[pl.BlockSpec(memory_space=pltpu.SMEM)] * 2
        + [in_hbm] * 3
        + [pl.BlockSpec(memory_space=pltpu.VMEM)],
        out_specs=[in_hbm] * 3,
        scratch_shapes=[
            pltpu.VMEM((PARTS, RING, bands, width), f32),
            pltpu.VMEM((RING, bands, cells // RING), f32),
            pltpu.VMEM((RING, RING, RING, 2, rows, all_bands), f32),
            pltpu.VMEM((bands, RING * all_bands), bf16),
            pltpu.VMEM((bands, RING * all_bands), bf16),
            pltpu.VMEM((cells // LANES, bands, LANES), bf16),
            pltpu.VMEM((cells // LANES, bands, LANES), bf16),
            pltpu.VMEM((slots, window, projs), f32),
            pltpu.VMEM((slots, bands, projs), f32),
            pltpu.VMEM((slots, bands, projs), f32),
            pltpu.VMEM((2, RING, RING, group, half, projs), f32),
            pltpu.VMEM((2, 2, 2, group, half, projs), f32),
            pltpu.VMEM((2, 2, RING, group, half, projs), f32),
            pltpu.VMEM((2, 2, group, sub, projs), f32),
            pltpu.VMEM((2, 2, group, half, projs), f32),
            pltpu.VMEM((group * projs, bands), f32),
            pltpu.VMEM((RING, strip, bands), f32),
            pltpu.VMEM((RING, strip, bands), f32),
            pltpu.VMEM((group * projs, bands), f32),
            pltpu.VMEM((group, bands, projs), f32),
            pltpu.VMEM((GROUP, window + 2 * LANES, projs), f32),
            pltpu.VMEM((2, 2 * projs, window + LANES), bf16),
            dma((2 * RING,)),
            dma((3 * PARTS,)),
            dma((2,)),
            dma((2,)),
        ]
        + [dma(shape) for shape in counts for _ in range(2)],
        compiler_params=pltpu.CompilerParams(
            collective_id=0, has_side_effects=True, vmem_limit_bytes=60 << 20
        ),
        name="exchange",
    )(
        table, weights, orbitals, projectors, rotation.reshape(RING, RING, 2, rows, all_bands), matrices
    )
    return factors.reshape(atoms, bands, projs), rotated, columns


def per_device(orbitals, projectors, window_start, slot_atom, atom_home, atom_matrices, rotation):
    dom = lax.axis_index("dom").astype(jnp.int32).reshape(1)
    window = projectors.shape[1]
    table, weights = list_slots(
        dom, window_start, slot_atom, atom_home, atom_matrices.shape[0], orbitals.shape[1], window + LANES
    )
    factors, rotated, columns = exchange(table, weights, orbitals, projectors, rotation, atom_matrices)
    return update(table, factors, columns, rotated)


def solution(mesh):
    in_specs = (
        P("band", "dom"),
        P("dom", None, None),
        P("dom"),
        P(),
        P(),
        P("dom", None, None),
        P("band", None),
    )
    out_specs = P("band", "dom")
    return jax.shard_map(
        per_device, mesh=mesh, in_specs=in_specs, out_specs=out_specs, check_vma=False
    )
```
